32 devices in a mesh: lat: 4 (over y, core), lon: 8 (over z, x).
Axes of the slice: x: 2, y: 2, z: 4, core: 2. Of those that a mesh axis runs over, the one named last changes fastest.
Arguments:
- field: bfloat16 [64, 128, 384], P('lat', 'lon'), may hold values from -6 to 6
- obs_jac: bfloat16 [32, 32, 128, 384], P(None, ('lat', 'lon')), may hold values from -0.3125 to 0.3125
- obs_frac: bfloat16 [32, 32, 2, 128], P(None, ('lat', 'lon')), may hold values from 0 to 1
- obs_innov: bfloat16 [32, 32, 128], P(None, ('lat', 'lon')), may hold values from -6 to 6
- obs_rinv: bfloat16 [32, 32, 128], P(None, ('lat', 'lon')), may hold values from 1 to 16
- obs_cells: int32 [32, 32, 128], P(None, ('lat', 'lon')), may hold values from -1 to 270, as said below
Outputs:
- departures: float32 [32, 32, 128], P(None, ('lat', 'lon'))
- field_grad: float32 [64, 128, 384], P('lat', 'lon')
The draws below stay inside these ranges and needn't reach their ends.
Inputs may be any that keep to these rules, and one draw needn't show every extreme that they name: `obs_cells`: in block (o, p) the live slots come first, at least one and at most 128; a live slot holds r * 17 + q with r below 16 and q below 16; slot 0 of every block holds the cell at r = 15, q = 15; the number of live slots varies by owner.
All inputs are finite; a program needn't handle non-finite values.
Results may differ from the reference program's by a relative error of at most 0.0046.
Values may be sent and summed in bfloat16 or wider, within the bound.
A program may use at most 128 MiB of HBM per device.

```python
import math
import jax
import jax.numpy as jnp
from jax import lax

LAT_DEV = 16
LON_DEV = 16
SLOTS = 128
WIDTH = 384
NLAT = 64
NLON = 128
N_LON = 8
DEVICES = 32


def draw_obs_cells(key, part):
    key_level, key_cut, key_row, key_col, key_pick = jax.random.split(key, 5)
    level_vals = jax.random.randint(key_level, (DEVICES, 1), 1, 5)
    chosen = jax.random.permutation(key_pick, DEVICES)[0]
    level_vals = jnp.where(jnp.arange(DEVICES)[:, None] == chosen, 4, level_vals)
    cut_vals = jax.random.randint(key_cut, (DEVICES, DEVICES), 0, SLOTS // 4)
    live_count = SLOTS * level_vals // 4 - cut_vals
    first_src = jnp.arange(DEVICES)[None, :] == 0
    live_count = jnp.where(first_src & (level_vals == 4), SLOTS, live_count)
    row_vals = jax.random.randint(key_row, (DEVICES, DEVICES, SLOTS), 0, LAT_DEV)
    col_vals = jax.random.randint(key_col, (DEVICES, DEVICES, SLOTS), 0, LON_DEV)
    slot_idx = jnp.arange(SLOTS)[None, None, :]
    cell_vals = row_vals * (LON_DEV + 1) + col_vals
    cell_vals = jnp.where(slot_idx == 0, LAT_DEV * (LON_DEV + 1) - 2, cell_vals)
    cell_vals = jnp.where(slot_idx < live_count[:, :, None], cell_vals, -1)
    return cell_vals.astype(jnp.int32)


def block_levels(own_key, shape, cuts, smallest, largest):
    factor_of = 1.0
    for dim, parts in cuts:
        steps = jax.random.uniform(jax.random.fold_in(jax.random.fold_in(own_key, 6), dim), (parts,), jnp.float32, smallest / len(cuts), largest / len(cuts))
        factor_of = factor_of * jnp.repeat(jnp.exp(steps), shape[dim] // parts).reshape((-1,) + (1,) * (len(shape) - 1 - dim))
    return factor_of


def normal_values(key, shape, scale, reach, cuts=(), kind=jnp.bfloat16):
    values = jax.random.normal(key, shape, jnp.float32) * scale
    if len(cuts) > 0:
        values = block_levels(key, shape, cuts, -0.22, 0.18) * values
    return jnp.clip(values, min=-reach, max=reach).astype(kind)


def setup_inputs(seed: int = 0) -> dict:
    splits = jax.random.split(jax.random.key(seed), 7)
    return {
        "field": normal_values(splits[0], (NLAT, NLON, WIDTH), 1.0, 6.0, ((0, 4), (1, 8))),
        "obs_jac": normal_values(splits[1], (DEVICES, DEVICES, SLOTS, WIDTH), WIDTH ** -0.5, 0.3125, ((1, 32),)),
        "obs_frac": jnp.clip(1.0 * jax.random.uniform(splits[2], (DEVICES, DEVICES, 2, SLOTS), jnp.float32) ** block_levels(splits[2], (DEVICES, DEVICES, 2, SLOTS), ((1, 32),), -0.2, 0.2), 0.0, 1.0).astype(jnp.bfloat16),
        "obs_innov": normal_values(splits[3], (DEVICES, DEVICES, SLOTS), 1.0, 6.0, ((1, 32),)),
        "obs_rinv": jnp.clip(jnp.exp(math.log(16.0) - 2.7725887 * jax.random.uniform(splits[4], (DEVICES, DEVICES, SLOTS), jnp.float32) ** block_levels(splits[4], (DEVICES, DEVICES, SLOTS), ((1, 32),), -0.2, 0.2)), 1.0, 16.0).astype(jnp.bfloat16),
        "obs_cells": draw_obs_cells(jax.random.fold_in(splits[6], 71), 0),
    }


def local_terms(col_table, stride, cell_ids, frac_lat, frac_lon, innovation, inv_error, jacobian, grad_ext):
    is_live = cell_ids >= 0
    corner = jnp.where(is_live, cell_ids, 0).astype(jnp.int32)
    lat_part = frac_lat.astype(jnp.float32)
    lon_part = frac_lon.astype(jnp.float32)
    raw_weights = ((1.0 - lat_part) * (1.0 - lon_part), lat_part * (1.0 - lon_part), (1.0 - lat_part) * lon_part, lat_part * lon_part)
    rounded = lax.optimization_barrier(tuple(weight.astype(jnp.bfloat16) for weight in raw_weights))
    weights = tuple(weight.astype(jnp.float32) for weight in rounded)
    offsets = (0, stride, 1, stride + 1)
    interp = jnp.zeros((cell_ids.shape[0], col_table.shape[1]), jnp.float32)
    for weight, offset in zip(weights, offsets):
        interp = interp + weight[:, None] * col_table[corner + offset].astype(jnp.float32)
    jac_wide = jacobian.astype(jnp.float32)
    evolved = jnp.sum(interp * jac_wide, axis=1)
    departure = jnp.where(is_live, evolved - innovation.astype(jnp.float32), jnp.zeros((), jnp.float32))
    contrib_low = lax.optimization_barrier(((inv_error.astype(jnp.float32) * departure)[:, None] * jac_wide).astype(jnp.bfloat16))
    contrib = contrib_low.astype(jnp.float32)
    for weight, offset in zip(weights, offsets):
        grad_ext = grad_ext.at[corner + offset].add(weight[:, None] * contrib)
    return departure, grad_ext


def reference(field, obs_jac, obs_frac, obs_innov, obs_rinv, obs_cells):
    width_all = field.shape[2]
    stride = LON_DEV + 1
    extended = jnp.concatenate([field, field[:, :1]], axis=1)
    extended = jnp.concatenate([extended, jnp.zeros((1, NLON + 1, width_all), field.dtype)], axis=0)
    owners = jnp.arange(DEVICES, dtype=jnp.int32)

    def visit_owner(grad_all, pieces):
        owner_id, jac_rows, frac_pair, innov_vals, rinv_vals, cell_vals = pieces
        row_start = ((owner_id // N_LON) * LAT_DEV).astype(jnp.int32)
        col_start = ((owner_id % N_LON) * LON_DEV).astype(jnp.int32)
        zero_idx = jnp.zeros((), jnp.int32)
        col_table = lax.dynamic_slice(extended, (row_start, col_start, zero_idx), (LAT_DEV + 1, stride, width_all)).reshape(-1, width_all)
        local_grad = jnp.zeros(((LAT_DEV + 1) * stride, width_all), jnp.float32)
        departure, local_grad = local_terms(col_table, stride, cell_vals.reshape(-1), frac_pair[:, 0, :].reshape(-1), frac_pair[:, 1, :].reshape(-1), innov_vals.reshape(-1), rinv_vals.reshape(-1), jac_rows.reshape(-1, width_all), local_grad)
        old_grad = lax.dynamic_slice(grad_all, (row_start, col_start, zero_idx), (LAT_DEV + 1, stride, width_all))
        grad_all = lax.dynamic_update_slice(grad_all, old_grad + local_grad.reshape(LAT_DEV + 1, stride, width_all), (row_start, col_start, zero_idx))
        return grad_all, departure.reshape(cell_vals.shape)

    grad_all = jnp.zeros((NLAT + 1, NLON + 1, width_all), jnp.float32)
    grad_all, departures = lax.scan(visit_owner, grad_all, (owners, obs_jac, obs_frac, obs_innov, obs_rinv, obs_cells))
    field_grad = grad_all[:NLAT, :NLON].at[:, 0].add(grad_all[:NLAT, NLON])
    return departures, field_grad
```

```python
import functools
import math

import jax
import jax.numpy as jnp
from jax import lax
from jax.experimental import pallas as pl
from jax.experimental.pallas import tpu as pltpu
from jax.sharding import PartitionSpec as P

MESH = pl.DeviceIdType.MESH
AWAY = -1000.0


def visit_order(z, line):
    half = line // 2
    if z < half:
        return [*range(half, line), *(p for p in range(half) if p != z), z]
    return [*range(half - 1, -1, -1), *(p for p in range(half, line) if p != z), z]


def pick(z, values):
    chosen = jnp.int32(values[0])
    for p in range(1, len(values)):
        chosen = jnp.where(z == p, jnp.int32(values[p]), chosen)
    return chosen


def weight_rows(position, frac, rows):
    ids = lax.broadcasted_iota(jnp.int32, (rows, position.shape[1]), 0).astype(jnp.float32)
    zero = jnp.zeros_like(ids)
    return jnp.where(
        ids == position, 1.0 - frac, jnp.where(ids == position + 1.0, frac, zero)
    )


def kernel(
    lat_n, lon_n, line, rows, cols, tile,
    field, cell_ref, frac_ref, innov_ref, rinv_ref, jac,
    gmain, hrecv, dep_out,
    edge, innov, rinv, meta,
    tbl, met, jrecv, dep, part, gsend, rbuf, hsend,
    f_send, f_recv, e_send, e_recv, m_send, m_recv, j_send, j_recv, d_send, d_recv,
    g_send, g_recv, h_send, h_recv, from_low, from_high,
):
    inner = lon_n // line
    plane = lat_n * inner
    slots = jac.shape[3]
    cells = rows * cols
    halo = cells + cols
    lat, lon = lax.axis_index("lat"), lax.axis_index("lon")
    z, xi = lon // inner, lon % inner
    here = lat * inner + xi
    lat_up, lat_down = (lat + 1) % lat_n, (lat + lat_n - 1) % lat_n
    lon_up, lon_down = (lon + 1) % lon_n, (lon + lon_n - 1) % lon_n
    z_low, x_low = lon_down // inner, lon_down % inner
    orders = [visit_order(p, line) for p in range(line)]
    visits = [pick(z, [order[n] for order in orders]) for n in range(line)]

    def remote(src, dst, send, recv, to):
        return pltpu.make_async_remote_copy(
            src_ref=src, dst_ref=dst, send_sem=send, recv_sem=recv,
            device_id=to, device_id_type=MESH,
        )

    def landed(like, sem):
        pltpu.make_async_copy(like, like, sem).wait()

    def mate(i):
        to = (here + i) % plane
        return to, (to // inner, z * inner + to % inner)

    has_low, has_high = z > 0, z < line - 1
    inside_line = has_low & has_high
    low, high = (lat, lon - inner), (lat, lon + inner)
    barrier = pltpu.get_barrier_semaphore()

    @pl.when(has_low)
    def _():
        pl.semaphore_signal(barrier, inc=1, device_id=low, device_id_type=MESH)

    @pl.when(has_high)
    def _():
        pl.semaphore_signal(barrier, inc=1, device_id=high, device_id_type=MESH)

    def greet(i, carry):
        pl.semaphore_signal(barrier, inc=1, device_id=mate(i)[1], device_id_type=MESH)
        return carry

    lax.fori_loop(1, plane, greet, 0)

    own_field = tbl.at[z, pl.ds(0, cells)]
    pltpu.make_async_copy(field, own_field, f_recv.at[z]).start()
    for g in visits:
        pltpu.make_async_copy(
            jac.at[lat, g, xi], jrecv.at[g, pl.ds(0, slots)], j_recv.at[g]
        ).start()
    innov[...] = innov_ref[...].astype(jnp.float32)
    rinv[...] = rinv_ref[...].astype(jnp.float32)

    def build(i, carry):
        to, _ = mate(i)
        for g in range(line):
            owner = (to // inner) * lon_n + g * inner + to % inner
            cell = cell_ref[owner].astype(jnp.float32)
            live = cell >= 0.0
            row = jnp.floor((cell + 0.5) * (1.0 / (cols + 1)))
            meta[i, g] = jnp.concatenate(
                [
                    jnp.where(live, row, AWAY),
                    jnp.where(live, cell - row * (cols + 1), AWAY),
                    frac_ref[owner].astype(jnp.float32),
                    innov[pl.ds(owner, 1), :],
                    rinv[pl.ds(owner, 1), :],
                    jnp.zeros((2, slots), jnp.float32),
                ],
                axis=0,
            ).astype(meta.dtype)
        return carry

    lax.fori_loop(0, plane, build, 0)
    landed(own_field, f_recv.at[z])
    edge[...] = jnp.concatenate(
        [tbl[z, pl.ds(r * cols, cols), :].astype(jnp.float32)[0:1] for r in range(rows)], axis=0
    ).astype(edge.dtype)
    pltpu.make_async_copy(meta.at[0], met.at[:, :, pl.ds(0, slots)], m_recv).start()
    pl.semaphore_wait(barrier, plane - 1 + has_low.astype(jnp.int32) + has_high.astype(jnp.int32))

    def send_field(g, up):
        piece = tbl.at[g, pl.ds(0, cells)]
        remote(piece, piece, f_send, f_recv.at[g], high if up else low).start()

    @pl.when(has_low)
    def _():
        send_field(z, False)

    @pl.when(has_high)
    def _():
        send_field(z, True)

    def send_meta(i, carry):
        place = pl.ds(pl.multiple_of(i * slots, slots), slots)
        remote(meta.at[i], met.at[:, :, place], m_send, m_recv, mate(i)[1]).start()
        return carry

    def send_jac(n):
        g = visits[n]

        def one(i, carry):
            to, at = mate(i)
            place = pl.ds(pl.multiple_of(i * slots, slots), slots)
            remote(
                jac.at[to // inner, g, to % inner], jrecv.at[g, place], j_send, j_recv.at[g], at
            ).start()
            return carry

        return one

    lax.fori_loop(1, plane, send_meta, 0)
    lax.fori_loop(1, plane // 2, send_jac(0), 0)

    for _ in range(line - 1):
        @pl.when(has_low)
        def _():
            pl.semaphore_signal(from_high, inc=1, device_id=low, device_id_type=MESH)

        @pl.when(has_high)
        def _():
            pl.semaphore_signal(from_low, inc=1, device_id=high, device_id_type=MESH)

        @pl.when(has_low)
        def _():
            pl.semaphore_wait(from_low, 1)

        @pl.when(has_high)
        def _():
            pl.semaphore_wait(from_high, 1)

    for i in range(line):
        to = (z + i) % line
        remote(tbl.at[z, pl.ds(0, cols)], tbl.at[z, pl.ds(cells, cols)], e_send,
               e_recv.at[z], (lat_down, to * inner + xi)).start()
        remote(edge, tbl.at[z_low, pl.ds(halo, rows)], e_send,
               e_recv.at[z_low], (lat, to * inner + x_low)).start()
        remote(edge, tbl.at[z_low, pl.ds(halo + rows, rows)], e_send,
               e_recv.at[z_low], (lat_down, to * inner + x_low)).start()
    lax.fori_loop(plane // 2, plane, send_jac(0), 0)
    for n in range(1, line):
        lax.fori_loop(1, plane, send_jac(n), 0)

    def forward(d):
        @pl.when(inside_line & (z >= d))
        def _():
            landed(own_field, f_recv.at[z - d])
            send_field(z - d, True)

        @pl.when(inside_line & (z + d < line))
        def _():
            landed(own_field, f_recv.at[z + d])
            send_field(z + d, False)

    landed(met, m_recv)
    inside = jnp.where(lat < lat_n - 1, 1.0, 0.0)
    width = tile * slots
    tiles = plane // tile
    pad = -(-(max(rows, cols) + 1) // 8) * 8

    def compute(n, g):
        into = part.at[n]
        if tiles > 1:
            into[...] = jnp.zeros(into.shape, into.dtype)

        def one_tile(t, carry):
            lanes = pl.ds(pl.multiple_of(t * width, width), width)
            info = met[g, :, lanes].astype(jnp.float32)
            lat_w = weight_rows(info[0:1], info[2:3], pad)
            lon_w = weight_rows(info[1:2], info[3:4], pad)
            lon_c = lon_w[:cols]
            lon_e = lon_w[cols:cols + 1]
            lat_n_row = lat_w[rows:rows + 1] * inside
            first = lax.broadcasted_iota(jnp.int32, (rows, width), 0) == 0
            blocks = [lat_w[r:r + 1] * lon_c for r in range(rows)]
            blocks.append(lat_n_row * lon_c)
            blocks.append(lat_w[:rows] * lon_e)
            blocks.append(
                jnp.where(first, jnp.broadcast_to(lat_n_row * lon_e, (rows, width)), 0.0)
            )
            spread = jnp.concatenate(blocks, axis=0).astype(jnp.bfloat16).astype(jnp.float32)
            jac_t = jrecv[g, lanes]
            products = lax.dot_general(
                tbl[g], jac_t, (((1,), (1,)), ((), ())), preferred_element_type=jnp.float32
            )
            evolved = jnp.sum(spread * products, axis=0, keepdims=True)
            departure = jnp.where(info[0:1] >= 0.0, evolved - info[4:5], 0.0)
            dep[g, :, lanes] = departure
            scaled = (spread * (info[5:6] * departure)).astype(jnp.bfloat16)
            partial = jnp.dot(scaled, jac_t, preferred_element_type=jnp.float32)
            if tiles > 1:
                into[...] += partial
            else:
                into[...] = partial
            return carry

        if tiles > 1:
            lax.fori_loop(0, tiles, one_tile, 0)
        else:
            one_tile(0, 0)

    def send_dep(g):
        def one(i, carry):
            to = (here + plane - i) % plane
            place = pl.ds(pl.multiple_of(i * slots, slots), slots)
            remote(
                dep.at[g, :, place], dep_out.at[lat, g, xi], d_send, d_recv,
                (to // inner, z * inner + to % inner),
            ).start()
            return carry

        lax.fori_loop(1, plane, one, 0)
        pltpu.make_async_copy(dep.at[g, :, pl.ds(0, slots)], dep_out.at[lat, g, xi], d_recv).start()

    def finish(n, incoming):
        g = visits[n]
        total = part[n]
        if incoming:
            landed(rbuf.at[g], g_recv.at[g])
            total = total + rbuf[g].astype(jnp.float32)
        gsend[n] = total.astype(gsend.dtype)
        up = g > z
        next_z = jnp.where(up, z + 1, z - 1)
        slot = jnp.where((g == next_z) & jnp.logical_not(up), line, g)
        remote(gsend.at[n], rbuf.at[slot], g_send, g_recv.at[slot],
               (lat, next_z * inner + xi)).start()

    def pass_on(n):
        @pl.when(inside_line)
        def _():
            finish(n, True)

    for d in range(1, max(line // 2, 1)):
        forward(d)
    for n in range(line):
        g = visits[n]
        if n < line - 1:
            @pl.when(jnp.logical_not(inside_line))
            def _():
                landed(own_field, f_recv.at[g])
        landed(tbl.at[g, pl.ds(cells, cols + 2 * rows)], e_recv.at[g])
        landed(jrecv.at[g], j_recv.at[g])
        compute(n, g)
        send_dep(g)
        if n < line - 1:
            @pl.when(jnp.logical_not(inside_line))
            def _():
                finish(n, False)
        if n == 0:
            for d in range(max(line // 2, 1), line - 1):
                forward(d)
        elif n == 1 and n < line - 1:
            pass_on(0)
            pass_on(1)
        elif n < line - 1:
            pass_on(n)

    @pl.when(has_low)
    def _():
        landed(rbuf.at[z], g_recv.at[z])
        part[line - 1] += rbuf[z].astype(jnp.float32)

    @pl.when(has_high)
    def _():
        landed(rbuf.at[line], g_recv.at[line])
        part[line - 1] += rbuf[line].astype(jnp.float32)

    hsend[...] = part[line - 1, pl.ds(cells, cols + 2 * rows), :].astype(hsend.dtype)
    remote(hsend.at[pl.ds(0, cols)], hrecv.at[0], h_send, h_recv, (lat_up, lon)).start()
    remote(hsend.at[pl.ds(cols, rows)], hrecv.at[1], h_send, h_recv, (lat, lon_up)).start()
    remote(hsend.at[pl.ds(cols + rows, rows)], hrecv.at[2], h_send, h_recv,
           (lat_up, lon_up)).start()
    gmain[...] = part[line - 1, pl.ds(0, cells), :]

    others = pl.ds(0, (plane - 1) * slots)
    for up in (False, True):
        for i in range(line):
            sent = (z >= i) & has_high if up else (z + i < line) & has_low

            @pl.when(sent & (inside_line | (i == 0)))
            def _():
                landed(own_field, f_send)
    landed(tbl.at[:, pl.ds(cells, cols + 2 * rows)], e_send)
    landed(met.at[:, :, others], m_send)
    landed(jrecv.at[:, others], j_send)
    landed(dep.at[:, :, others], d_send)
    landed(gsend, g_send)
    landed(hsend, h_send)
    landed(hrecv, h_recv)
    landed(dep_out, d_recv)


def last_sums(rows, cols, gmain, hrecv, dep, grad_out, dep_out):
    dep_out[...] = dep[...]
    grad_out[...] = gmain[...]
    grad_out[pl.ds(0, cols), :] += hrecv[0].astype(jnp.float32)
    east = hrecv[1].astype(jnp.float32)
    corner = hrecv[2].astype(jnp.float32)
    for r in range(rows):
        extra = east[r:r + 1]
        if r == 0:
            extra = extra + corner[0:1]
        grad_out[pl.ds(r * cols, 1), :] += extra


def shards(mesh_shape, field, obs_jac, obs_frac, obs_innov, obs_rinv, obs_cells):
    lat_n, lon_n = mesh_shape
    line = math.gcd(lon_n // 2, 4)
    inner = lon_n // line
    plane = lat_n * inner
    total = lat_n * lon_n
    rows, cols, wide = field.shape
    slots = obs_jac.shape[2]
    tile = math.gcd(plane, 8)
    cells = rows * cols
    table = cells + cols + 2 * rows
    f32, bf16 = jnp.float32, jnp.bfloat16
    dma = pltpu.SemaphoreType.DMA
    one = pltpu.SemaphoreType.DMA(())
    vmem = pl.BlockSpec(memory_space=pltpu.VMEM)
    anywhere = pl.BlockSpec(memory_space=pl.ANY)
    parts = pl.pallas_call(
        functools.partial(kernel, lat_n, lon_n, line, rows, cols, tile),
        out_shape=(
            jax.ShapeDtypeStruct((cells, wide), f32),
            jax.ShapeDtypeStruct((3, rows, wide), bf16),
            jax.ShapeDtypeStruct((lat_n, line, inner, 1, slots), f32),
        ),
        in_specs=[anywhere, vmem, vmem, vmem, vmem, anywhere],
        out_specs=(vmem,) * 3,
        scratch_shapes=[
            pltpu.VMEM((rows, wide), bf16),
            pltpu.VMEM((total, slots), f32),
            pltpu.VMEM((total, slots), f32),
            pltpu.VMEM((plane, line, 8, slots), bf16),
            pltpu.VMEM((line, table, wide), bf16),
            pltpu.VMEM((line, 8, plane * slots), bf16),
            pltpu.VMEM((line, plane * slots, wide), bf16),
            pltpu.VMEM((line, 1, plane * slots), f32),
            pltpu.VMEM((line, table, wide), f32),
            pltpu.VMEM((line - 1, table, wide), bf16),
            pltpu.VMEM((line + 1, table, wide), bf16),
            pltpu.VMEM((table - cells, wide), bf16),
            one, dma((line,)),
            one, dma((line,)),
            one, one,
            one, dma((line,)),
            one, one,
            one, dma((line + 1,)),
            one, one,
            pltpu.SemaphoreType.REGULAR, pltpu.SemaphoreType.REGULAR,
        ],
        compiler_params=pltpu.CompilerParams(
            collective_id=0, has_side_effects=True, vmem_limit_bytes=60 * 1024 * 1024
        ),
    )(
        field.reshape(cells, wide),
        obs_cells,
        obs_frac.reshape(total, 2, slots),
        obs_innov.reshape(total, slots),
        obs_rinv.reshape(total, slots),
        obs_jac.reshape(lat_n, line, inner, slots, wide),
    )
    grad, departures = pl.pallas_call(
        functools.partial(last_sums, rows, cols),
        out_shape=(
            jax.ShapeDtypeStruct((cells, wide), f32),
            jax.ShapeDtypeStruct((total, 1, slots), f32),
        ),
        in_specs=[vmem] * 3,
        out_specs=(vmem, vmem),
    )(*parts[:2], parts[2].reshape(total, 1, slots))
    return departures, grad.reshape(rows, cols, wide)


def solution(mesh):
    placed = (
        P("lat", "lon", None),
        P(None, ("lat", "lon"), None, None),
        P(None, ("lat", "lon"), None, None),
        P(None, ("lat", "lon"), None),
        P(None, ("lat", "lon"), None),
        P(None, ("lat", "lon"), None),
    )
    return jax.shard_map(
        functools.partial(shards, (mesh.shape["lat"], mesh.shape["lon"])),
        mesh=mesh,
        in_specs=placed,
        out_specs=(P(None, ("lat", "lon"), None), P("lat", "lon", None)),
        check_vma=False,
    )
```

```python
import functools
import math

import jax
import jax.numpy as jnp
from jax import lax
from jax.experimental import pallas as pl
from jax.experimental.pallas import tpu as pltpu
from jax.sharding import PartitionSpec as P

MESH = pl.DeviceIdType.MESH
AWAY = -1000.0


def visit_order(z, line):
    half = line // 2
    if z < half:
        return [*range(half, line), *(p for p in range(half) if p != z), z]
    return [*range(half - 1, -1, -1), *(p for p in range(half, line) if p != z), z]


def pick(z, values):
    chosen = jnp.int32(values[0])
    for p in range(1, len(values)):
        chosen = jnp.where(z == p, jnp.int32(values[p]), chosen)
    return chosen


def weight_rows(position, frac, rows):
    ids = lax.broadcasted_iota(jnp.int32, (rows, position.shape[1]), 0).astype(jnp.float32)
    zero = jnp.zeros_like(ids)
    return jnp.where(
        ids == position, 1.0 - frac, jnp.where(ids == position + 1.0, frac, zero)
    )


def kernel(
    lat_n, lon_n, line, rows, cols, tile,
    field, cell_ref, frac_ref, innov_ref, rinv_ref, jac,
    gmain, hrecv, dep_out,
    edge, innov, rinv, meta,
    tbl, met, jrecv, dep, part, gsend, rbuf, hsend,
    f_local, f_send, f_recv, e_send, e_recv, m_send, m_recv, j_send, j_recv, d_send, d_recv,
    g_send, g_recv, h_send, h_recv, from_low, from_high,
):
    inner = lon_n // line
    plane = lat_n * inner
    slots = jac.shape[3]
    cells = rows * cols
    halo = cells + cols
    lat, lon = lax.axis_index("lat"), lax.axis_index("lon")
    z, xi = lon // inner, lon % inner
    here = lat * inner + xi
    lat_up, lat_down = (lat + 1) % lat_n, (lat + lat_n - 1) % lat_n
    lon_up, lon_down = (lon + 1) % lon_n, (lon + lon_n - 1) % lon_n
    z_low, x_low = lon_down // inner, lon_down % inner
    orders = [visit_order(p, line) for p in range(line)]
    visits = [pick(z, [order[n] for order in orders]) for n in range(line)]

    def remote(src, dst, send, recv, to):
        return pltpu.make_async_remote_copy(
            src_ref=src, dst_ref=dst, send_sem=send, recv_sem=recv,
            device_id=to, device_id_type=MESH,
        )

    def landed(like, sem):
        pltpu.make_async_copy(like, like, sem).wait()

    def pieces(size):
        cut = -(-size // 32) * 16
        return (pl.ds(0, cut), pl.ds(cut, size - cut))

    field_pieces, table_pieces = pieces(cells), pieces(cells + cols + 2 * rows)

    def mate(i):
        to = (here + i) % plane
        return to, (to // inner, z * inner + to % inner)

    has_low, has_high = z > 0, z < line - 1
    inside_line = has_low & has_high
    low, high = (lat, lon - inner), (lat, lon + inner)
    barrier = pltpu.get_barrier_semaphore()

    @pl.when(has_low)
    def _():
        pl.semaphore_signal(barrier, inc=1, device_id=low, device_id_type=MESH)

    @pl.when(has_high)
    def _():
        pl.semaphore_signal(barrier, inc=1, device_id=high, device_id_type=MESH)

    def greet(i, carry):
        pl.semaphore_signal(barrier, inc=1, device_id=mate(i)[1], device_id_type=MESH)
        return carry

    lax.fori_loop(1, plane, greet, 0)

    own_field = tbl.at[z, pl.ds(0, cells)]
    local = pltpu.make_async_copy(field, own_field, f_local)
    local.start()
    for g in visits:
        pltpu.make_async_copy(
            jac.at[lat, g, xi], jrecv.at[g, pl.ds(0, slots)], j_recv.at[g]
        ).start()

    @pl.when(jnp.logical_not(has_low))
    def _():
        rbuf[z] = jnp.zeros(rbuf.shape[1:], rbuf.dtype)

    @pl.when(jnp.logical_not(has_high))
    def _():
        rbuf[line] = jnp.zeros(rbuf.shape[1:], rbuf.dtype)

    innov[...] = innov_ref[...].astype(jnp.float32)
    rinv[...] = rinv_ref[...].astype(jnp.float32)

    def build(i, carry):
        to, _ = mate(i)
        for g in range(line):
            owner = (to // inner) * lon_n + g * inner + to % inner
            cell = cell_ref[owner].astype(jnp.float32)
            live = cell >= 0.0
            row = jnp.floor((cell + 0.5) * (1.0 / (cols + 1)))
            meta[i, g] = jnp.concatenate(
                [
                    jnp.where(live, row, AWAY),
                    jnp.where(live, cell - row * (cols + 1), AWAY),
                    frac_ref[owner].astype(jnp.float32),
                    innov[pl.ds(owner, 1), :],
                    rinv[pl.ds(owner, 1), :],
                    jnp.zeros((2, slots), jnp.float32),
                ],
                axis=0,
            ).astype(meta.dtype)
        return carry

    lax.fori_loop(0, plane, build, 0)
    local.wait()
    edge[...] = jnp.concatenate(
        [tbl[z, pl.ds(r * cols, cols), :].astype(jnp.float32)[0:1] for r in range(rows)], axis=0
    ).astype(edge.dtype)
    pltpu.make_async_copy(meta.at[0], met.at[:, :, pl.ds(0, slots)], m_recv).start()
    pl.semaphore_wait(barrier, plane - 1 + has_low.astype(jnp.int32) + has_high.astype(jnp.int32))

    def send_field(g, c, up):
        piece = tbl.at[g, field_pieces[c]]
        remote(piece, piece, f_send, f_recv.at[g, c], high if up else low).start()

    for c in range(2):
        @pl.when(has_low)
        def _():
            send_field(z, c, False)

        @pl.when(has_high)
        def _():
            send_field(z, c, True)

    def send_meta(i, carry):
        place = pl.ds(pl.multiple_of(i * slots, slots), slots)
        remote(meta.at[i], met.at[:, :, place], m_send, m_recv, mate(i)[1]).start()
        return carry

    def send_jac(n):
        g = visits[n]

        def one(i, carry):
            to, at = mate(i)
            place = pl.ds(pl.multiple_of(i * slots, slots), slots)
            remote(
                jac.at[to // inner, g, to % inner], jrecv.at[g, place], j_send, j_recv.at[g], at
            ).start()
            return carry

        return one

    lax.fori_loop(1, plane, send_meta, 0)
    lax.fori_loop(1, plane, send_jac(0), 0)

    for _ in range(line - 1):
        @pl.when(has_low)
        def _():
            pl.semaphore_signal(from_high, inc=1, device_id=low, device_id_type=MESH)

        @pl.when(has_high)
        def _():
            pl.semaphore_signal(from_low, inc=1, device_id=high, device_id_type=MESH)

        @pl.when(has_low)
        def _():
            pl.semaphore_wait(from_low, 1)

        @pl.when(has_high)
        def _():
            pl.semaphore_wait(from_high, 1)

    for i in range(line):
        to = (z + i) % line
        remote(tbl.at[z, pl.ds(0, cols)], tbl.at[z, pl.ds(cells, cols)], e_send,
               e_recv.at[z], (lat_down, to * inner + xi)).start()
        remote(edge, tbl.at[z_low, pl.ds(halo, rows)], e_send,
               e_recv.at[z_low], (lat, to * inner + x_low)).start()
        remote(edge, tbl.at[z_low, pl.ds(halo + rows, rows)], e_send,
               e_recv.at[z_low], (lat_down, to * inner + x_low)).start()
    for n in range(1, line):
        lax.fori_loop(1, plane, send_jac(n), 0)

    def field_landed(g, c):
        landed(tbl.at[g, field_pieces[c]], f_recv.at[g, c])

    def forward(d):
        for c in range(2):
            @pl.when(inside_line & (z >= d))
            def _():
                field_landed(z - d, c)
                send_field(z - d, c, True)

            @pl.when(inside_line & (z + d < line))
            def _():
                field_landed(z + d, c)
                send_field(z + d, c, False)

    landed(met, m_recv)
    inside = jnp.where(lat < lat_n - 1, 1.0, 0.0)
    width = tile * slots
    tiles = plane // tile
    pad = -(-(max(rows, cols) + 1) // 8) * 8

    def terms(g, t):
        lanes = pl.ds(pl.multiple_of(t * width, width), width)
        info = met[g, :, lanes].astype(jnp.float32)
        lat_w = weight_rows(info[0:1], info[2:3], pad)
        lon_w = weight_rows(info[1:2], info[3:4], pad)
        lon_c = lon_w[:cols]
        lon_e = lon_w[cols:cols + 1]
        lat_n_row = lat_w[rows:rows + 1] * inside
        first = lax.broadcasted_iota(jnp.int32, (rows, width), 0) == 0
        blocks = [lat_w[r:r + 1] * lon_c for r in range(rows)]
        blocks.append(lat_n_row * lon_c)
        blocks.append(lat_w[:rows] * lon_e)
        blocks.append(
            jnp.where(first, jnp.broadcast_to(lat_n_row * lon_e, (rows, width)), 0.0)
        )
        spread = jnp.concatenate(blocks, axis=0).astype(jnp.bfloat16).astype(jnp.float32)
        jac_t = jrecv[g, lanes]
        products = lax.dot_general(
            tbl[g], jac_t, (((1,), (1,)), ((), ())), preferred_element_type=jnp.float32
        )
        evolved = jnp.sum(spread * products, axis=0, keepdims=True)
        departure = jnp.where(info[0:1] >= 0.0, evolved - info[4:5], 0.0)
        dep[g, :, lanes] = departure
        return (spread * (info[5:6] * departure)).astype(jnp.bfloat16), jac_t

    def compute(n, g):
        into = part.at[n]

        def one_tile(t, carry):
            scaled, jac_t = terms(g, t)
            into[...] += jnp.dot(scaled, jac_t, preferred_element_type=jnp.float32)
            return carry

        if tiles > 1:
            into[...] = jnp.zeros(into.shape, into.dtype)
            lax.fori_loop(0, tiles, one_tile, 0)
        else:
            scaled, jac_t = terms(g, 0)
            into[...] = jnp.dot(scaled, jac_t, preferred_element_type=jnp.float32)

    def send_dep(g):
        def one(i, carry):
            to = (here + plane - i) % plane
            place = pl.ds(pl.multiple_of(i * slots, slots), slots)
            remote(
                dep.at[g, :, place], dep_out.at[lat, g, xi], d_send, d_recv,
                (to // inner, z * inner + to % inner),
            ).start()
            return carry

        lax.fori_loop(1, plane, one, 0)
        pltpu.make_async_copy(dep.at[g, :, pl.ds(0, slots)], dep_out.at[lat, g, xi], d_recv).start()

    def finish(n, incoming):
        g = visits[n]
        up = g > z
        next_z = jnp.where(up, z + 1, z - 1)
        slot = jnp.where((g == next_z) & jnp.logical_not(up), line, g)
        for c, at in enumerate(table_pieces):
            total = part[n, at, :]
            if incoming:
                landed(rbuf.at[g, at], g_recv.at[g, c])
                total = total + rbuf[g, at, :].astype(jnp.float32)
            gsend[n, at, :] = total.astype(gsend.dtype)
            remote(gsend.at[n, at], rbuf.at[slot, at], g_send, g_recv.at[slot, c],
                   (lat, next_z * inner + xi)).start()

    def pass_on(n):
        @pl.when(inside_line)
        def _():
            finish(n, True)

    for d in range(1, max(line // 2, 1)):
        forward(d)
    for n in range(line - 1):
        g = visits[n]

        @pl.when(jnp.logical_not(inside_line))
        def _():
            for c in range(2):
                field_landed(g, c)

        landed(tbl.at[g, pl.ds(cells, cols + 2 * rows)], e_recv.at[g])
        landed(jrecv.at[g], j_recv.at[g])
        compute(n, g)
        send_dep(g)

        @pl.when(jnp.logical_not(inside_line))
        def _():
            finish(n, False)

        if n == 0:
            for d in range(max(line // 2, 1), line - 1):
                forward(d)
        elif n == 1:
            pass_on(0)
            pass_on(1)
        else:
            pass_on(n)

    main, rim = pl.ds(0, cells), pl.ds(cells, cols + 2 * rows)
    landed(tbl.at[z, rim], e_recv.at[z])
    landed(jrecv.at[z], j_recv.at[z])

    def arrived(at):
        return rbuf[z, at, :].astype(jnp.float32) + rbuf[line, at, :].astype(jnp.float32)

    def send_rim(values):
        for c, at in enumerate(table_pieces):
            @pl.when(has_low)
            def _():
                landed(rbuf.at[z, at], g_recv.at[z, c])

            @pl.when(has_high)
            def _():
                landed(rbuf.at[line, at], g_recv.at[line, c])

        hsend[...] = (values + arrived(rim)).astype(hsend.dtype)
        remote(hsend.at[pl.ds(cols + rows, rows)], hrecv.at[2], h_send, h_recv,
               (lat_up, lon_up)).start()
        remote(hsend.at[pl.ds(cols, rows)], hrecv.at[1], h_send, h_recv, (lat, lon_up)).start()
        remote(hsend.at[pl.ds(0, cols)], hrecv.at[0], h_send, h_recv, (lat_up, lon)).start()

    if tiles > 1:
        compute(line - 1, z)
        send_rim(part[line - 1, rim, :])
        send_dep(z)
        gmain[...] = part[line - 1, main, :] + arrived(main)
    else:
        scaled, jac_t = terms(z, 0)
        send_rim(jnp.dot(scaled[cells:], jac_t, preferred_element_type=jnp.float32))
        send_dep(z)
        gmain[...] = arrived(main) + jnp.dot(
            scaled[:cells], jac_t, preferred_element_type=jnp.float32
        )

    others = pl.ds(0, (plane - 1) * slots)
    for up in (False, True):
        for i in range(line):
            sent = (z >= i) & has_high if up else (z + i < line) & has_low

            @pl.when(sent & (inside_line | (i == 0)))
            def _():
                landed(own_field, f_send)
    landed(tbl.at[:, pl.ds(cells, cols + 2 * rows)], e_send)
    landed(met.at[:, :, others], m_send)
    landed(jrecv.at[:, others], j_send)
    landed(dep.at[:, :, others], d_send)
    landed(gsend, g_send)
    landed(hsend, h_send)
    landed(hrecv, h_recv)
    landed(dep_out, d_recv)


def last_sums(rows, cols, gmain, hrecv, dep, grad_out, dep_out):
    dep_out[...] = dep[...]
    grad_out[...] = gmain[...]
    grad_out[pl.ds(0, cols), :] += hrecv[0].astype(jnp.float32)
    east = hrecv[1].astype(jnp.float32)
    corner = hrecv[2].astype(jnp.float32)
    for r in range(rows):
        extra = east[r:r + 1]
        if r == 0:
            extra = extra + corner[0:1]
        grad_out[pl.ds(r * cols, 1), :] += extra


def shards(mesh_shape, field, obs_jac, obs_frac, obs_innov, obs_rinv, obs_cells):
    lat_n, lon_n = mesh_shape
    line = math.gcd(lon_n // 2, 4)
    inner = lon_n // line
    plane = lat_n * inner
    total = lat_n * lon_n
    rows, cols, wide = field.shape
    slots = obs_jac.shape[2]
    tile = math.gcd(plane, 8)
    cells = rows * cols
    table = cells + cols + 2 * rows
    f32, bf16 = jnp.float32, jnp.bfloat16
    dma = pltpu.SemaphoreType.DMA
    one = pltpu.SemaphoreType.DMA(())
    vmem = pl.BlockSpec(memory_space=pltpu.VMEM)
    anywhere = pl.BlockSpec(memory_space=pltpu.HBM)
    parts = pl.pallas_call(
        functools.partial(kernel, lat_n, lon_n, line, rows, cols, tile),
        out_shape=(
            pltpu.VMEM((cells, wide), f32),
            pltpu.VMEM((3, rows, wide), bf16),
            pltpu.VMEM((lat_n, line, inner, 1, slots), f32),
        ),
        in_specs=[anywhere, vmem, vmem, vmem, vmem, anywhere],
        out_specs=(vmem,) * 3,
        scratch_shapes=[
            pltpu.VMEM((rows, wide), bf16),
            pltpu.VMEM((total, slots), f32),
            pltpu.VMEM((total, slots), f32),
            pltpu.VMEM((plane, line, 8, slots), bf16),
            pltpu.VMEM((line, table, wide), bf16),
            pltpu.VMEM((line, 8, plane * slots), bf16),
            pltpu.VMEM((line, plane * slots, wide), bf16),
            pltpu.VMEM((line, 1, plane * slots), f32),
            pltpu.VMEM((line, table, wide), f32),
            pltpu.VMEM((line - 1, table, wide), bf16),
            pltpu.VMEM((line + 1, table, wide), bf16),
            pltpu.VMEM((table - cells, wide), bf16),
            one, one, dma((line, 2)),
            one, dma((line,)),
            one, one,
            one, dma((line,)),
            one, one,
            one, dma((line + 1, 2)),
            one, one,
            pltpu.SemaphoreType.REGULAR, pltpu.SemaphoreType.REGULAR,
        ],
        compiler_params=pltpu.CompilerParams(
            collective_id=0, has_side_effects=True, vmem_limit_bytes=62 * 1024 * 1024
        ),
    )(
        field.reshape(cells, wide),
        obs_cells,
        obs_frac.reshape(total, 2, slots),
        obs_innov.reshape(total, slots),
        obs_rinv.reshape(total, slots),
        obs_jac.reshape(lat_n, line, inner, slots, wide),
    )
    grad, departures = pl.pallas_call(
        functools.partial(last_sums, rows, cols),
        out_shape=(
            jax.ShapeDtypeStruct((cells, wide), f32),
            jax.ShapeDtypeStruct((total, 1, slots), f32),
        ),
        in_specs=[vmem] * 3,
        out_specs=(vmem, vmem),
        compiler_params=pltpu.CompilerParams(vmem_limit_bytes=8 * 1024 * 1024),
    )(*parts[:2], parts[2].reshape(total, 1, slots))
    return departures, grad.reshape(rows, cols, wide)


def solution(mesh):
    placed = (
        P("lat", "lon", None),
        P(None, ("lat", "lon"), None, None),
        P(None, ("lat", "lon"), None, None),
        P(None, ("lat", "lon"), None),
        P(None, ("lat", "lon"), None),
        P(None, ("lat", "lon"), None),
    )
    return jax.shard_map(
        functools.partial(shards, (mesh.shape["lat"], mesh.shape["lon"])),
        mesh=mesh,
        in_specs=placed,
        out_specs=(P(None, ("lat", "lon"), None), P("lat", "lon", None)),
        check_vma=False,
    )
```

```python
import functools
import math

import jax
import jax.numpy as jnp
from jax import lax
from jax.experimental import pallas as pl
from jax.experimental.pallas import tpu as pltpu
from jax.sharding import PartitionSpec as P

MESH = pl.DeviceIdType.MESH
AWAY = -1000.0


def visit_order(z, line):
    half = line // 2
    if z < half:
        return [*range(half, line), *(p for p in range(half) if p != z), z]
    return [*range(half - 1, -1, -1), *(p for p in range(half, line) if p != z), z]


def pick(z, values):
    chosen = jnp.int32(values[0])
    for p in range(1, len(values)):
        chosen = jnp.where(z == p, jnp.int32(values[p]), chosen)
    return chosen


def weight_rows(position, frac, rows):
    ids = lax.broadcasted_iota(jnp.int32, (rows, position.shape[1]), 0).astype(jnp.float32)
    zero = jnp.zeros_like(ids)
    return jnp.where(
        ids == position, 1.0 - frac, jnp.where(ids == position + 1.0, frac, zero)
    )


def kernel(
    lat_n, lon_n, line, rows, cols, tile,
    field, cell_ref, frac_ref, innov_ref, rinv_ref, jac,
    gmain, hrecv, dep_out,
    edge, innov, rinv, meta,
    tbl, met, jrecv, dep, part, gsend, rbuf, hsend,
    f_local, f_send, f_recv, e_send, e_own, b_send, e_recv, m_send, m_recv, j_send, j_recv, d_send, d_recv,
    g_send, g_recv, h_send, h_recv, from_low, from_high,
):
    inner = lon_n // line
    plane = lat_n * inner
    slots = jac.shape[3]
    cells = rows * cols
    halo = cells + cols
    lat, lon = lax.axis_index("lat"), lax.axis_index("lon")
    z, xi = lon // inner, lon % inner
    here = lat * inner + xi
    lat_up, lat_down = (lat + 1) % lat_n, (lat + lat_n - 1) % lat_n
    lon_up, lon_down = (lon + 1) % lon_n, (lon + lon_n - 1) % lon_n
    z_low, x_low = lon_down // inner, lon_down % inner
    orders = [visit_order(p, line) for p in range(line)]
    visits = [pick(z, [order[n] for order in orders]) for n in range(line)]

    def remote(src, dst, send, recv, to):
        return pltpu.make_async_remote_copy(
            src_ref=src, dst_ref=dst, send_sem=send, recv_sem=recv,
            device_id=to, device_id_type=MESH,
        )

    def landed(like, sem):
        pltpu.make_async_copy(like, like, sem).wait()

    def pieces(size):
        cut = -(-size // 32) * 16
        return (pl.ds(0, cut), pl.ds(cut, size - cut))

    field_pieces, table_pieces = pieces(cells), pieces(cells + cols + 2 * rows)

    def mate(i):
        to = (here + i) % plane
        return to, (to // inner, z * inner + to % inner)

    has_low, has_high = z > 0, z < line - 1
    inside_line = has_low & has_high
    low, high = (lat, lon - inner), (lat, lon + inner)
    barrier = pltpu.get_barrier_semaphore()

    @pl.when(has_low)
    def _():
        pl.semaphore_signal(barrier, inc=1, device_id=low, device_id_type=MESH)

    @pl.when(has_high)
    def _():
        pl.semaphore_signal(barrier, inc=1, device_id=high, device_id_type=MESH)

    def greet(i, carry):
        pl.semaphore_signal(barrier, inc=1, device_id=mate(i)[1], device_id_type=MESH)
        return carry

    lax.fori_loop(1, plane, greet, 0)

    own_field = tbl.at[z, pl.ds(0, cells)]
    local = pltpu.make_async_copy(field, own_field, f_local)
    local.start()
    for g in visits:
        pltpu.make_async_copy(
            jac.at[lat, g, xi], jrecv.at[g, pl.ds(0, slots)], j_recv.at[g, 0]
        ).start()

    @pl.when(jnp.logical_not(has_low))
    def _():
        rbuf[z] = jnp.zeros(rbuf.shape[1:], rbuf.dtype)

    @pl.when(jnp.logical_not(has_high))
    def _():
        rbuf[line] = jnp.zeros(rbuf.shape[1:], rbuf.dtype)

    has_south, has_north = lat > 0, lat < lat_n - 1
    row_rim, edge_rim = pl.ds(cells, cols), pl.ds(halo, rows)
    corner_rim, rim = pl.ds(halo + rows, rows), pl.ds(cells, cols + 2 * rows)

    @pl.when(jnp.logical_not(has_north))
    def _():
        tbl[z, row_rim, :] = jnp.zeros((cols, tbl.shape[2]), tbl.dtype)
        tbl[z, corner_rim, :] = jnp.zeros((rows, tbl.shape[2]), tbl.dtype)

    @pl.when(jnp.logical_not(has_south))
    def _():
        hrecv[0] = jnp.zeros(hrecv.shape[1:], hrecv.dtype)
        hrecv[2] = jnp.zeros(hrecv.shape[1:], hrecv.dtype)

    innov[...] = innov_ref[...].astype(jnp.float32)
    rinv[...] = rinv_ref[...].astype(jnp.float32)

    def build(i, carry):
        to, _ = mate(i)
        for g in range(line):
            owner = (to // inner) * lon_n + g * inner + to % inner
            cell = cell_ref[owner].astype(jnp.float32)
            live = cell >= 0.0
            row = jnp.floor((cell + 0.5) * (1.0 / (cols + 1)))
            meta[i, g] = jnp.concatenate(
                [
                    jnp.where(live, row, AWAY),
                    jnp.where(live, cell - row * (cols + 1), AWAY),
                    frac_ref[owner].astype(jnp.float32),
                    innov[pl.ds(owner, 1), :],
                    rinv[pl.ds(owner, 1), :],
                    jnp.zeros((2, slots), jnp.float32),
                ],
                axis=0,
            ).astype(meta.dtype)
        return carry

    lax.fori_loop(0, plane, build, 0)
    local.wait()
    edge[...] = jnp.concatenate(
        [tbl[z, pl.ds(r * cols, cols), :].astype(jnp.float32)[0:1] for r in range(rows)], axis=0
    ).astype(edge.dtype)
    pltpu.make_async_copy(meta.at[0], met.at[:, :, pl.ds(0, slots)], m_recv).start()
    pl.semaphore_wait(barrier, plane - 1 + has_low.astype(jnp.int32) + has_high.astype(jnp.int32))

    def send_field(g, c, up):
        piece = tbl.at[g, field_pieces[c]]
        remote(piece, piece, f_send, f_recv.at[g, c], high if up else low).start()

    def send_meta(i, carry):
        place = pl.ds(pl.multiple_of(i * slots, slots), slots)
        remote(meta.at[i], met.at[:, :, place], m_send, m_recv, mate(i)[1]).start()
        return carry

    half = plane // 2

    def jac_landed(g, h):
        landed(jrecv.at[g, pl.ds(h * half * slots, half * slots)], j_recv.at[g, h])

    def send_jac(n):
        g = visits[n]

        def one(i, carry):
            to, at = mate(i)
            place = pl.ds(pl.multiple_of(i * slots, slots), slots)
            remote(
                jac.at[to // inner, g, to % inner], jrecv.at[g, place], j_send,
                j_recv.at[g, i // half], at
            ).start()
            return carry

        return one

    def send_edge():
        remote(edge, tbl.at[z_low, edge_rim], e_send, e_own, (lat, lon_down)).start()

        @pl.when(has_south)
        def _():
            remote(edge, tbl.at[z_low, corner_rim], e_send, e_own, (lat_down, lon_down)).start()

    early = plane - plane // 4
    lax.fori_loop(1, plane, send_meta, 0)
    lax.fori_loop(1, 3, send_jac(0), 0)
    for c in range(2):
        @pl.when(has_low)
        def _():
            send_field(z, c, False)

        @pl.when(has_high)
        def _():
            send_field(z, c, True)

    @pl.when(has_south)
    def _():
        remote(tbl.at[z, pl.ds(0, cols)], tbl.at[z, row_rim], e_send, e_own,
               (lat_down, lon)).start()

    @pl.when(xi > 0)
    def _():
        send_edge()

    lax.fori_loop(3, early, send_jac(0), 0)

    for _ in range(line - 1):
        @pl.when(has_low)
        def _():
            pl.semaphore_signal(from_high, inc=1, device_id=low, device_id_type=MESH)

        @pl.when(has_high)
        def _():
            pl.semaphore_signal(from_low, inc=1, device_id=high, device_id_type=MESH)

        @pl.when(has_low)
        def _():
            pl.semaphore_wait(from_low, 1)

        @pl.when(has_high)
        def _():
            pl.semaphore_wait(from_high, 1)

    @pl.when(xi == 0)
    def _():
        send_edge()

    lax.fori_loop(early, plane, send_jac(0), 0)
    for n in range(1, line):
        lax.fori_loop(1, plane, send_jac(n), 0)

    def field_landed(g, c):
        landed(tbl.at[g, field_pieces[c]], f_recv.at[g, c])

    def forward(d):
        for c in range(2):
            @pl.when(inside_line & (z >= d))
            def _():
                field_landed(z - d, c)
                send_field(z - d, c, True)

            @pl.when(inside_line & (z + d < line))
            def _():
                field_landed(z + d, c)
                send_field(z + d, c, False)

    inside = jnp.where(lat < lat_n - 1, 1.0, 0.0)
    width = tile * slots
    tiles = plane // tile
    pad = -(-(max(rows, cols) + 1) // 8) * 8

    def terms(g, t, width):
        lanes = pl.ds(pl.multiple_of(t * width, width), width)
        info = met[g, :, lanes].astype(jnp.float32)
        lat_w = weight_rows(info[0:1], info[2:3], pad)
        lon_w = weight_rows(info[1:2], info[3:4], pad)
        lon_c = lon_w[:cols]
        lon_e = lon_w[cols:cols + 1]
        lat_n_row = lat_w[rows:rows + 1] * inside
        first = lax.broadcasted_iota(jnp.int32, (rows, width), 0) == 0
        blocks = [lat_w[r:r + 1] * lon_c for r in range(rows)]
        blocks.append(lat_n_row * lon_c)
        blocks.append(lat_w[:rows] * lon_e)
        blocks.append(
            jnp.where(first, jnp.broadcast_to(lat_n_row * lon_e, (rows, width)), 0.0)
        )
        spread = jnp.concatenate(blocks, axis=0).astype(jnp.bfloat16).astype(jnp.float32)
        jac_t = jrecv[g, lanes]
        products = lax.dot_general(
            tbl[g], jac_t, (((1,), (1,)), ((), ())), preferred_element_type=jnp.float32
        )
        evolved = jnp.sum(spread * products, axis=0, keepdims=True)
        departure = jnp.where(info[0:1] >= 0.0, evolved - info[4:5], 0.0)
        dep[g, :, lanes] = departure
        return (spread * (info[5:6] * departure)).astype(jnp.bfloat16), jac_t

    def compute(n, g):
        into = part.at[n]

        def one_tile(t, carry):
            scaled, jac_t = terms(g, t, width)
            into[...] += jnp.dot(scaled, jac_t, preferred_element_type=jnp.float32)
            return carry

        if tiles > 1:
            into[...] = jnp.zeros(into.shape, into.dtype)
            lax.fori_loop(0, tiles, one_tile, 0)
        else:
            scaled, jac_t = terms(g, 0, width)
            into[...] = jnp.dot(scaled, jac_t, preferred_element_type=jnp.float32)

    def send_dep(g, first, last):
        def one(i, carry):
            to = (here + plane - i) % plane
            place = pl.ds(pl.multiple_of(i * slots, slots), slots)
            remote(
                dep.at[g, :, place], dep_out.at[lat, g, xi], d_send, d_recv,
                (to // inner, z * inner + to % inner),
            ).start()
            return carry

        lax.fori_loop(max(first, 1), last, one, 0)
        if first == 0:
            pltpu.make_async_copy(
                dep.at[g, :, pl.ds(0, slots)], dep_out.at[lat, g, xi], d_recv
            ).start()

    def finish(n, incoming):
        g = visits[n]
        up = g > z
        next_z = jnp.where(up, z + 1, z - 1)
        slot = jnp.where((g == next_z) & jnp.logical_not(up), line, g)
        for c, at in enumerate(table_pieces):
            total = part[n, at, :]
            if incoming:
                landed(rbuf.at[g, at], g_recv.at[g, c])
                total = total + rbuf[g, at, :].astype(jnp.float32)
            gsend[n, at, :] = total.astype(gsend.dtype)
            remote(gsend.at[n, at], rbuf.at[slot, at], g_send, g_recv.at[slot, c],
                   (lat, next_z * inner + xi)).start()

    def pass_on(n):
        @pl.when(inside_line)
        def _():
            finish(n, True)

    for d in range(1, max(line // 2, 1)):
        forward(d)

    @pl.when(has_north)
    def _():
        landed(tbl.at[z, rim], e_own)

    @pl.when(jnp.logical_not(has_north))
    def _():
        landed(edge, e_own)

    for i in range(1, line):
        remote(tbl.at[z, rim], tbl.at[z, rim], b_send, e_recv.at[z],
               (lat, (z + i) % line * inner + xi)).start()
    landed(met, m_recv)
    for n in range(line - 1):
        g = visits[n]

        @pl.when(jnp.logical_not(inside_line))
        def _():
            for c in range(2):
                field_landed(g, c)

        landed(tbl.at[g, rim], e_recv.at[g])
        jac_landed(g, 0)
        jac_landed(g, 1)
        compute(n, g)
        send_dep(g, 0, plane)

        @pl.when(jnp.logical_not(inside_line))
        def _():
            finish(n, False)

        if n == 0:
            for d in range(max(line // 2, 1), line - 1):
                forward(d)
        elif n == 1:
            pass_on(0)
            pass_on(1)
        else:
            pass_on(n)

    main = pl.ds(0, cells)

    def arrived(at):
        return rbuf[z, at, :].astype(jnp.float32) + rbuf[line, at, :].astype(jnp.float32)

    def send_rim(values):
        for c, at in enumerate(table_pieces):
            @pl.when(has_low)
            def _():
                landed(rbuf.at[z, at], g_recv.at[z, c])

            @pl.when(has_high)
            def _():
                landed(rbuf.at[line, at], g_recv.at[line, c])

        hsend[...] = (values + arrived(rim)).astype(hsend.dtype)
        remote(hsend.at[pl.ds(cols, rows)], hrecv.at[1], h_send, h_recv, (lat, lon_up)).start()

        @pl.when(has_north)
        def _():
            remote(hsend.at[pl.ds(cols + rows, rows)], hrecv.at[2], h_send, h_recv,
                   (lat_up, lon_up)).start()
            remote(hsend.at[pl.ds(0, cols)], hrecv.at[0], h_send, h_recv, (lat_up, lon)).start()

    if tiles > 1:
        jac_landed(z, 0)
        jac_landed(z, 1)
        compute(line - 1, z)
        send_rim(part[line - 1, rim, :])
        send_dep(z, 0, plane)
        gmain[...] = part[line - 1, main, :] + arrived(main)
    else:
        jac_landed(z, 0)
        scaled, jac_t = terms(z, 0, half * slots)
        part[line - 1] = jnp.dot(scaled, jac_t, preferred_element_type=jnp.float32)
        send_dep(z, 0, half)
        jac_landed(z, 1)
        scaled, jac_t = terms(z, 1, half * slots)
        send_rim(part[line - 1, rim, :] + jnp.dot(
            scaled[cells:], jac_t, preferred_element_type=jnp.float32
        ))
        send_dep(z, half, plane)
        gmain[...] = arrived(main) + part[line - 1, main, :] + jnp.dot(
            scaled[:cells], jac_t, preferred_element_type=jnp.float32
        )

    others = pl.ds(0, (plane - 1) * slots)
    for up in (False, True):
        for i in range(line):
            sent = (z >= i) & has_high if up else (z + i < line) & has_low

            @pl.when(sent & (inside_line | (i == 0)))
            def _():
                landed(own_field, f_send)
    @pl.when(has_south)
    def _():
        landed(tbl.at[z, rim], e_send)

    @pl.when(jnp.logical_not(has_south))
    def _():
        landed(edge, e_send)

    landed(tbl.at[pl.ds(0, line - 1), rim], b_send)
    landed(met.at[:, :, others], m_send)
    landed(jrecv.at[:, others], j_send)
    landed(dep.at[:, :, others], d_send)
    landed(gsend, g_send)
    @pl.when(has_north)
    def _():
        landed(hsend, h_send)

    @pl.when(jnp.logical_not(has_north))
    def _():
        landed(edge, h_send)

    @pl.when(has_south)
    def _():
        landed(hrecv, h_recv)

    @pl.when(jnp.logical_not(has_south))
    def _():
        landed(edge, h_recv)

    landed(dep_out, d_recv)


def last_sums(rows, cols, gmain, hrecv, dep, grad_out, dep_out):
    dep_out[...] = dep[...]
    grad_out[...] = gmain[...]
    grad_out[pl.ds(0, cols), :] += hrecv[0].astype(jnp.float32)
    east = hrecv[1].astype(jnp.float32)
    corner = hrecv[2].astype(jnp.float32)
    for r in range(rows):
        extra = east[r:r + 1]
        if r == 0:
            extra = extra + corner[0:1]
        grad_out[pl.ds(r * cols, 1), :] += extra


def shards(mesh_shape, field, obs_jac, obs_frac, obs_innov, obs_rinv, obs_cells):
    lat_n, lon_n = mesh_shape
    line = math.gcd(lon_n // 2, 4)
    inner = lon_n // line
    plane = lat_n * inner
    total = lat_n * lon_n
    rows, cols, wide = field.shape
    slots = obs_jac.shape[2]
    tile = math.gcd(plane, 8)
    cells = rows * cols
    table = cells + cols + 2 * rows
    f32, bf16 = jnp.float32, jnp.bfloat16
    dma = pltpu.SemaphoreType.DMA
    one = pltpu.SemaphoreType.DMA(())
    vmem = pl.BlockSpec(memory_space=pltpu.VMEM)
    anywhere = pl.BlockSpec(memory_space=pltpu.HBM)
    parts = pl.pallas_call(
        functools.partial(kernel, lat_n, lon_n, line, rows, cols, tile),
        out_shape=(
            pltpu.VMEM((cells, wide), f32),
            pltpu.VMEM((3, rows, wide), bf16),
            pltpu.VMEM((lat_n, line, inner, 1, slots), f32),
        ),
        in_specs=[anywhere, vmem, vmem, vmem, vmem, anywhere],
        out_specs=(vmem,) * 3,
        scratch_shapes=[
            pltpu.VMEM((rows, wide), bf16),
            pltpu.VMEM((total, slots), f32),
            pltpu.VMEM((total, slots), f32),
            pltpu.VMEM((plane, line, 8, slots), bf16),
            pltpu.VMEM((line, table, wide), bf16),
            pltpu.VMEM((line, 8, plane * slots), bf16),
            pltpu.VMEM((line, plane * slots, wide), bf16),
            pltpu.VMEM((line, 1, plane * slots), f32),
            pltpu.VMEM((line, table, wide), f32),
            pltpu.VMEM((line - 1, table, wide), bf16),
            pltpu.VMEM((line + 1, table, wide), bf16),
            pltpu.VMEM((table - cells, wide), bf16),
            one, one, dma((line, 2)),
            one, one, one, dma((line,)),
            one, one,
            one, dma((line, 2)),
            one, one,
            one, dma((line + 1, 2)),
            one, one,
            pltpu.SemaphoreType.REGULAR, pltpu.SemaphoreType.REGULAR,
        ],
        compiler_params=pltpu.CompilerParams(
            collective_id=0, has_side_effects=True, vmem_limit_bytes=62 * 1024 * 1024
        ),
    )(
        field.reshape(cells, wide),
        obs_cells,
        obs_frac.reshape(total, 2, slots),
        obs_innov.reshape(total, slots),
        obs_rinv.reshape(total, slots),
        obs_jac.reshape(lat_n, line, inner, slots, wide),
    )
    grad, departures = pl.pallas_call(
        functools.partial(last_sums, rows, cols),
        out_shape=(
            jax.ShapeDtypeStruct((cells, wide), f32),
            jax.ShapeDtypeStruct((total, 1, slots), f32),
        ),
        in_specs=[vmem] * 3,
        out_specs=(vmem, vmem),
        compiler_params=pltpu.CompilerParams(vmem_limit_bytes=8 * 1024 * 1024),
    )(*parts[:2], parts[2].reshape(total, 1, slots))
    return departures, grad.reshape(rows, cols, wide)


def solution(mesh):
    placed = (
        P("lat", "lon", None),
        P(None, ("lat", "lon"), None, None),
        P(None, ("lat", "lon"), None, None),
        P(None, ("lat", "lon"), None),
        P(None, ("lat", "lon"), None),
        P(None, ("lat", "lon"), None),
    )
    return jax.shard_map(
        functools.partial(shards, (mesh.shape["lat"], mesh.shape["lon"])),
        mesh=mesh,
        in_specs=placed,
        out_specs=(P(None, ("lat", "lon"), None), P("lat", "lon", None)),
        check_vma=False,
    )
```

```python
import functools
import math

import jax
import jax.numpy as jnp
from jax import lax
from jax.experimental import pallas as pl
from jax.experimental.pallas import tpu as pltpu
from jax.sharding import PartitionSpec as P

MESH = pl.DeviceIdType.MESH
AWAY = -1000.0


def visit_order(z, line):
    half = line // 2
    if z < half:
        return [*range(half, line), *(p for p in range(half) if p != z), z]
    return [*range(half - 1, -1, -1), *(p for p in range(half, line) if p != z), z]


def pick(z, values):
    chosen = jnp.int32(values[0])
    for p in range(1, len(values)):
        chosen = jnp.where(z == p, jnp.int32(values[p]), chosen)
    return chosen


def weight_rows(position, frac, rows):
    ids = lax.broadcasted_iota(jnp.int32, (rows, position.shape[1]), 0).astype(jnp.float32)
    zero = jnp.zeros_like(ids)
    return jnp.where(
        ids == position, 1.0 - frac, jnp.where(ids == position + 1.0, frac, zero)
    )


def kernel(
    lat_n, lon_n, line, rows, cols, tile,
    field, cell_ref, frac_ref, innov_ref, rinv_ref, jac,
    gmain, hrecv, dep_out,
    edge, innov, rinv, meta, lent,
    tbl, met, jrecv, dep, part, gsend, rbuf, hsend,
    f_local, f_send, f_recv, e_send, e_own, b_send, e_recv, m_send, m_recv, l_send, l_recv, s_send, s_recv, j_send, j_recv, d_send, d_recv,
    g_send, g_recv, h_send, h_recv, from_low, from_high,
):
    inner = lon_n // line
    plane = lat_n * inner
    slots = jac.shape[3]
    cells = rows * cols
    halo = cells + cols
    lat, lon = lax.axis_index("lat"), lax.axis_index("lon")
    z, xi = lon // inner, lon % inner
    here = lat * inner + xi
    lat_up, lat_down = (lat + 1) % lat_n, (lat + lat_n - 1) % lat_n
    lon_up, lon_down = (lon + 1) % lon_n, (lon + lon_n - 1) % lon_n
    z_low, x_low = lon_down // inner, lon_down % inner
    orders = [visit_order(p, line) for p in range(line)]
    visits = [pick(z, [order[n] for order in orders]) for n in range(line)]

    def remote(src, dst, send, recv, to):
        return pltpu.make_async_remote_copy(
            src_ref=src, dst_ref=dst, send_sem=send, recv_sem=recv,
            device_id=to, device_id_type=MESH,
        )

    def landed(like, sem):
        pltpu.make_async_copy(like, like, sem).wait()

    def pieces(size, count):
        cuts = [-(-size * c // (16 * count)) * 16 for c in range(count)] + [size]
        return [pl.ds(a, b - a) for a, b in zip(cuts, cuts[1:])]

    field_pieces = pieces(cells, f_recv.shape[1])
    table_pieces = [pl.ds(cells, cols + 2 * rows), *pieces(cells, g_recv.shape[1] - 1)]

    def mate(i):
        to_lat, to_x = (lat + i // inner) % lat_n, (xi + i % inner) % inner
        return to_lat, to_x, (to_lat, z * inner + to_x)

    def lent_out(i, g):
        return (z == line - 1) & (i == moved) & (g == there)

    def source(i):
        return (lat + lat_n - i // inner) % lat_n, (xi + inner - i % inner) % inner

    moved = (lat_n // 2) * inner + inner // 2
    there = jnp.where(lat % 2 == 0, line - 2, max(line - 3, 0))
    lender, taker = z == line - 1, z == there
    spare = pl.ds(plane * slots, slots)

    has_low, has_high = z > 0, z < line - 1
    inside_line = has_low & has_high
    low, high = (lat, lon - inner), (lat, lon + inner)
    barrier = pltpu.get_barrier_semaphore()

    @pl.when(has_low)
    def _():
        pl.semaphore_signal(barrier, inc=1, device_id=low, device_id_type=MESH)

    @pl.when(has_high)
    def _():
        pl.semaphore_signal(barrier, inc=1, device_id=high, device_id_type=MESH)

    def greet(i, carry):
        pl.semaphore_signal(barrier, inc=1, device_id=mate(i)[2], device_id_type=MESH)
        return carry

    lax.fori_loop(1, plane, greet, 0)

    own_field = tbl.at[z, pl.ds(0, cells)]
    local = pltpu.make_async_copy(field, own_field, f_local)
    local.start()
    for g in visits:
        pltpu.make_async_copy(
            jac.at[lat, g, xi], jrecv.at[g, pl.ds(0, slots)], j_recv.at[g, 0]
        ).start()

    @pl.when(jnp.logical_not(has_low))
    def _():
        rbuf[z] = jnp.zeros(rbuf.shape[1:], rbuf.dtype)

    @pl.when(jnp.logical_not(has_high))
    def _():
        rbuf[line] = jnp.zeros(rbuf.shape[1:], rbuf.dtype)

    has_south, has_north = lat > 0, lat < lat_n - 1
    row_rim, edge_rim = pl.ds(cells, cols), pl.ds(halo, rows)
    corner_rim, rim = pl.ds(halo + rows, rows), pl.ds(cells, cols + 2 * rows)

    @pl.when(jnp.logical_not(has_north))
    def _():
        tbl[z, row_rim, :] = jnp.zeros((cols, tbl.shape[2]), tbl.dtype)
        tbl[z, corner_rim, :] = jnp.zeros((rows, tbl.shape[2]), tbl.dtype)

    @pl.when(jnp.logical_not(has_south))
    def _():
        hrecv[0] = jnp.zeros(hrecv.shape[1:], hrecv.dtype)
        hrecv[2] = jnp.zeros(hrecv.shape[1:], hrecv.dtype)

    innov[...] = innov_ref[...].astype(jnp.float32)
    rinv[...] = rinv_ref[...].astype(jnp.float32)

    def build(i, carry):
        to_lat, to_x, _ = mate(i)
        for g in range(line):
            owner = to_lat * lon_n + g * inner + to_x
            cell = cell_ref[owner].astype(jnp.float32)
            live = cell >= 0.0
            row = jnp.floor((cell + 0.5) * (1.0 / (cols + 1)))
            meta[i, g] = jnp.concatenate(
                [
                    jnp.where(live, row, AWAY),
                    jnp.where(live, cell - row * (cols + 1), AWAY),
                    frac_ref[owner].astype(jnp.float32),
                    innov[pl.ds(owner, 1), :],
                    rinv[pl.ds(owner, 1), :],
                    jnp.zeros((2, slots), jnp.float32),
                ],
                axis=0,
            ).astype(meta.dtype)
        return carry

    lax.fori_loop(0, plane, build, 0)

    @pl.when(lender)
    def _():
        lent[...] = meta[moved, there]
        meta[moved, there] = jnp.full(lent.shape, AWAY, lent.dtype)
        jrecv[there, pl.ds(moved * slots, slots), :] = jnp.zeros(
            (slots, jrecv.shape[2]), jrecv.dtype
        )

    local.wait()
    edge[...] = jnp.concatenate(
        [tbl[z, pl.ds(r * cols, cols), :].astype(jnp.float32)[0:1] for r in range(rows)], axis=0
    ).astype(edge.dtype)
    pltpu.make_async_copy(meta.at[0], met.at[:, :, pl.ds(0, slots)], m_recv).start()
    pl.semaphore_wait(barrier, plane - 1 + has_low.astype(jnp.int32) + has_high.astype(jnp.int32))

    def send_field(g, c, up):
        piece = tbl.at[g, field_pieces[c]]
        remote(piece, piece, f_send, f_recv.at[g, c], high if up else low).start()

    def send_meta(i, carry):
        place = pl.ds(pl.multiple_of(i * slots, slots), slots)
        remote(meta.at[i], met.at[:, :, place], m_send, m_recv, mate(i)[2]).start()
        return carry

    half = plane // 2

    def jac_landed(g, h):
        landed(jrecv.at[g, pl.ds(h * half * slots, half * slots)], j_recv.at[g, h])

    def send_jac(n):
        g = visits[n]

        def one(i, carry):
            @pl.when(jnp.logical_not(lent_out(i, g)))
            def _():
                to_lat, to_x, at = mate(i)
                place = pl.ds(pl.multiple_of(i * slots, slots), slots)
                remote(
                    jac.at[to_lat, g, to_x], jrecv.at[g, place], j_send,
                    j_recv.at[g, i // half], at,
                ).start()

            return carry

        return one

    def send_edge():
        remote(edge, tbl.at[z_low, edge_rim], e_send, e_own, (lat, lon_down)).start()

        @pl.when(has_south)
        def _():
            remote(edge, tbl.at[z_low, corner_rim], e_send, e_own, (lat_down, lon_down)).start()

    early = plane - plane // 4
    lax.fori_loop(1, plane, send_meta, 0)
    lax.fori_loop(1, 3, send_jac(0), 0)
    for c in range(len(field_pieces)):
        @pl.when(has_low & (z >= line // 2))
        def _():
            send_field(z, c, False)

        @pl.when(has_high & (z < line // 2))
        def _():
            send_field(z, c, True)

    @pl.when(has_south)
    def _():
        remote(tbl.at[z, pl.ds(0, cols)], tbl.at[z, row_rim], e_send, e_own,
               (lat_down, lon)).start()

    @pl.when(xi > 0)
    def _():
        send_edge()

    lax.fori_loop(3, early, send_jac(0), 0)

    for _ in range(line - 1):
        @pl.when(has_low)
        def _():
            pl.semaphore_signal(from_high, inc=1, device_id=low, device_id_type=MESH)

        @pl.when(has_high)
        def _():
            pl.semaphore_signal(from_low, inc=1, device_id=high, device_id_type=MESH)

        @pl.when(has_low)
        def _():
            pl.semaphore_wait(from_low, 1)

        @pl.when(has_high)
        def _():
            pl.semaphore_wait(from_high, 1)

    @pl.when(xi == 0)
    def _():
        send_edge()

    lax.fori_loop(early, plane, send_jac(0), 0)
    for n in range(1, line):
        lax.fori_loop(1, plane, send_jac(n), 0)

    @pl.when(lender)
    def _():
        to_lat, to_x, _ = mate(moved)
        at = (to_lat, there * inner + to_x)
        remote(lent, met.at[there, :, spare], l_send, l_recv, at).start()
        remote(jac.at[to_lat, there, to_x], jrecv.at[there, spare], j_send, s_recv, at).start()

    def field_landed(g, c):
        landed(tbl.at[g, field_pieces[c]], f_recv.at[g, c])

    def forward(d):
        for c in range(len(field_pieces)):
            @pl.when(inside_line & (z >= d))
            def _():
                field_landed(z - d, c)
                send_field(z - d, c, True)

            @pl.when(inside_line & (z + d < line))
            def _():
                field_landed(z + d, c)
                send_field(z + d, c, False)

    inside = jnp.where(lat < lat_n - 1, 1.0, 0.0)
    width = tile * slots
    tiles = plane // tile
    pad = -(-(max(rows, cols) + 1) // 8) * 8

    def terms(g, t, width):
        lanes = pl.ds(pl.multiple_of(t * width, width), width)
        info = met[g, :, lanes].astype(jnp.float32)
        lat_w = weight_rows(info[0:1], info[2:3], pad)
        lon_w = weight_rows(info[1:2], info[3:4], pad)
        lon_c = lon_w[:cols]
        lon_e = lon_w[cols:cols + 1]
        lat_n_row = lat_w[rows:rows + 1] * inside
        first = lax.broadcasted_iota(jnp.int32, (rows, width), 0) == 0
        blocks = [lat_w[r:r + 1] * lon_c for r in range(rows)]
        blocks.append(lat_n_row * lon_c)
        blocks.append(lat_w[:rows] * lon_e)
        blocks.append(
            jnp.where(first, jnp.broadcast_to(lat_n_row * lon_e, (rows, width)), 0.0)
        )
        spread = jnp.concatenate(blocks, axis=0).astype(jnp.bfloat16).astype(jnp.float32)
        jac_t = jrecv[g, lanes]
        products = lax.dot_general(
            tbl[g], jac_t, (((1,), (1,)), ((), ())), preferred_element_type=jnp.float32
        )
        evolved = jnp.sum(spread * products, axis=0, keepdims=True)
        departure = jnp.where(info[0:1] >= 0.0, evolved - info[4:5], 0.0)
        dep[g, :, lanes] = departure
        return (spread * (info[5:6] * departure)).astype(jnp.bfloat16), jac_t

    def compute(n, g):
        into = part.at[n]

        def one_tile(t, carry):
            scaled, jac_t = terms(g, t, width)
            into[...] += jnp.dot(scaled, jac_t, preferred_element_type=jnp.float32)
            return carry

        if tiles > 1:
            into[...] = jnp.zeros(into.shape, into.dtype)
            lax.fori_loop(0, tiles, one_tile, 0)
        else:
            scaled, jac_t = terms(g, 0, width)
            into[...] = jnp.dot(scaled, jac_t, preferred_element_type=jnp.float32)

    def send_dep(g, first, last):
        def one(i, carry):
            @pl.when(jnp.logical_not(lent_out(i, g)))
            def _():
                to_lat, to_x = source(i)
                place = pl.ds(pl.multiple_of(i * slots, slots), slots)
                remote(
                    dep.at[g, :, place], dep_out.at[lat, g, xi], d_send, d_recv,
                    (to_lat, z * inner + to_x),
                ).start()

            return carry

        lax.fori_loop(max(first, 1), last, one, 0)
        if first == 0:
            pltpu.make_async_copy(
                dep.at[g, :, pl.ds(0, slots)], dep_out.at[lat, g, xi], d_recv
            ).start()

    def finish(n, incoming):
        g = visits[n]
        up = g > z
        next_z = jnp.where(up, z + 1, z - 1)
        slot = jnp.where((g == next_z) & jnp.logical_not(up), line, g)
        for c, at in enumerate(table_pieces):
            total = part[n, at, :]
            if incoming:
                landed(rbuf.at[g, at], g_recv.at[g, c])
                total = total + rbuf[g, at, :].astype(jnp.float32)
            gsend[n, at, :] = total.astype(gsend.dtype)
            remote(gsend.at[n, at], rbuf.at[slot, at], g_send, g_recv.at[slot, c],
                   (lat, next_z * inner + xi)).start()

    def pass_on(n):
        @pl.when(inside_line)
        def _():
            finish(n, True)

    for d in range(1, max(line // 2, 1)):
        forward(d)

    @pl.when(has_north)
    def _():
        landed(tbl.at[z, rim], e_own)

    @pl.when(jnp.logical_not(has_north))
    def _():
        landed(edge, e_own)

    for i in range(1, line):
        remote(tbl.at[z, rim], tbl.at[z, rim], b_send, e_recv.at[z],
               (lat, (z + i) % line * inner + xi)).start()
    landed(met.at[:, :, pl.ds(0, plane * slots)], m_recv)
    for n in range(line - 1):
        g = visits[n]

        @pl.when(jnp.logical_not(inside_line))
        def _():
            for c in range(len(field_pieces)):
                field_landed(g, c)

        landed(tbl.at[g, rim], e_recv.at[g])
        jac_landed(g, 1 - moved // half)

        @pl.when(lent_out(moved, g))
        def _():
            landed(jrecv.at[g, pl.ds(slots, (half - 1) * slots)], j_recv.at[g, moved // half])

        @pl.when(jnp.logical_not(lent_out(moved, g)))
        def _():
            jac_landed(g, moved // half)

        compute(n, g)
        send_dep(g, 0, plane)

        @pl.when(jnp.logical_not(inside_line))
        def _():
            finish(n, False)

        if n == 0:
            for d in range(max(line // 2, 1), line - 1):
                forward(d)
            for c in range(len(field_pieces)):
                @pl.when(has_low & (z < line // 2))
                def _():
                    send_field(z, c, False)

                @pl.when(has_high & (z >= line // 2))
                def _():
                    send_field(z, c, True)
        elif n == 1:
            pass_on(0)
            pass_on(1)
        else:
            pass_on(n)

    main = pl.ds(0, cells)

    def arrived(at):
        return rbuf[z, at, :].astype(jnp.float32) + rbuf[line, at, :].astype(jnp.float32)

    def sums_landed(first, last):
        for c in range(first, last):
            at = table_pieces[c]

            @pl.when(has_low)
            def _():
                landed(rbuf.at[z, at], g_recv.at[z, c])

            @pl.when(has_high)
            def _():
                landed(rbuf.at[line, at], g_recv.at[line, c])

    def send_rim(values):
        sums_landed(0, 1)
        hsend[...] = (values + arrived(rim)).astype(hsend.dtype)
        remote(hsend.at[pl.ds(cols, rows)], hrecv.at[1], h_send, h_recv, (lat, lon_up)).start()

        @pl.when(has_north)
        def _():
            remote(hsend.at[pl.ds(cols + rows, rows)], hrecv.at[2], h_send, h_recv,
                   (lat_up, lon_up)).start()
            remote(hsend.at[pl.ds(0, cols)], hrecv.at[0], h_send, h_recv, (lat_up, lon)).start()

    def take_spare():
        landed(met.at[z, :, spare], l_recv)
        landed(jrecv.at[z, spare], s_recv)
        return terms(z, plane, slots)

    def return_spare():
        to_lat, to_x = source(moved)
        remote(dep.at[z, :, spare], dep_out.at[lat, z, xi], s_send, d_recv,
               (to_lat, (line - 1) * inner + to_x)).start()

    def add(terms_of):
        scaled, jac_t = terms_of
        part[line - 1] += jnp.dot(scaled, jac_t, preferred_element_type=jnp.float32)

    def conclude(terms_of, send_rest):
        scaled, jac_t = terms_of
        send_rim(part[line - 1, rim, :] + jnp.dot(
            scaled[cells:], jac_t, preferred_element_type=jnp.float32
        ))
        send_rest()
        sums_landed(1, len(table_pieces))
        gmain[...] = arrived(main) + part[line - 1, main, :] + jnp.dot(
            scaled[:cells], jac_t, preferred_element_type=jnp.float32
        )

    jac_landed(z, 0)
    if tiles > 1:
        jac_landed(z, 1)
        compute(line - 1, z)
        send_dep(z, 0, plane)

        @pl.when(taker)
        def _():
            add(take_spare())
            return_spare()

        send_rim(part[line - 1, rim, :])
        sums_landed(1, len(table_pieces))
        gmain[...] = part[line - 1, main, :] + arrived(main)
    else:
        scaled, jac_t = terms(z, 0, half * slots)
        part[line - 1] = jnp.dot(scaled, jac_t, preferred_element_type=jnp.float32)
        send_dep(z, 0, half)
        jac_landed(z, 1)

        @pl.when(taker)
        def _():
            add(terms(z, 1, half * slots))
            send_dep(z, half, plane)
            conclude(take_spare(), return_spare)

        @pl.when(jnp.logical_not(taker))
        def _():
            conclude(terms(z, 1, half * slots), lambda: send_dep(z, half, plane))

    others = pl.ds(0, (plane - 1) * slots)
    for up in (False, True):
        for i in range(line):
            sent = (z >= i) & has_high if up else (z + i < line) & has_low

            @pl.when(sent & (inside_line | (i == 0)))
            def _():
                landed(own_field, f_send)
    @pl.when(has_south)
    def _():
        landed(tbl.at[z, rim], e_send)

    @pl.when(jnp.logical_not(has_south))
    def _():
        landed(edge, e_send)

    landed(tbl.at[pl.ds(0, line - 1), rim], b_send)
    landed(met.at[:, :, others], m_send)
    landed(jrecv.at[:, others], j_send)
    landed(dep.at[pl.ds(0, line - 1), :, others], d_send)
    landed(dep.at[0, :, pl.ds(0, (plane - 2) * slots)], d_send)

    @pl.when(jnp.logical_not(lender))
    def _():
        landed(dep.at[0, :, pl.ds(0, slots)], d_send)

    @pl.when(lender)
    def _():
        landed(lent, l_send)

    @pl.when(taker)
    def _():
        landed(dep.at[0, :, spare], s_send)

    landed(gsend, g_send)
    @pl.when(has_north)
    def _():
        landed(hsend, h_send)

    @pl.when(jnp.logical_not(has_north))
    def _():
        landed(edge, h_send)

    @pl.when(has_south)
    def _():
        landed(hrecv, h_recv)

    @pl.when(jnp.logical_not(has_south))
    def _():
        landed(edge, h_recv)

    landed(dep_out, d_recv)


def last_sums(rows, cols, gmain, hrecv, dep, grad_out, dep_out):
    dep_out[...] = dep[...]
    grad_out[...] = gmain[...]
    grad_out[pl.ds(0, cols), :] += hrecv[0].astype(jnp.float32)
    east = hrecv[1].astype(jnp.float32)
    corner = hrecv[2].astype(jnp.float32)
    for r in range(rows):
        extra = east[r:r + 1]
        if r == 0:
            extra = extra + corner[0:1]
        grad_out[pl.ds(r * cols, 1), :] += extra


def shards(mesh_shape, field, obs_jac, obs_frac, obs_innov, obs_rinv, obs_cells):
    lat_n, lon_n = mesh_shape
    line = math.gcd(lon_n // 2, 4)
    inner = lon_n // line
    plane = lat_n * inner
    total = lat_n * lon_n
    rows, cols, wide = field.shape
    slots = obs_jac.shape[2]
    tile = math.gcd(plane, 8)
    cells = rows * cols
    table = cells + cols + 2 * rows
    f32, bf16 = jnp.float32, jnp.bfloat16
    dma = pltpu.SemaphoreType.DMA
    one = pltpu.SemaphoreType.DMA(())
    vmem = pl.BlockSpec(memory_space=pltpu.VMEM)
    anywhere = pl.BlockSpec(memory_space=pltpu.HBM)
    parts = pl.pallas_call(
        functools.partial(kernel, lat_n, lon_n, line, rows, cols, tile),
        out_shape=(
            pltpu.VMEM((cells, wide), f32),
            pltpu.VMEM((3, rows, wide), bf16),
            pltpu.VMEM((lat_n, line, inner, 1, slots), f32),
        ),
        in_specs=[anywhere, vmem, vmem, vmem, vmem, anywhere],
        out_specs=(vmem,) * 3,
        scratch_shapes=[
            pltpu.VMEM((rows, wide), bf16),
            pltpu.VMEM((total, slots), f32),
            pltpu.VMEM((total, slots), f32),
            pltpu.VMEM((plane, line, 8, slots), bf16),
            pltpu.VMEM((8, slots), bf16),
            pltpu.VMEM((line, table, wide), bf16),
            pltpu.VMEM((line, 8, (plane + 1) * slots), bf16),
            pltpu.VMEM((line, (plane + 1) * slots, wide), bf16),
            pltpu.VMEM((line, 1, (plane + 1) * slots), f32),
            pltpu.VMEM((line, table, wide), f32),
            pltpu.VMEM((line - 1, table, wide), bf16),
            pltpu.VMEM((line + 1, table, wide), bf16),
            pltpu.VMEM((table - cells, wide), bf16),
            one, one, dma((line, 2)),
            one, one, one, dma((line,)),
            one, one,
            one, one, one, one,
            one, dma((line, 2)),
            one, one,
            one, dma((line + 1, 3)),
            one, one,
            pltpu.SemaphoreType.REGULAR, pltpu.SemaphoreType.REGULAR,
        ],
        compiler_params=pltpu.CompilerParams(
            collective_id=0, has_side_effects=True, vmem_limit_bytes=62 * 1024 * 1024
        ),
    )(
        field.reshape(cells, wide),
        obs_cells,
        obs_frac.reshape(total, 2, slots),
        obs_innov.reshape(total, slots),
        obs_rinv.reshape(total, slots),
        obs_jac.reshape(lat_n, line, inner, slots, wide),
    )
    grad, departures = pl.pallas_call(
        functools.partial(last_sums, rows, cols),
        out_shape=(
            jax.ShapeDtypeStruct((cells, wide), f32),
            jax.ShapeDtypeStruct((total, 1, slots), f32),
        ),
        in_specs=[vmem] * 3,
        out_specs=(vmem, vmem),
        compiler_params=pltpu.CompilerParams(vmem_limit_bytes=8 * 1024 * 1024),
    )(*parts[:2], parts[2].reshape(total, 1, slots))
    return departures, grad.reshape(rows, cols, wide)


def solution(mesh):
    placed = (
        P("lat", "lon", None),
        P(None, ("lat", "lon"), None, None),
        P(None, ("lat", "lon"), None, None),
        P(None, ("lat", "lon"), None),
        P(None, ("lat", "lon"), None),
        P(None, ("lat", "lon"), None),
    )
    return jax.shard_map(
        functools.partial(shards, (mesh.shape["lat"], mesh.shape["lon"])),
        mesh=mesh,
        in_specs=placed,
        out_specs=(P(None, ("lat", "lon"), None), P("lat", "lon", None)),
        check_vma=False,
    )
```

```python
import functools
import math

import jax
import jax.numpy as jnp
from jax import lax
from jax.experimental import pallas as pl
from jax.experimental.pallas import tpu as pltpu
from jax.sharding import PartitionSpec as P

MESH = pl.DeviceIdType.MESH
AWAY = -1000.0


def visit_order(z, line):
    half = line // 2
    if z < half:
        return [*range(half, line), *(p for p in range(half) if p != z), z]
    return [*range(half - 1, -1, -1), *(p for p in range(half, line) if p != z), z]


def pick(z, values):
    chosen = jnp.int32(values[0])
    for p in range(1, len(values)):
        chosen = jnp.where(z == p, jnp.int32(values[p]), chosen)
    return chosen


def weight_rows(position, frac, rows):
    ids = lax.broadcasted_iota(jnp.int32, (rows, position.shape[1]), 0).astype(jnp.float32)
    zero = jnp.zeros_like(ids)
    return jnp.where(
        ids == position, 1.0 - frac, jnp.where(ids == position + 1.0, frac, zero)
    )


def kernel(
    lat_n, lon_n, line, rows, cols, tile,
    field, cell_in, frac_in, innov_in, rinv_in, jac,
    gmain, hrecv, dep_out,
    cell_ref, frac_ref, innov_ref, rinv_ref,
    edge, innov, rinv, rowcol, meta, lent,
    tbl, met, jrecv, dep, part, gsend, rbuf, hsend,
    f_local, s_local, f_send, f_recv, e_send, e_own, b_send, e_recv, m_send, m_recv, l_send, l_recv, s_send, s_recv, j_send, j_recv, d_send, d_recv,
    g_send, g_recv, h_send, h_recv, from_low, from_high,
):
    inner = lon_n // line
    plane = lat_n * inner
    slots = jac.shape[3]
    cells = rows * cols
    halo = cells + cols
    lat, lon = lax.axis_index("lat"), lax.axis_index("lon")
    z, xi = lon // inner, lon % inner
    here = lat * inner + xi
    lat_up, lat_down = (lat + 1) % lat_n, (lat + lat_n - 1) % lat_n
    lon_up, lon_down = (lon + 1) % lon_n, (lon + lon_n - 1) % lon_n
    z_low, x_low = lon_down // inner, lon_down % inner
    orders = [visit_order(p, line) for p in range(line)]
    visits = [pick(z, [order[n] for order in orders]) for n in range(line)]

    def remote(src, dst, send, recv, to):
        return pltpu.make_async_remote_copy(
            src_ref=src, dst_ref=dst, send_sem=send, recv_sem=recv,
            device_id=to, device_id_type=MESH,
        )

    def landed(like, sem):
        pltpu.make_async_copy(like, like, sem).wait()

    def pieces(size, count):
        cuts = [-(-size * c // (16 * count)) * 16 for c in range(count)] + [size]
        return [pl.ds(a, b - a) for a, b in zip(cuts, cuts[1:])]

    field_pieces = pieces(cells, f_recv.shape[1])
    table_pieces = [pl.ds(cells, cols + 2 * rows), *pieces(cells, g_recv.shape[1] - 1)]

    def mate(i):
        to_lat, to_x = (lat + i // inner) % lat_n, (xi + i % inner) % inner
        return to_lat, to_x, (to_lat, z * inner + to_x)

    def lent_out(i, g):
        return (z == line - 1) & (i == moved) & (g == there)

    def source(i):
        return (lat + lat_n - i // inner) % lat_n, (xi + inner - i % inner) % inner

    moved = (lat_n // 2) * inner + inner // 2
    there = jnp.where(lat % 2 == 0, line - 2, max(line - 3, 0))
    lender, taker = z == line - 1, z == there
    spare = pl.ds(plane * slots, slots)

    has_low, has_high = z > 0, z < line - 1
    inside_line = has_low & has_high
    low, high = (lat, lon - inner), (lat, lon + inner)
    barrier = pltpu.get_barrier_semaphore()

    @pl.when(has_low)
    def _():
        pl.semaphore_signal(barrier, inc=1, device_id=low, device_id_type=MESH)

    @pl.when(has_high)
    def _():
        pl.semaphore_signal(barrier, inc=1, device_id=high, device_id_type=MESH)

    def greet(i, carry):
        pl.semaphore_signal(barrier, inc=1, device_id=mate(i)[2], device_id_type=MESH)
        return carry

    lax.fori_loop(1, plane, greet, 0)

    own_field = tbl.at[z, pl.ds(0, cells)]
    local = pltpu.make_async_copy(field, own_field, f_local)
    smalls = [
        pltpu.make_async_copy(src, dst, s_local.at[k])
        for k, (src, dst) in enumerate((
            (cell_in, cell_ref), (frac_in, frac_ref), (innov_in, innov_ref), (rinv_in, rinv_ref),
        ))
    ]
    for copy in (*smalls, local):
        copy.start()
    for g in visits:
        pltpu.make_async_copy(
            jac.at[lat, g, xi], jrecv.at[g, pl.ds(0, slots)], j_recv.at[g, 0]
        ).start()

    @pl.when(jnp.logical_not(has_low))
    def _():
        rbuf[z] = jnp.zeros(rbuf.shape[1:], rbuf.dtype)

    @pl.when(jnp.logical_not(has_high))
    def _():
        rbuf[line] = jnp.zeros(rbuf.shape[1:], rbuf.dtype)

    has_south, has_north = lat > 0, lat < lat_n - 1
    row_rim, edge_rim = pl.ds(cells, cols), pl.ds(halo, rows)
    corner_rim, rim = pl.ds(halo + rows, rows), pl.ds(cells, cols + 2 * rows)

    @pl.when(jnp.logical_not(has_north))
    def _():
        tbl[z, row_rim, :] = jnp.zeros((cols, tbl.shape[2]), tbl.dtype)
        tbl[z, corner_rim, :] = jnp.zeros((rows, tbl.shape[2]), tbl.dtype)

    @pl.when(jnp.logical_not(has_south))
    def _():
        hrecv[0] = jnp.zeros(hrecv.shape[1:], hrecv.dtype)
        hrecv[2] = jnp.zeros(hrecv.shape[1:], hrecv.dtype)

    for copy in smalls:
        copy.wait()
    innov[...] = innov_ref[...].astype(jnp.float32)
    rinv[...] = rinv_ref[...].astype(jnp.float32)
    cell = cell_ref[...].astype(jnp.float32)
    live = cell >= 0.0
    row = jnp.floor((cell + 0.5) * (1.0 / (cols + 1)))
    rowcol[0] = jnp.where(live, row, AWAY)
    rowcol[1] = jnp.where(live, cell - row * (cols + 1), AWAY)

    def build(i, carry):
        to_lat, to_x, _ = mate(i)
        for g in range(line):
            owner = to_lat * lon_n + g * inner + to_x
            meta[i, g] = jnp.concatenate(
                [
                    rowcol[0, pl.ds(owner, 1), :],
                    rowcol[1, pl.ds(owner, 1), :],
                    frac_ref[owner].astype(jnp.float32),
                    innov[pl.ds(owner, 1), :],
                    rinv[pl.ds(owner, 1), :],
                    jnp.zeros((2, slots), jnp.float32),
                ],
                axis=0,
            ).astype(meta.dtype)
        return carry

    lax.fori_loop(0, plane, build, 0)

    @pl.when(lender)
    def _():
        lent[...] = meta[moved, there]
        meta[moved, there] = jnp.full(lent.shape, AWAY, lent.dtype)
        jrecv[there, pl.ds(moved * slots, slots), :] = jnp.zeros(
            (slots, jrecv.shape[2]), jrecv.dtype
        )

    local.wait()
    edge[...] = jnp.concatenate(
        [tbl[z, pl.ds(r * cols, cols), :].astype(jnp.float32)[0:1] for r in range(rows)], axis=0
    ).astype(edge.dtype)
    pltpu.make_async_copy(meta.at[0], met.at[:, :, pl.ds(0, slots)], m_recv).start()
    pl.semaphore_wait(barrier, plane - 1 + has_low.astype(jnp.int32) + has_high.astype(jnp.int32))

    def send_field(g, c, up):
        piece = tbl.at[g, field_pieces[c]]
        remote(piece, piece, f_send, f_recv.at[g, c], high if up else low).start()

    def send_meta(i, carry):
        place = pl.ds(pl.multiple_of(i * slots, slots), slots)
        remote(meta.at[i], met.at[:, :, place], m_send, m_recv, mate(i)[2]).start()
        return carry

    half = plane // 2
    bounds = (0, half, plane - 1, plane)
    moved_piece = 0 if moved < half else 1 if moved < plane - 1 else 2

    def piece_of(i):
        return (i >= half).astype(jnp.int32) + (i >= plane - 1).astype(jnp.int32)

    def jac_landed(g, *which):
        for h in which:
            lanes = pl.ds(bounds[h] * slots, (bounds[h + 1] - bounds[h]) * slots)
            landed(jrecv.at[g, lanes], j_recv.at[g, h])

    def send_jac(n):
        g = visits[n]

        def one(i, carry):
            @pl.when(jnp.logical_not(lent_out(i, g)))
            def _():
                to_lat, to_x, at = mate(i)
                place = pl.ds(pl.multiple_of(i * slots, slots), slots)
                remote(
                    jac.at[to_lat, g, to_x], jrecv.at[g, place], j_send,
                    j_recv.at[g, piece_of(i)], at,
                ).start()

            return carry

        return one

    def send_edge():
        remote(edge, tbl.at[z_low, edge_rim], e_send, e_own, (lat, lon_down)).start()

        @pl.when(has_south)
        def _():
            remote(edge, tbl.at[z_low, corner_rim], e_send, e_own, (lat_down, lon_down)).start()

    early = plane - plane // 4
    lax.fori_loop(1, plane, send_meta, 0)
    lax.fori_loop(1, 3, send_jac(0), 0)
    for c in range(len(field_pieces)):
        @pl.when(has_low & (z >= line // 2))
        def _():
            send_field(z, c, False)

        @pl.when(has_high & (z < line // 2))
        def _():
            send_field(z, c, True)

    @pl.when(has_south)
    def _():
        remote(tbl.at[z, pl.ds(0, cols)], tbl.at[z, row_rim], e_send, e_own,
               (lat_down, lon)).start()

    @pl.when(xi > 0)
    def _():
        send_edge()

    lax.fori_loop(3, early, send_jac(0), 0)

    for _ in range(line - 1):
        @pl.when(has_low)
        def _():
            pl.semaphore_signal(from_high, inc=1, device_id=low, device_id_type=MESH)

        @pl.when(has_high)
        def _():
            pl.semaphore_signal(from_low, inc=1, device_id=high, device_id_type=MESH)

        @pl.when(has_low)
        def _():
            pl.semaphore_wait(from_low, 1)

        @pl.when(has_high)
        def _():
            pl.semaphore_wait(from_high, 1)

    @pl.when(xi == 0)
    def _():
        send_edge()

    lax.fori_loop(early, plane, send_jac(0), 0)
    for n in range(1, line):
        lax.fori_loop(1, plane, send_jac(n), 0)

    @pl.when(lender)
    def _():
        to_lat, to_x, _ = mate(moved)
        at = (to_lat, there * inner + to_x)
        remote(lent, met.at[there, :, spare], l_send, l_recv, at).start()
        remote(jac.at[to_lat, there, to_x], jrecv.at[there, spare], j_send, s_recv, at).start()

    def field_landed(g, c):
        landed(tbl.at[g, field_pieces[c]], f_recv.at[g, c])

    def forward(d):
        for c in range(len(field_pieces)):
            @pl.when(inside_line & (z >= d))
            def _():
                field_landed(z - d, c)
                send_field(z - d, c, True)

            @pl.when(inside_line & (z + d < line))
            def _():
                field_landed(z + d, c)
                send_field(z + d, c, False)

    inside = jnp.where(lat < lat_n - 1, 1.0, 0.0)
    width = tile * slots
    tiles = plane // tile
    pad = -(-(max(rows, cols) + 1) // 8) * 8

    def terms(g, start, width):
        lanes = pl.ds(pl.multiple_of(start, slots), width)
        info = met[g, :, lanes].astype(jnp.float32)
        lat_w = weight_rows(info[0:1], info[2:3], pad)
        lon_w = weight_rows(info[1:2], info[3:4], pad)
        lon_c = lon_w[:cols]
        lon_e = lon_w[cols:cols + 1]
        lat_n_row = lat_w[rows:rows + 1] * inside
        first = lax.broadcasted_iota(jnp.int32, (rows, width), 0) == 0
        blocks = [lat_w[r:r + 1] * lon_c for r in range(rows)]
        blocks.append(lat_n_row * lon_c)
        blocks.append(lat_w[:rows] * lon_e)
        blocks.append(
            jnp.where(first, jnp.broadcast_to(lat_n_row * lon_e, (rows, width)), 0.0)
        )
        spread = jnp.concatenate(blocks, axis=0).astype(jnp.bfloat16).astype(jnp.float32)
        jac_t = jrecv[g, lanes]
        products = lax.dot_general(
            tbl[g], jac_t, (((1,), (1,)), ((), ())), preferred_element_type=jnp.float32
        )
        evolved = jnp.sum(spread * products, axis=0, keepdims=True)
        departure = jnp.where(info[0:1] >= 0.0, evolved - info[4:5], 0.0)
        dep[g, :, lanes] = departure
        return (spread * (info[5:6] * departure)).astype(jnp.bfloat16), jac_t

    def compute(n, g):
        into = part.at[n]

        def one_tile(t, carry):
            scaled, jac_t = terms(g, t * width, width)
            into[...] += jnp.dot(scaled, jac_t, preferred_element_type=jnp.float32)
            return carry

        if tiles > 1:
            into[...] = jnp.zeros(into.shape, into.dtype)
            lax.fori_loop(0, tiles, one_tile, 0)
        else:
            scaled, jac_t = terms(g, 0, width)
            into[...] = jnp.dot(scaled, jac_t, preferred_element_type=jnp.float32)

    def send_dep(g, first, last):
        def one(i, carry):
            @pl.when(jnp.logical_not(lent_out(i, g)))
            def _():
                to_lat, to_x = source(i)
                place = pl.ds(pl.multiple_of(i * slots, slots), slots)
                remote(
                    dep.at[g, :, place], dep_out.at[lat, g, xi], d_send, d_recv,
                    (to_lat, z * inner + to_x),
                ).start()

            return carry

        lax.fori_loop(max(first, 1), last, one, 0)
        if first == 0:
            pltpu.make_async_copy(
                dep.at[g, :, pl.ds(0, slots)], dep_out.at[lat, g, xi], d_recv
            ).start()

    def finish(n, incoming):
        g = visits[n]
        up = g > z
        next_z = jnp.where(up, z + 1, z - 1)
        slot = jnp.where((g == next_z) & jnp.logical_not(up), line, g)
        for c, at in enumerate(table_pieces):
            total = part[n, at, :]
            if incoming:
                landed(rbuf.at[g, at], g_recv.at[g, c])
                total = total + rbuf[g, at, :].astype(jnp.float32)
            gsend[n, at, :] = total.astype(gsend.dtype)
            remote(gsend.at[n, at], rbuf.at[slot, at], g_send, g_recv.at[slot, c],
                   (lat, next_z * inner + xi)).start()

    def pass_on(n):
        @pl.when(inside_line)
        def _():
            finish(n, True)

    for d in range(1, max(line // 2, 1)):
        forward(d)

    @pl.when(has_north)
    def _():
        landed(tbl.at[z, rim], e_own)

    @pl.when(jnp.logical_not(has_north))
    def _():
        landed(edge, e_own)

    for i in range(1, line):
        remote(tbl.at[z, rim], tbl.at[z, rim], b_send, e_recv.at[z],
               (lat, (z + i) % line * inner + xi)).start()
    landed(met.at[:, :, pl.ds(0, plane * slots)], m_recv)
    for n in range(line - 1):
        g = visits[n]

        @pl.when(jnp.logical_not(inside_line))
        def _():
            for c in range(len(field_pieces)):
                field_landed(g, c)

        landed(tbl.at[g, rim], e_recv.at[g])
        jac_landed(g, *(h for h in range(3) if h != moved_piece))

        @pl.when(lent_out(moved, g))
        def _():
            rest = bounds[moved_piece + 1] - bounds[moved_piece] - 1
            if rest > 0:
                landed(jrecv.at[g, pl.ds(0, rest * slots)], j_recv.at[g, moved_piece])

        @pl.when(jnp.logical_not(lent_out(moved, g)))
        def _():
            jac_landed(g, moved_piece)

        compute(n, g)
        send_dep(g, 0, plane)

        @pl.when(jnp.logical_not(inside_line))
        def _():
            finish(n, False)

        if n == 0:
            for d in range(max(line // 2, 1), line - 1):
                forward(d)
            for c in range(len(field_pieces)):
                @pl.when(has_low & (z < line // 2))
                def _():
                    send_field(z, c, False)

                @pl.when(has_high & (z >= line // 2))
                def _():
                    send_field(z, c, True)
        elif n == 1:
            pass_on(0)
            pass_on(1)
        else:
            pass_on(n)

    main = pl.ds(0, cells)

    def arrived(at):
        return rbuf[z, at, :].astype(jnp.float32) + rbuf[line, at, :].astype(jnp.float32)

    def sums_landed(first, last):
        for c in range(first, last):
            at = table_pieces[c]

            @pl.when(has_low)
            def _():
                landed(rbuf.at[z, at], g_recv.at[z, c])

            @pl.when(has_high)
            def _():
                landed(rbuf.at[line, at], g_recv.at[line, c])

    def send_rim(values):
        sums_landed(0, 1)
        hsend[...] = (values + arrived(rim)).astype(hsend.dtype)
        remote(hsend.at[pl.ds(cols, rows)], hrecv.at[1], h_send, h_recv, (lat, lon_up)).start()

        @pl.when(has_north)
        def _():
            remote(hsend.at[pl.ds(cols + rows, rows)], hrecv.at[2], h_send, h_recv,
                   (lat_up, lon_up)).start()
            remote(hsend.at[pl.ds(0, cols)], hrecv.at[0], h_send, h_recv, (lat_up, lon)).start()

    def take_spare():
        landed(met.at[z, :, spare], l_recv)
        landed(jrecv.at[z, spare], s_recv)
        return terms(z, plane * slots, slots)

    def return_spare():
        to_lat, to_x = source(moved)
        remote(dep.at[z, :, spare], dep_out.at[lat, z, xi], s_send, d_recv,
               (to_lat, (line - 1) * inner + to_x)).start()

    def add(terms_of):
        scaled, jac_t = terms_of
        part[line - 1] += jnp.dot(scaled, jac_t, preferred_element_type=jnp.float32)

    def conclude(terms_of, send_rest):
        scaled, jac_t = terms_of
        send_rim(part[line - 1, rim, :] + jnp.dot(
            scaled[cells:], jac_t, preferred_element_type=jnp.float32
        ))
        send_rest()
        sums_landed(1, len(table_pieces))
        gmain[...] = arrived(main) + part[line - 1, main, :] + jnp.dot(
            scaled[:cells], jac_t, preferred_element_type=jnp.float32
        )

    if tiles > 1:
        jac_landed(z, 0, 1, 2)
        compute(line - 1, z)
        send_dep(z, 0, plane)

        @pl.when(taker)
        def _():
            add(take_spare())
            return_spare()

        send_rim(part[line - 1, rim, :])
        sums_landed(1, len(table_pieces))
        gmain[...] = part[line - 1, main, :] + arrived(main)
    else:
        jac_landed(z, 0)
        scaled, jac_t = terms(z, 0, half * slots)
        part[line - 1] = jnp.dot(scaled, jac_t, preferred_element_type=jnp.float32)
        send_dep(z, 0, half)
        jac_landed(z, 1)

        @pl.when(taker)
        def _():
            jac_landed(z, 2)
            add(terms(z, half * slots, half * slots))
            send_dep(z, half, plane)
            conclude(take_spare(), return_spare)

        @pl.when(jnp.logical_not(taker))
        def _():
            add(terms(z, half * slots, (half - 1) * slots))
            send_dep(z, half, plane - 1)
            jac_landed(z, 2)
            conclude(
                terms(z, (plane - 1) * slots, slots), lambda: send_dep(z, plane - 1, plane)
            )

    others = pl.ds(0, (plane - 1) * slots)
    for up in (False, True):
        for i in range(line):
            sent = (z >= i) & has_high if up else (z + i < line) & has_low

            @pl.when(sent & (inside_line | (i == 0)))
            def _():
                landed(own_field, f_send)
    @pl.when(has_south)
    def _():
        landed(tbl.at[z, rim], e_send)

    @pl.when(jnp.logical_not(has_south))
    def _():
        landed(edge, e_send)

    landed(tbl.at[pl.ds(0, line - 1), rim], b_send)
    landed(met.at[:, :, others], m_send)
    landed(jrecv.at[:, others], j_send)
    landed(dep.at[pl.ds(0, line - 1), :, others], d_send)
    landed(dep.at[0, :, pl.ds(0, (plane - 2) * slots)], d_send)

    @pl.when(jnp.logical_not(lender))
    def _():
        landed(dep.at[0, :, pl.ds(0, slots)], d_send)

    @pl.when(lender)
    def _():
        landed(lent, l_send)

    @pl.when(taker)
    def _():
        landed(dep.at[0, :, spare], s_send)

    landed(gsend, g_send)
    @pl.when(has_north)
    def _():
        landed(hsend, h_send)

    @pl.when(jnp.logical_not(has_north))
    def _():
        landed(edge, h_send)

    @pl.when(has_south)
    def _():
        landed(hrecv, h_recv)

    @pl.when(jnp.logical_not(has_south))
    def _():
        landed(edge, h_recv)

    landed(dep_out, d_recv)


def last_sums(rows, cols, gmain, hrecv, dep, grad_out, dep_out):
    dep_out[...] = dep[...]
    grad_out[...] = gmain[...]
    grad_out[pl.ds(0, cols), :] += hrecv[0].astype(jnp.float32)
    east = hrecv[1].astype(jnp.float32)
    corner = hrecv[2].astype(jnp.float32)
    for r in range(rows):
        extra = east[r:r + 1]
        if r == 0:
            extra = extra + corner[0:1]
        grad_out[pl.ds(r * cols, 1), :] += extra


def shards(mesh_shape, field, obs_jac, obs_frac, obs_innov, obs_rinv, obs_cells):
    lat_n, lon_n = mesh_shape
    line = math.gcd(lon_n // 2, 4)
    inner = lon_n // line
    plane = lat_n * inner
    total = lat_n * lon_n
    rows, cols, wide = field.shape
    slots = obs_jac.shape[2]
    tile = math.gcd(plane, 8)
    cells = rows * cols
    table = cells + cols + 2 * rows
    f32, bf16 = jnp.float32, jnp.bfloat16
    dma = pltpu.SemaphoreType.DMA
    one = pltpu.SemaphoreType.DMA(())
    vmem = pl.BlockSpec(memory_space=pltpu.VMEM)
    anywhere = pl.BlockSpec(memory_space=pltpu.HBM)
    parts = pl.pallas_call(
        functools.partial(kernel, lat_n, lon_n, line, rows, cols, tile),
        out_shape=(
            pltpu.VMEM((cells, wide), f32),
            pltpu.VMEM((3, rows, wide), bf16),
            pltpu.VMEM((lat_n, line, inner, 1, slots), f32),
        ),
        in_specs=[anywhere] * 6,
        out_specs=(vmem,) * 3,
        scratch_shapes=[
            pltpu.VMEM((total, slots), jnp.int32),
            pltpu.VMEM((total, 2, slots), bf16),
            pltpu.VMEM((total, slots), bf16),
            pltpu.VMEM((total, slots), bf16),
            pltpu.VMEM((rows, wide), bf16),
            pltpu.VMEM((total, slots), f32),
            pltpu.VMEM((total, slots), f32),
            pltpu.VMEM((2, total, slots), f32),
            pltpu.VMEM((plane, line, 8, slots), bf16),
            pltpu.VMEM((8, slots), bf16),
            pltpu.VMEM((line, table, wide), bf16),
            pltpu.VMEM((line, 8, (plane + 1) * slots), bf16),
            pltpu.VMEM((line, (plane + 1) * slots, wide), bf16),
            pltpu.VMEM((line, 1, (plane + 1) * slots), f32),
            pltpu.VMEM((line, table, wide), f32),
            pltpu.VMEM((line - 1, table, wide), bf16),
            pltpu.VMEM((line + 1, table, wide), bf16),
            pltpu.VMEM((table - cells, wide), bf16),
            one, dma((4,)), one, dma((line, 2)),
            one, one, one, dma((line,)),
            one, one,
            one, one, one, one,
            one, dma((line, 3)),
            one, one,
            one, dma((line + 1, 3)),
            one, one,
            pltpu.SemaphoreType.REGULAR, pltpu.SemaphoreType.REGULAR,
        ],
        compiler_params=pltpu.CompilerParams(
            collective_id=0, has_side_effects=True, vmem_limit_bytes=62 * 1024 * 1024
        ),
    )(
        field.reshape(cells, wide),
        obs_cells.reshape(total, slots),
        obs_frac.reshape(total, 2, slots),
        obs_innov.reshape(total, slots),
        obs_rinv.reshape(total, slots),
        obs_jac.reshape(lat_n, line, inner, slots, wide),
    )
    grad, departures = pl.pallas_call(
        functools.partial(last_sums, rows, cols),
        out_shape=(
            jax.ShapeDtypeStruct((cells, wide), f32),
            jax.ShapeDtypeStruct((total, 1, slots), f32),
        ),
        in_specs=[vmem] * 3,
        out_specs=(vmem, vmem),
        compiler_params=pltpu.CompilerParams(vmem_limit_bytes=8 * 1024 * 1024),
    )(*parts[:2], parts[2].reshape(total, 1, slots))
    return departures, grad.reshape(rows, cols, wide)


def solution(mesh):
    placed = (
        P("lat", "lon", None),
        P(None, ("lat", "lon"), None, None),
        P(None, ("lat", "lon"), None, None),
        P(None, ("lat", "lon"), None),
        P(None, ("lat", "lon"), None),
        P(None, ("lat", "lon"), None),
    )
    return jax.shard_map(
        functools.partial(shards, (mesh.shape["lat"], mesh.shape["lon"])),
        mesh=mesh,
        in_specs=placed,
        out_specs=(P(None, ("lat", "lon"), None), P("lat", "lon", None)),
        check_vma=False,
    )
```

```python
import functools
import math

import jax
import jax.numpy as jnp
from jax import lax
from jax.experimental import pallas as pl
from jax.experimental.pallas import tpu as pltpu
from jax.sharding import PartitionSpec as P

MESH = pl.DeviceIdType.MESH
AWAY = -1000.0


def visit_order(z, line):
    half = line // 2
    if z < half:
        return [*range(half, line), *(p for p in range(half) if p != z), z]
    return [*range(half - 1, -1, -1), *(p for p in range(half, line) if p != z), z]


def pick(z, values):
    chosen = jnp.int32(values[0])
    for p in range(1, len(values)):
        chosen = jnp.where(z == p, jnp.int32(values[p]), chosen)
    return chosen


def weight_rows(position, frac, rows):
    ids = lax.broadcasted_iota(jnp.int32, (rows, position.shape[1]), 0).astype(jnp.float32)
    zero = jnp.zeros_like(ids)
    return jnp.where(
        ids == position, 1.0 - frac, jnp.where(ids == position + 1.0, frac, zero)
    )


def kernel(
    lat_n, lon_n, line, rows, cols, tile,
    field, cell_in, frac_in, innov_in, rinv_in, jac,
    gmain, hrecv, dep_out,
    cell_ref, frac_ref, innov_ref, rinv_ref,
    edge, innov, rinv, rowcol, meta, lent,
    tbl, met, jrecv, dep, part, gsend, rbuf, hsend,
    f_local, s_local, f_send, f_recv, e_send, e_own, b_send, e_recv, m_send, m_recv, l_send, l_recv, s_send, s_recv, j_send, j_recv, d_send, d_recv,
    g_send, g_recv, h_send, h_recv, from_low, from_high,
):
    inner = lon_n // line
    plane = lat_n * inner
    slots = jac.shape[3]
    cells = rows * cols
    halo = cells + cols
    lat, lon = lax.axis_index("lat"), lax.axis_index("lon")
    z, xi = lon // inner, lon % inner
    here = lat * inner + xi
    lat_up, lat_down = (lat + 1) % lat_n, (lat + lat_n - 1) % lat_n
    lon_up, lon_down = (lon + 1) % lon_n, (lon + lon_n - 1) % lon_n
    z_low, x_low = lon_down // inner, lon_down % inner
    orders = [visit_order(p, line) for p in range(line)]
    visits = [pick(z, [order[n] for order in orders]) for n in range(line)]

    def remote(src, dst, send, recv, to):
        return pltpu.make_async_remote_copy(
            src_ref=src, dst_ref=dst, send_sem=send, recv_sem=recv,
            device_id=to, device_id_type=MESH,
        )

    def landed(like, sem):
        pltpu.make_async_copy(like, like, sem).wait()

    def pieces(size, count):
        cuts = [-(-size * c // (16 * count)) * 16 for c in range(count)] + [size]
        return [pl.ds(a, b - a) for a, b in zip(cuts, cuts[1:])]

    field_pieces = pieces(cells, f_recv.shape[1])
    table_pieces = [pl.ds(cells, cols + 2 * rows), *pieces(cells, g_recv.shape[1] - 1)]

    def mate(i):
        to_lat, to_x = (lat + i // inner) % lat_n, (xi + i % inner) % inner
        return to_lat, to_x, (to_lat, z * inner + to_x)

    def lent_out(i, g):
        return (z == line - 1) & (i == moved) & (g == there)

    def source(i):
        return (lat + lat_n - i // inner) % lat_n, (xi + inner - i % inner) % inner

    moved = (lat_n // 2) * inner + inner // 2
    there = jnp.where(lat % 2 == 0, line - 2, max(line - 3, 0))
    lender, taker = z == line - 1, z == there
    spare = pl.ds(plane * slots, slots)

    has_low, has_high = z > 0, z < line - 1
    inside_line = has_low & has_high
    low, high = (lat, lon - inner), (lat, lon + inner)
    barrier = pltpu.get_barrier_semaphore()

    @pl.when(has_low)
    def _():
        pl.semaphore_signal(barrier, inc=1, device_id=low, device_id_type=MESH)

    @pl.when(has_high)
    def _():
        pl.semaphore_signal(barrier, inc=1, device_id=high, device_id_type=MESH)

    def greet(i, carry):
        pl.semaphore_signal(barrier, inc=1, device_id=mate(i)[2], device_id_type=MESH)
        return carry

    lax.fori_loop(1, plane, greet, 0)

    own_field = tbl.at[z, pl.ds(0, cells)]
    local = pltpu.make_async_copy(field, own_field, f_local)
    smalls = [
        pltpu.make_async_copy(src, dst, s_local.at[k])
        for k, (src, dst) in enumerate((
            (cell_in, cell_ref), (frac_in, frac_ref), (innov_in, innov_ref), (rinv_in, rinv_ref),
        ))
    ]
    for copy in (*smalls, local):
        copy.start()
    for g in visits:
        pltpu.make_async_copy(
            jac.at[lat, g, xi], jrecv.at[g, pl.ds(0, slots)], j_recv.at[g, 0]
        ).start()

    @pl.when(jnp.logical_not(has_low))
    def _():
        rbuf[z] = jnp.zeros(rbuf.shape[1:], rbuf.dtype)

    @pl.when(jnp.logical_not(has_high))
    def _():
        rbuf[line] = jnp.zeros(rbuf.shape[1:], rbuf.dtype)

    has_south, has_north = lat > 0, lat < lat_n - 1
    row_rim, edge_rim = pl.ds(cells, cols), pl.ds(halo, rows)
    tip = min(8, rows)
    corner_rim, rim = pl.ds(halo + rows, tip), pl.ds(cells, cols + 2 * rows)
    sent_rim = pl.ds(cells, cols + rows + tip)
    if rows > tip:
        tbl[z, pl.ds(halo + rows + tip, rows - tip), :] = jnp.zeros(
            (rows - tip, tbl.shape[2]), tbl.dtype
        )

    @pl.when(jnp.logical_not(has_north))
    def _():
        tbl[z, row_rim, :] = jnp.zeros((cols, tbl.shape[2]), tbl.dtype)
        tbl[z, corner_rim, :] = jnp.zeros((tip, tbl.shape[2]), tbl.dtype)

    @pl.when(jnp.logical_not(has_south))
    def _():
        hrecv[0] = jnp.zeros(hrecv.shape[1:], hrecv.dtype)
        hrecv[2] = jnp.zeros(hrecv.shape[1:], hrecv.dtype)

    for copy in smalls:
        copy.wait()
    innov[...] = innov_ref[...].astype(jnp.float32)
    rinv[...] = rinv_ref[...].astype(jnp.float32)
    cell = cell_ref[...].astype(jnp.float32)
    live = cell >= 0.0
    row = jnp.floor((cell + 0.5) * (1.0 / (cols + 1)))
    rowcol[0] = jnp.where(live, row, AWAY)
    rowcol[1] = jnp.where(live, cell - row * (cols + 1), AWAY)

    def build(i, carry):
        to_lat, to_x, _ = mate(i)
        for g in range(line):
            owner = to_lat * lon_n + g * inner + to_x
            meta[i, g] = jnp.concatenate(
                [
                    rowcol[0, pl.ds(owner, 1), :],
                    rowcol[1, pl.ds(owner, 1), :],
                    frac_ref[owner].astype(jnp.float32),
                    innov[pl.ds(owner, 1), :],
                    rinv[pl.ds(owner, 1), :],
                    jnp.zeros((2, slots), jnp.float32),
                ],
                axis=0,
            ).astype(meta.dtype)
        return carry

    lax.fori_loop(0, plane, build, 0)

    @pl.when(lender)
    def _():
        lent[...] = meta[moved, there]
        meta[moved, there] = jnp.full(lent.shape, AWAY, lent.dtype)
        jrecv[there, pl.ds(moved * slots, slots), :] = jnp.zeros(
            (slots, jrecv.shape[2]), jrecv.dtype
        )

    local.wait()
    edge[...] = jnp.concatenate(
        [tbl[z, pl.ds(r * cols, cols), :].astype(jnp.float32)[0:1] for r in range(rows)], axis=0
    ).astype(edge.dtype)
    pltpu.make_async_copy(meta.at[0], met.at[:, :, pl.ds(0, slots)], m_recv).start()
    pl.semaphore_wait(barrier, plane - 1 + has_low.astype(jnp.int32) + has_high.astype(jnp.int32))

    def send_field(g, c, up):
        piece = tbl.at[g, field_pieces[c]]
        remote(piece, piece, f_send, f_recv.at[g, c], high if up else low).start()

    def send_meta(i, carry):
        place = pl.ds(pl.multiple_of(i * slots, slots), slots)
        remote(meta.at[i], met.at[:, :, place], m_send, m_recv, mate(i)[2]).start()
        return carry

    half = plane // 2
    bounds = (0, half, plane - 1, plane)
    moved_piece = 0 if moved < half else 1 if moved < plane - 1 else 2

    def piece_of(i):
        return (i >= half).astype(jnp.int32) + (i >= plane - 1).astype(jnp.int32)

    def jac_landed(g, *which):
        for h in which:
            lanes = pl.ds(bounds[h] * slots, (bounds[h + 1] - bounds[h]) * slots)
            landed(jrecv.at[g, lanes], j_recv.at[g, h])

    def send_jac(n):
        g = visits[n]

        def one(i, carry):
            @pl.when(jnp.logical_not(lent_out(i, g)))
            def _():
                to_lat, to_x, at = mate(i)
                place = pl.ds(pl.multiple_of(i * slots, slots), slots)
                remote(
                    jac.at[to_lat, g, to_x], jrecv.at[g, place], j_send,
                    j_recv.at[g, piece_of(i)], at,
                ).start()

            return carry

        return one

    def send_edge():
        remote(edge, tbl.at[z_low, edge_rim], e_send, e_own, (lat, lon_down)).start()

        @pl.when(has_south)
        def _():
            remote(edge.at[pl.ds(0, tip)], tbl.at[z_low, corner_rim], e_send, e_own,
                   (lat_down, lon_down)).start()

    early = plane - plane // 4
    lax.fori_loop(1, plane, send_meta, 0)
    lax.fori_loop(1, 3, send_jac(0), 0)
    for c in range(len(field_pieces)):
        @pl.when(has_low & (z >= line // 2))
        def _():
            send_field(z, c, False)

        @pl.when(has_high & (z < line // 2))
        def _():
            send_field(z, c, True)

    @pl.when(has_south)
    def _():
        remote(tbl.at[z, pl.ds(0, cols)], tbl.at[z, row_rim], e_send, e_own,
               (lat_down, lon)).start()

    @pl.when(xi > 0)
    def _():
        send_edge()

    lax.fori_loop(3, early, send_jac(0), 0)

    for _ in range(line - 1):
        @pl.when(has_low)
        def _():
            pl.semaphore_signal(from_high, inc=1, device_id=low, device_id_type=MESH)

        @pl.when(has_high)
        def _():
            pl.semaphore_signal(from_low, inc=1, device_id=high, device_id_type=MESH)

        @pl.when(has_low)
        def _():
            pl.semaphore_wait(from_low, 1)

        @pl.when(has_high)
        def _():
            pl.semaphore_wait(from_high, 1)

    @pl.when(xi == 0)
    def _():
        send_edge()

    lax.fori_loop(early, plane, send_jac(0), 0)
    for n in range(1, line):
        lax.fori_loop(1, plane, send_jac(n), 0)

    @pl.when(lender)
    def _():
        to_lat, to_x, _ = mate(moved)
        at = (to_lat, there * inner + to_x)
        remote(lent, met.at[there, :, spare], l_send, l_recv, at).start()
        remote(jac.at[to_lat, there, to_x], jrecv.at[there, spare], j_send, s_recv, at).start()

    def field_landed(g, c):
        landed(tbl.at[g, field_pieces[c]], f_recv.at[g, c])

    def forward(d):
        for c in range(len(field_pieces)):
            @pl.when(inside_line & (z >= d))
            def _():
                field_landed(z - d, c)
                send_field(z - d, c, True)

            @pl.when(inside_line & (z + d < line))
            def _():
                field_landed(z + d, c)
                send_field(z + d, c, False)

    inside = jnp.where(lat < lat_n - 1, 1.0, 0.0)
    width = tile * slots
    tiles = plane // tile
    pad = -(-(max(rows, cols) + 1) // 8) * 8

    def terms(g, start, width):
        lanes = pl.ds(pl.multiple_of(start, slots), width)
        info = met[g, :, lanes].astype(jnp.float32)
        lat_w = weight_rows(info[0:1], info[2:3], pad)
        lon_w = weight_rows(info[1:2], info[3:4], pad)
        lon_c = lon_w[:cols]
        lon_e = lon_w[cols:cols + 1]
        lat_n_row = lat_w[rows:rows + 1] * inside
        first = lax.broadcasted_iota(jnp.int32, (rows, width), 0) == 0
        blocks = [lat_w[r:r + 1] * lon_c for r in range(rows)]
        blocks.append(lat_n_row * lon_c)
        blocks.append(lat_w[:rows] * lon_e)
        blocks.append(
            jnp.where(first, jnp.broadcast_to(lat_n_row * lon_e, (rows, width)), 0.0)
        )
        spread = jnp.concatenate(blocks, axis=0).astype(jnp.bfloat16).astype(jnp.float32)
        jac_t = jrecv[g, lanes]
        products = lax.dot_general(
            tbl[g], jac_t, (((1,), (1,)), ((), ())), preferred_element_type=jnp.float32
        )
        evolved = jnp.sum(spread * products, axis=0, keepdims=True)
        departure = jnp.where(info[0:1] >= 0.0, evolved - info[4:5], 0.0)
        dep[g, :, lanes] = departure
        return (spread * (info[5:6] * departure)).astype(jnp.bfloat16), jac_t

    def compute(n, g):
        into = part.at[n]

        def one_tile(t, carry):
            scaled, jac_t = terms(g, t * width, width)
            into[...] += jnp.dot(scaled, jac_t, preferred_element_type=jnp.float32)
            return carry

        if tiles > 1:
            into[...] = jnp.zeros(into.shape, into.dtype)
            lax.fori_loop(0, tiles, one_tile, 0)
        else:
            scaled, jac_t = terms(g, 0, width)
            into[...] = jnp.dot(scaled, jac_t, preferred_element_type=jnp.float32)

    def send_dep(g, first, last):
        def one(i, carry):
            @pl.when(jnp.logical_not(lent_out(i, g)))
            def _():
                to_lat, to_x = source(i)
                place = pl.ds(pl.multiple_of(i * slots, slots), slots)
                remote(
                    dep.at[g, :, place], dep_out.at[lat, g, xi], d_send, d_recv,
                    (to_lat, z * inner + to_x),
                ).start()

            return carry

        lax.fori_loop(max(first, 1), last, one, 0)
        if first == 0:
            pltpu.make_async_copy(
                dep.at[g, :, pl.ds(0, slots)], dep_out.at[lat, g, xi], d_recv
            ).start()

    def finish(n, incoming):
        g = visits[n]
        up = g > z
        next_z = jnp.where(up, z + 1, z - 1)
        slot = jnp.where((g == next_z) & jnp.logical_not(up), line, g)
        for c, at in enumerate(table_pieces):
            total = part[n, at, :]
            if incoming:
                landed(rbuf.at[g, at], g_recv.at[g, c])
                total = total + rbuf[g, at, :].astype(jnp.float32)
            gsend[n, at, :] = total.astype(gsend.dtype)
            remote(gsend.at[n, at], rbuf.at[slot, at], g_send, g_recv.at[slot, c],
                   (lat, next_z * inner + xi)).start()

    def pass_on(n):
        @pl.when(inside_line)
        def _():
            finish(n, True)

    for d in range(1, max(line // 2, 1)):
        forward(d)

    @pl.when(has_north)
    def _():
        landed(tbl.at[z, sent_rim], e_own)

    @pl.when(jnp.logical_not(has_north))
    def _():
        landed(edge, e_own)

    for i in range(1, line):
        remote(tbl.at[z, rim], tbl.at[z, rim], b_send, e_recv.at[z],
               (lat, (z + i) % line * inner + xi)).start()
    landed(met.at[:, :, pl.ds(0, plane * slots)], m_recv)
    for n in range(line - 1):
        g = visits[n]

        @pl.when(jnp.logical_not(inside_line))
        def _():
            for c in range(len(field_pieces)):
                field_landed(g, c)

        landed(tbl.at[g, rim], e_recv.at[g])
        jac_landed(g, *(h for h in range(3) if h != moved_piece))

        @pl.when(lent_out(moved, g))
        def _():
            rest = bounds[moved_piece + 1] - bounds[moved_piece] - 1
            if rest > 0:
                landed(jrecv.at[g, pl.ds(0, rest * slots)], j_recv.at[g, moved_piece])

        @pl.when(jnp.logical_not(lent_out(moved, g)))
        def _():
            jac_landed(g, moved_piece)

        compute(n, g)
        send_dep(g, 0, plane)

        @pl.when(jnp.logical_not(inside_line))
        def _():
            finish(n, False)

        if n == 0:
            for d in range(max(line // 2, 1), line - 1):
                forward(d)
            for c in range(len(field_pieces)):
                @pl.when(has_low & (z < line // 2))
                def _():
                    send_field(z, c, False)

                @pl.when(has_high & (z >= line // 2))
                def _():
                    send_field(z, c, True)
        elif n == 1:
            pass_on(0)
            pass_on(1)
        else:
            pass_on(n)

    main = pl.ds(0, cells)

    def arrived(at):
        return rbuf[z, at, :].astype(jnp.float32) + rbuf[line, at, :].astype(jnp.float32)

    def sums_landed(first, last):
        for c in range(first, last):
            at = table_pieces[c]

            @pl.when(has_low)
            def _():
                landed(rbuf.at[z, at], g_recv.at[z, c])

            @pl.when(has_high)
            def _():
                landed(rbuf.at[line, at], g_recv.at[line, c])

    def send_rim(values):
        sums_landed(0, 1)
        hsend[...] = (values + arrived(rim)).astype(hsend.dtype)
        remote(hsend.at[pl.ds(cols, rows)], hrecv.at[1], h_send, h_recv, (lat, lon_up)).start()

        @pl.when(has_north)
        def _():
            remote(hsend.at[pl.ds(cols + rows, tip)], hrecv.at[2, pl.ds(0, tip)], h_send, h_recv,
                   (lat_up, lon_up)).start()
            remote(hsend.at[pl.ds(0, cols)], hrecv.at[0], h_send, h_recv, (lat_up, lon)).start()

    def take_spare():
        landed(met.at[z, :, spare], l_recv)
        landed(jrecv.at[z, spare], s_recv)
        return terms(z, plane * slots, slots)

    def return_spare():
        to_lat, to_x = source(moved)
        remote(dep.at[z, :, spare], dep_out.at[lat, z, xi], s_send, d_recv,
               (to_lat, (line - 1) * inner + to_x)).start()

    def add(terms_of):
        scaled, jac_t = terms_of
        part[line - 1] += jnp.dot(scaled, jac_t, preferred_element_type=jnp.float32)

    def conclude(terms_of, send_rest):
        scaled, jac_t = terms_of
        send_rim(part[line - 1, rim, :] + jnp.dot(
            scaled[cells:], jac_t, preferred_element_type=jnp.float32
        ))
        send_rest()
        sums_landed(1, len(table_pieces))
        gmain[...] = arrived(main) + part[line - 1, main, :] + jnp.dot(
            scaled[:cells], jac_t, preferred_element_type=jnp.float32
        )

    if tiles > 1:
        jac_landed(z, 0, 1, 2)
        compute(line - 1, z)
        send_dep(z, 0, plane)

        @pl.when(taker)
        def _():
            add(take_spare())
            return_spare()

        send_rim(part[line - 1, rim, :])
        sums_landed(1, len(table_pieces))
        gmain[...] = part[line - 1, main, :] + arrived(main)
    else:
        jac_landed(z, 0)
        scaled, jac_t = terms(z, 0, half * slots)
        part[line - 1] = jnp.dot(scaled, jac_t, preferred_element_type=jnp.float32)
        send_dep(z, 0, half)
        jac_landed(z, 1)

        @pl.when(taker)
        def _():
            jac_landed(z, 2)
            add(terms(z, half * slots, half * slots))
            send_dep(z, half, plane)
            conclude(take_spare(), return_spare)

        @pl.when(jnp.logical_not(taker))
        def _():
            add(terms(z, half * slots, (half - 1) * slots))
            send_dep(z, half, plane - 1)
            jac_landed(z, 2)
            conclude(
                terms(z, (plane - 1) * slots, slots), lambda: send_dep(z, plane - 1, plane)
            )

    others = pl.ds(0, (plane - 1) * slots)
    for up in (False, True):
        for i in range(line):
            sent = (z >= i) & has_high if up else (z + i < line) & has_low

            @pl.when(sent & (inside_line | (i == 0)))
            def _():
                landed(own_field, f_send)
    @pl.when(has_south)
    def _():
        landed(tbl.at[z, sent_rim], e_send)

    @pl.when(jnp.logical_not(has_south))
    def _():
        landed(edge, e_send)

    landed(tbl.at[pl.ds(0, line - 1), rim], b_send)
    landed(met.at[:, :, others], m_send)
    landed(jrecv.at[:, others], j_send)
    landed(dep.at[pl.ds(0, line - 1), :, others], d_send)
    landed(dep.at[0, :, pl.ds(0, (plane - 2) * slots)], d_send)

    @pl.when(jnp.logical_not(lender))
    def _():
        landed(dep.at[0, :, pl.ds(0, slots)], d_send)

    @pl.when(lender)
    def _():
        landed(lent, l_send)

    @pl.when(taker)
    def _():
        landed(dep.at[0, :, spare], s_send)

    landed(gsend, g_send)
    @pl.when(has_north)
    def _():
        landed(tbl.at[z, sent_rim], h_send)

    @pl.when(jnp.logical_not(has_north))
    def _():
        landed(edge, h_send)

    @pl.when(has_south)
    def _():
        landed(tbl.at[z, sent_rim], h_recv)

    @pl.when(jnp.logical_not(has_south))
    def _():
        landed(edge, h_recv)

    landed(dep_out, d_recv)


def last_sums(rows, cols, gmain, hrecv, dep, grad_out, dep_out):
    dep_out[...] = dep[...]
    grad_out[...] = gmain[...]
    grad_out[pl.ds(0, cols), :] += hrecv[0].astype(jnp.float32)
    east = hrecv[1].astype(jnp.float32)
    corner = hrecv[2].astype(jnp.float32)
    for r in range(rows):
        extra = east[r:r + 1]
        if r == 0:
            extra = extra + corner[0:1]
        grad_out[pl.ds(r * cols, 1), :] += extra


def shards(mesh_shape, field, obs_jac, obs_frac, obs_innov, obs_rinv, obs_cells):
    lat_n, lon_n = mesh_shape
    line = math.gcd(lon_n // 2, 4)
    inner = lon_n // line
    plane = lat_n * inner
    total = lat_n * lon_n
    rows, cols, wide = field.shape
    slots = obs_jac.shape[2]
    tile = math.gcd(plane, 8)
    cells = rows * cols
    table = cells + cols + 2 * rows
    f32, bf16 = jnp.float32, jnp.bfloat16
    dma = pltpu.SemaphoreType.DMA
    one = pltpu.SemaphoreType.DMA(())
    vmem = pl.BlockSpec(memory_space=pltpu.VMEM)
    anywhere = pl.BlockSpec(memory_space=pltpu.HBM)
    parts = pl.pallas_call(
        functools.partial(kernel, lat_n, lon_n, line, rows, cols, tile),
        out_shape=(
            pltpu.VMEM((cells, wide), f32),
            pltpu.VMEM((3, rows, wide), bf16),
            pltpu.VMEM((lat_n, line, inner, 1, slots), f32),
        ),
        in_specs=[anywhere] * 6,
        out_specs=(vmem,) * 3,
        scratch_shapes=[
            pltpu.VMEM((total, slots), jnp.int32),
            pltpu.VMEM((total, 2, slots), bf16),
            pltpu.VMEM((total, slots), bf16),
            pltpu.VMEM((total, slots), bf16),
            pltpu.VMEM((rows, wide), bf16),
            pltpu.VMEM((total, slots), f32),
            pltpu.VMEM((total, slots), f32),
            pltpu.VMEM((2, total, slots), f32),
            pltpu.VMEM((plane, line, 8, slots), bf16),
            pltpu.VMEM((8, slots), bf16),
            pltpu.VMEM((line, table, wide), bf16),
            pltpu.VMEM((line, 8, (plane + 1) * slots), bf16),
            pltpu.VMEM((line, (plane + 1) * slots, wide), bf16),
            pltpu.VMEM((line, 1, (plane + 1) * slots), f32),
            pltpu.VMEM((line, table, wide), f32),
            pltpu.VMEM((line - 1, table, wide), bf16),
            pltpu.VMEM((line + 1, table, wide), bf16),
            pltpu.VMEM((table - cells, wide), bf16),
            one, dma((4,)), one, dma((line, 2)),
            one, one, one, dma((line,)),
            one, one,
            one, one, one, one,
            one, dma((line, 3)),
            one, one,
            one, dma((line + 1, 3)),
            one, one,
            pltpu.SemaphoreType.REGULAR, pltpu.SemaphoreType.REGULAR,
        ],
        compiler_params=pltpu.CompilerParams(
            collective_id=0, has_side_effects=True, vmem_limit_bytes=62 * 1024 * 1024
        ),
    )(
        field.reshape(cells, wide),
        obs_cells.reshape(total, slots),
        obs_frac.reshape(total, 2, slots),
        obs_innov.reshape(total, slots),
        obs_rinv.reshape(total, slots),
        obs_jac.reshape(lat_n, line, inner, slots, wide),
    )
    grad, departures = pl.pallas_call(
        functools.partial(last_sums, rows, cols),
        out_shape=(
            jax.ShapeDtypeStruct((cells, wide), f32),
            jax.ShapeDtypeStruct((total, 1, slots), f32),
        ),
        in_specs=[vmem] * 3,
        out_specs=(vmem, vmem),
        compiler_params=pltpu.CompilerParams(vmem_limit_bytes=8 * 1024 * 1024),
    )(*parts[:2], parts[2].reshape(total, 1, slots))
    return departures, grad.reshape(rows, cols, wide)


def solution(mesh):
    placed = (
        P("lat", "lon", None),
        P(None, ("lat", "lon"), None, None),
        P(None, ("lat", "lon"), None, None),
        P(None, ("lat", "lon"), None),
        P(None, ("lat", "lon"), None),
        P(None, ("lat", "lon"), None),
    )
    return jax.shard_map(
        functools.partial(shards, (mesh.shape["lat"], mesh.shape["lon"])),
        mesh=mesh,
        in_specs=placed,
        out_specs=(P(None, ("lat", "lon"), None), P("lat", "lon", None)),
        check_vma=False,
    )
```

```python
import functools
import math

import jax
import jax.numpy as jnp
from jax import lax
from jax.experimental import pallas as pl
from jax.experimental.pallas import tpu as pltpu
from jax.sharding import PartitionSpec as P

MESH = pl.DeviceIdType.MESH
AWAY = -1000.0


def visit_order(z, line):
    half = line // 2
    if z < half:
        return [*range(half, line), *(p for p in range(half) if p != z), z]
    return [*range(half - 1, -1, -1), *(p for p in range(half, line) if p != z), z]


def pick(z, values):
    chosen = jnp.int32(values[0])
    for p in range(1, len(values)):
        chosen = jnp.where(z == p, jnp.int32(values[p]), chosen)
    return chosen


def weight_rows(position, frac, rows):
    ids = lax.broadcasted_iota(jnp.int32, (rows, position.shape[1]), 0).astype(jnp.float32)
    zero = jnp.zeros_like(ids)
    return jnp.where(
        ids == position, 1.0 - frac, jnp.where(ids == position + 1.0, frac, zero)
    )


def kernel(
    lat_n, lon_n, line, rows, cols, tile,
    field, cell_in, frac_in, innov_in, rinv_in, jac,
    gmain, hrecv, dep_out,
    cell_ref, frac_ref, innov_ref, rinv_ref,
    edge, innov, rinv, rowcol, meta, lent,
    tbl, met, jrecv, dep, part, gsend, rbuf, hsend,
    f_local, s_local, f_send, f_recv, e_send, e_own, b_send, e_recv, m_send, m_recv, l_send, l_recv, s_send, s_recv, j_send, j_recv, d_send, d_recv,
    g_send, g_recv, h_send, h_recv, from_low, from_high,
):
    inner = lon_n // line
    plane = lat_n * inner
    slots = jac.shape[3]
    cells = rows * cols
    halo = cells + cols
    lat, lon = lax.axis_index("lat"), lax.axis_index("lon")
    z, xi = lon // inner, lon % inner
    here = lat * inner + xi
    lat_up, lat_down = (lat + 1) % lat_n, (lat + lat_n - 1) % lat_n
    lon_up, lon_down = (lon + 1) % lon_n, (lon + lon_n - 1) % lon_n
    z_low, x_low = lon_down // inner, lon_down % inner
    orders = [visit_order(p, line) for p in range(line)]
    visits = [pick(z, [order[n] for order in orders]) for n in range(line)]

    def remote(src, dst, send, recv, to):
        return pltpu.make_async_remote_copy(
            src_ref=src, dst_ref=dst, send_sem=send, recv_sem=recv,
            device_id=to, device_id_type=MESH,
        )

    def landed(like, sem):
        pltpu.make_async_copy(like, like, sem).wait()

    def pieces(size, count):
        cuts = [-(-size * c // (16 * count)) * 16 for c in range(count)] + [size]
        return [pl.ds(a, b - a) for a, b in zip(cuts, cuts[1:])]

    field_pieces = pieces(cells, f_recv.shape[1])
    table_pieces = [pl.ds(cells, cols + 2 * rows), *pieces(cells, g_recv.shape[1] - 1)]

    def mate(i):
        to_lat, to_x = (lat + i // inner) % lat_n, (xi + i % inner) % inner
        return to_lat, to_x, (to_lat, z * inner + to_x)

    def lent_out(i, g):
        return (z == line - 1) & (i == moved) & (g == there)

    def source(i):
        return (lat + lat_n - i // inner) % lat_n, (xi + inner - i % inner) % inner

    moved = (lat_n // 2) * inner + inner // 2
    there = jnp.where(lat % 2 == 0, line - 2, max(line - 3, 0))
    lender, taker = z == line - 1, z == there
    spare = pl.ds(plane * slots, slots)

    has_low, has_high = z > 0, z < line - 1
    inside_line = has_low & has_high
    low, high = (lat, lon - inner), (lat, lon + inner)
    barrier = pltpu.get_barrier_semaphore()

    @pl.when(has_low)
    def _():
        pl.semaphore_signal(barrier, inc=1, device_id=low, device_id_type=MESH)

    @pl.when(has_high)
    def _():
        pl.semaphore_signal(barrier, inc=1, device_id=high, device_id_type=MESH)

    def greet(i, carry):
        pl.semaphore_signal(barrier, inc=1, device_id=mate(i)[2], device_id_type=MESH)
        return carry

    lax.fori_loop(1, plane, greet, 0)

    own_field = tbl.at[z, pl.ds(0, cells)]
    local = pltpu.make_async_copy(field, own_field, f_local)
    smalls = [
        pltpu.make_async_copy(src, dst, s_local.at[k])
        for k, (src, dst) in enumerate((
            (cell_in, cell_ref), (frac_in, frac_ref), (innov_in, innov_ref), (rinv_in, rinv_ref),
        ))
    ]
    for copy in (*smalls, local):
        copy.start()
    for g in visits:
        pltpu.make_async_copy(
            jac.at[lat, g, xi], jrecv.at[g, pl.ds(0, slots)], j_recv.at[g, 0]
        ).start()

    @pl.when(jnp.logical_not(has_low))
    def _():
        rbuf[z] = jnp.zeros(rbuf.shape[1:], rbuf.dtype)

    @pl.when(jnp.logical_not(has_high))
    def _():
        rbuf[line] = jnp.zeros(rbuf.shape[1:], rbuf.dtype)

    has_south, has_north = lat > 0, lat < lat_n - 1
    row_rim, edge_rim = pl.ds(cells, cols), pl.ds(halo, rows)
    tip = min(8, rows)
    corner_rim, rim = pl.ds(halo + rows, tip), pl.ds(cells, cols + 2 * rows)
    sent_rim = pl.ds(cells, cols + rows + tip)
    if rows > tip:
        tbl[z, pl.ds(halo + rows + tip, rows - tip), :] = jnp.zeros(
            (rows - tip, tbl.shape[2]), tbl.dtype
        )

    @pl.when(jnp.logical_not(has_north))
    def _():
        tbl[z, row_rim, :] = jnp.zeros((cols, tbl.shape[2]), tbl.dtype)
        tbl[z, corner_rim, :] = jnp.zeros((tip, tbl.shape[2]), tbl.dtype)

    @pl.when(jnp.logical_not(has_south))
    def _():
        hrecv[0] = jnp.zeros(hrecv.shape[1:], hrecv.dtype)
        hrecv[2] = jnp.zeros(hrecv.shape[1:], hrecv.dtype)

    for copy in smalls:
        copy.wait()
    innov[...] = innov_ref[...].astype(jnp.float32)
    rinv[...] = rinv_ref[...].astype(jnp.float32)
    cell = cell_ref[...].astype(jnp.float32)
    live = cell >= 0.0
    row = jnp.floor((cell + 0.5) * (1.0 / (cols + 1)))
    rowcol[0] = jnp.where(live, row, AWAY)
    rowcol[1] = jnp.where(live, cell - row * (cols + 1), AWAY)

    def build(i, carry):
        to_lat, to_x, _ = mate(i)
        for g in range(line):
            owner = to_lat * lon_n + g * inner + to_x
            meta[i, g] = jnp.concatenate(
                [
                    rowcol[0, pl.ds(owner, 1), :],
                    rowcol[1, pl.ds(owner, 1), :],
                    frac_ref[owner].astype(jnp.float32),
                    innov[pl.ds(owner, 1), :],
                    rinv[pl.ds(owner, 1), :],
                    jnp.zeros((2, slots), jnp.float32),
                ],
                axis=0,
            ).astype(meta.dtype)
        return carry

    lax.fori_loop(0, plane, build, 0)

    @pl.when(lender)
    def _():
        lent[...] = meta[moved, there]
        meta[moved, there] = jnp.full(lent.shape, AWAY, lent.dtype)
        jrecv[there, pl.ds(moved * slots, slots), :] = jnp.zeros(
            (slots, jrecv.shape[2]), jrecv.dtype
        )

    local.wait()
    edge[...] = jnp.concatenate(
        [tbl[z, pl.ds(r * cols, cols), :].astype(jnp.float32)[0:1] for r in range(rows)], axis=0
    ).astype(edge.dtype)
    pltpu.make_async_copy(meta.at[0], met.at[:, :, pl.ds(0, slots)], m_recv).start()
    pl.semaphore_wait(barrier, plane - 1 + has_low.astype(jnp.int32) + has_high.astype(jnp.int32))

    def send_field(g, c, up):
        piece = tbl.at[g, field_pieces[c]]
        remote(piece, piece, f_send, f_recv.at[g, c], high if up else low).start()

    def send_meta(i, carry):
        place = pl.ds(pl.multiple_of(i * slots, slots), slots)
        remote(meta.at[i], met.at[:, :, place], m_send, m_recv, mate(i)[2]).start()
        return carry

    half = plane // 2
    bounds = (0, half, plane - 1, plane)
    moved_piece = 0 if moved < half else 1 if moved < plane - 1 else 2

    def piece_of(i):
        return (i >= half).astype(jnp.int32) + (i >= plane - 1).astype(jnp.int32)

    def jac_landed(g, *which):
        for h in which:
            lanes = pl.ds(bounds[h] * slots, (bounds[h + 1] - bounds[h]) * slots)
            landed(jrecv.at[g, lanes], j_recv.at[g, h])

    def send_jac(n):
        g = visits[n]

        def one(i, carry):
            @pl.when(jnp.logical_not(lent_out(i, g)))
            def _():
                to_lat, to_x, at = mate(i)
                place = pl.ds(pl.multiple_of(i * slots, slots), slots)
                remote(
                    jac.at[to_lat, g, to_x], jrecv.at[g, place], j_send,
                    j_recv.at[g, piece_of(i)], at,
                ).start()

            return carry

        return one

    def send_edge():
        remote(edge, tbl.at[z_low, edge_rim], e_send, e_own, (lat, lon_down)).start()

        @pl.when(has_south)
        def _():
            remote(edge.at[pl.ds(0, tip)], tbl.at[z_low, corner_rim], e_send, e_own,
                   (lat_down, lon_down)).start()

    early = plane - plane // 4
    lax.fori_loop(1, plane, send_meta, 0)
    lax.fori_loop(1, 3, send_jac(0), 0)
    for c in range(len(field_pieces)):
        @pl.when(has_low & (z >= line // 2))
        def _():
            send_field(z, c, False)

        @pl.when(has_high & (z < line // 2))
        def _():
            send_field(z, c, True)

    @pl.when(has_south)
    def _():
        remote(tbl.at[z, pl.ds(0, cols)], tbl.at[z, row_rim], e_send, e_own,
               (lat_down, lon)).start()

    @pl.when(xi > 0)
    def _():
        send_edge()

    lax.fori_loop(3, early, send_jac(0), 0)

    for _ in range(line - 1):
        @pl.when(has_low)
        def _():
            pl.semaphore_signal(from_high, inc=1, device_id=low, device_id_type=MESH)

        @pl.when(has_high)
        def _():
            pl.semaphore_signal(from_low, inc=1, device_id=high, device_id_type=MESH)

        @pl.when(has_low)
        def _():
            pl.semaphore_wait(from_low, 1)

        @pl.when(has_high)
        def _():
            pl.semaphore_wait(from_high, 1)

    @pl.when(xi == 0)
    def _():
        send_edge()

    lax.fori_loop(early, plane, send_jac(0), 0)
    for n in range(1, line):
        lax.fori_loop(1, plane, send_jac(n), 0)

    @pl.when(lender)
    def _():
        to_lat, to_x, _ = mate(moved)
        at = (to_lat, there * inner + to_x)
        remote(lent, met.at[there, :, spare], l_send, l_recv, at).start()
        remote(jac.at[to_lat, there, to_x], jrecv.at[there, spare], j_send, s_recv, at).start()

    def field_landed(g, c):
        landed(tbl.at[g, field_pieces[c]], f_recv.at[g, c])

    def forward(d):
        for c in range(len(field_pieces)):
            @pl.when(inside_line & (z >= d))
            def _():
                field_landed(z - d, c)
                send_field(z - d, c, True)

            @pl.when(inside_line & (z + d < line))
            def _():
                field_landed(z + d, c)
                send_field(z + d, c, False)

    inside = jnp.where(lat < lat_n - 1, 1.0, 0.0)
    width = tile * slots
    tiles = plane // tile
    pad = -(-(max(rows, cols) + 1) // 8) * 8

    def terms(g, start, width):
        lanes = pl.ds(pl.multiple_of(start, slots), width)
        info = met[g, :, lanes].astype(jnp.float32)
        lat_w = weight_rows(info[0:1], info[2:3], pad)
        lon_w = weight_rows(info[1:2], info[3:4], pad)
        lon_c = lon_w[:cols]
        lon_e = lon_w[cols:cols + 1]
        lat_n_row = lat_w[rows:rows + 1] * inside
        first = lax.broadcasted_iota(jnp.int32, (rows, width), 0) == 0
        blocks = [lat_w[r:r + 1] * lon_c for r in range(rows)]
        blocks.append(lat_n_row * lon_c)
        blocks.append(lat_w[:rows] * lon_e)
        blocks.append(
            jnp.where(first, jnp.broadcast_to(lat_n_row * lon_e, (rows, width)), 0.0)
        )
        spread = jnp.concatenate(blocks, axis=0).astype(jnp.bfloat16).astype(jnp.float32)
        jac_t = jrecv[g, lanes]
        products = lax.dot_general(
            tbl[g], jac_t, (((1,), (1,)), ((), ())), preferred_element_type=jnp.float32
        )
        evolved = jnp.sum(spread * products, axis=0, keepdims=True)
        departure = jnp.where(info[0:1] >= 0.0, evolved - info[4:5], 0.0)
        dep[g, :, lanes] = departure
        return (spread * (info[5:6] * departure)).astype(jnp.bfloat16), jac_t

    def compute(n, g):
        into = part.at[n]

        def one_tile(t, carry):
            scaled, jac_t = terms(g, t * width, width)
            into[...] += jnp.dot(scaled, jac_t, preferred_element_type=jnp.float32)
            return carry

        if tiles > 1:
            into[...] = jnp.zeros(into.shape, into.dtype)
            lax.fori_loop(0, tiles, one_tile, 0)
        else:
            scaled, jac_t = terms(g, 0, width)
            into[...] = jnp.dot(scaled, jac_t, preferred_element_type=jnp.float32)

    def send_dep(g, first, last):
        def one(i, carry):
            @pl.when(jnp.logical_not(lent_out(i, g)))
            def _():
                to_lat, to_x = source(i)
                place = pl.ds(pl.multiple_of(i * slots, slots), slots)
                remote(
                    dep.at[g, :, place], dep_out.at[lat, g, xi], d_send, d_recv,
                    (to_lat, z * inner + to_x),
                ).start()

            return carry

        lax.fori_loop(max(first, 1), last, one, 0)
        if first == 0:
            pltpu.make_async_copy(
                dep.at[g, :, pl.ds(0, slots)], dep_out.at[lat, g, xi], d_recv
            ).start()

    def finish(n, incoming):
        g = visits[n]
        up = g > z
        next_z = jnp.where(up, z + 1, z - 1)
        slot = jnp.where((g == next_z) & jnp.logical_not(up), line, g)
        for c, at in enumerate(table_pieces):
            total = part[n, at, :]
            if incoming:
                landed(rbuf.at[g, at], g_recv.at[g, c])
                total = total + rbuf[g, at, :].astype(jnp.float32)
            gsend[n, at, :] = total.astype(gsend.dtype)
            remote(gsend.at[n, at], rbuf.at[slot, at], g_send, g_recv.at[slot, c],
                   (lat, next_z * inner + xi)).start()

    def pass_on(n):
        @pl.when(inside_line)
        def _():
            finish(n, True)

    for d in range(1, max(line // 2, 1)):
        forward(d)

    @pl.when(has_north)
    def _():
        landed(tbl.at[z, sent_rim], e_own)

    @pl.when(jnp.logical_not(has_north))
    def _():
        landed(edge, e_own)

    for i in range(1, line):
        remote(tbl.at[z, rim], tbl.at[z, rim], b_send, e_recv.at[z],
               (lat, (z + i) % line * inner + xi)).start()
    landed(met.at[:, :, pl.ds(0, plane * slots)], m_recv)
    for n in range(line - 1):
        g = visits[n]

        @pl.when(jnp.logical_not(inside_line))
        def _():
            for c in range(len(field_pieces)):
                field_landed(g, c)

        landed(tbl.at[g, rim], e_recv.at[g])
        jac_landed(g, *(h for h in range(3) if h != moved_piece))

        @pl.when(lent_out(moved, g))
        def _():
            rest = bounds[moved_piece + 1] - bounds[moved_piece] - 1
            if rest > 0:
                landed(jrecv.at[g, pl.ds(0, rest * slots)], j_recv.at[g, moved_piece])

        @pl.when(jnp.logical_not(lent_out(moved, g)))
        def _():
            jac_landed(g, moved_piece)

        compute(n, g)
        send_dep(g, 0, plane)

        @pl.when(jnp.logical_not(inside_line))
        def _():
            finish(n, False)

        if n == 0:
            for d in range(max(line // 2, 1), line - 1):
                forward(d)
            for c in range(len(field_pieces)):
                @pl.when(has_low & (z < line // 2))
                def _():
                    send_field(z, c, False)

                @pl.when(has_high & (z >= line // 2))
                def _():
                    send_field(z, c, True)
        elif n == 1:
            pass_on(0)
            pass_on(1)
        else:
            pass_on(n)

    main = pl.ds(0, cells)

    def arrived(at):
        return rbuf[z, at, :].astype(jnp.float32) + rbuf[line, at, :].astype(jnp.float32)

    def sums_landed(first, last):
        for c in range(first, last):
            at = table_pieces[c]

            @pl.when(has_low)
            def _():
                landed(rbuf.at[z, at], g_recv.at[z, c])

            @pl.when(has_high)
            def _():
                landed(rbuf.at[line, at], g_recv.at[line, c])

    def gather_rim():
        sums_landed(0, 1)
        part[line - 1, rim, :] += arrived(rim)

    def send_rim(values):
        hsend[...] = values.astype(hsend.dtype)
        remote(hsend.at[pl.ds(cols, rows)], hrecv.at[1], h_send, h_recv, (lat, lon_up)).start()

        @pl.when(has_north)
        def _():
            remote(hsend.at[pl.ds(cols + rows, tip)], hrecv.at[2, pl.ds(0, tip)], h_send, h_recv,
                   (lat_up, lon_up)).start()
            remote(hsend.at[pl.ds(0, cols)], hrecv.at[0], h_send, h_recv, (lat_up, lon)).start()

    def take_spare():
        landed(met.at[z, :, spare], l_recv)
        landed(jrecv.at[z, spare], s_recv)
        return terms(z, plane * slots, slots)

    def return_spare():
        to_lat, to_x = source(moved)
        remote(dep.at[z, :, spare], dep_out.at[lat, z, xi], s_send, d_recv,
               (to_lat, (line - 1) * inner + to_x)).start()

    def add(terms_of):
        scaled, jac_t = terms_of
        part[line - 1] += jnp.dot(scaled, jac_t, preferred_element_type=jnp.float32)

    def conclude(terms_of, send_rest):
        scaled, jac_t = terms_of
        send_rest()
        send_rim(part[line - 1, rim, :] + jnp.dot(
            scaled[cells:], jac_t, preferred_element_type=jnp.float32
        ))
        sums_landed(1, len(table_pieces))
        gmain[...] = arrived(main) + part[line - 1, main, :] + jnp.dot(
            scaled[:cells], jac_t, preferred_element_type=jnp.float32
        )

    if tiles > 1:
        jac_landed(z, 0, 1, 2)
        compute(line - 1, z)
        send_dep(z, 0, plane)

        @pl.when(taker)
        def _():
            add(take_spare())
            return_spare()

        gather_rim()
        send_rim(part[line - 1, rim, :])
        sums_landed(1, len(table_pieces))
        gmain[...] = part[line - 1, main, :] + arrived(main)
    else:
        jac_landed(z, 0)
        scaled, jac_t = terms(z, 0, half * slots)
        part[line - 1] = jnp.dot(scaled, jac_t, preferred_element_type=jnp.float32)
        send_dep(z, 0, half)
        jac_landed(z, 1)

        @pl.when(taker)
        def _():
            jac_landed(z, 2)
            add(terms(z, half * slots, half * slots))
            gather_rim()
            send_dep(z, half, plane)
            conclude(take_spare(), return_spare)

        @pl.when(jnp.logical_not(taker))
        def _():
            add(terms(z, half * slots, (half - 1) * slots))
            gather_rim()
            send_dep(z, half, plane - 1)
            jac_landed(z, 2)
            conclude(
                terms(z, (plane - 1) * slots, slots), lambda: send_dep(z, plane - 1, plane)
            )

    others = pl.ds(0, (plane - 1) * slots)
    for up in (False, True):
        for i in range(line):
            sent = (z >= i) & has_high if up else (z + i < line) & has_low

            @pl.when(sent & (inside_line | (i == 0)))
            def _():
                landed(own_field, f_send)
    @pl.when(has_south)
    def _():
        landed(tbl.at[z, sent_rim], e_send)

    @pl.when(jnp.logical_not(has_south))
    def _():
        landed(edge, e_send)

    landed(tbl.at[pl.ds(0, line - 1), rim], b_send)
    landed(met.at[:, :, others], m_send)
    landed(jrecv.at[:, others], j_send)
    landed(dep.at[pl.ds(0, line - 1), :, others], d_send)
    landed(dep.at[0, :, pl.ds(0, (plane - 2) * slots)], d_send)

    @pl.when(jnp.logical_not(lender))
    def _():
        landed(dep.at[0, :, pl.ds(0, slots)], d_send)

    @pl.when(lender)
    def _():
        landed(lent, l_send)

    @pl.when(taker)
    def _():
        landed(dep.at[0, :, spare], s_send)

    landed(gsend, g_send)
    @pl.when(has_north)
    def _():
        landed(tbl.at[z, sent_rim], h_send)

    @pl.when(jnp.logical_not(has_north))
    def _():
        landed(edge, h_send)

    @pl.when(has_south)
    def _():
        landed(tbl.at[z, sent_rim], h_recv)

    @pl.when(jnp.logical_not(has_south))
    def _():
        landed(edge, h_recv)

    landed(dep_out, d_recv)


def last_sums(rows, cols, gmain, hrecv, dep, grad_out, dep_out):
    dep_out[...] = dep[...]
    grad_out[...] = gmain[...]
    grad_out[pl.ds(0, cols), :] += hrecv[0].astype(jnp.float32)
    east = hrecv[1].astype(jnp.float32)
    corner = hrecv[2].astype(jnp.float32)
    for r in range(rows):
        extra = east[r:r + 1]
        if r == 0:
            extra = extra + corner[0:1]
        grad_out[pl.ds(r * cols, 1), :] += extra


def shards(mesh_shape, field, obs_jac, obs_frac, obs_innov, obs_rinv, obs_cells):
    lat_n, lon_n = mesh_shape
    line = math.gcd(lon_n // 2, 4)
    inner = lon_n // line
    plane = lat_n * inner
    total = lat_n * lon_n
    rows, cols, wide = field.shape
    slots = obs_jac.shape[2]
    tile = math.gcd(plane, 8)
    cells = rows * cols
    table = cells + cols + 2 * rows
    f32, bf16 = jnp.float32, jnp.bfloat16
    dma = pltpu.SemaphoreType.DMA
    one = pltpu.SemaphoreType.DMA(())
    vmem = pl.BlockSpec(memory_space=pltpu.VMEM)
    anywhere = pl.BlockSpec(memory_space=pltpu.HBM)
    parts = pl.pallas_call(
        functools.partial(kernel, lat_n, lon_n, line, rows, cols, tile),
        out_shape=(
            pltpu.VMEM((cells, wide), f32),
            pltpu.VMEM((3, rows, wide), bf16),
            pltpu.VMEM((lat_n, line, inner, 1, slots), f32),
        ),
        in_specs=[anywhere] * 6,
        out_specs=(vmem,) * 3,
        scratch_shapes=[
            pltpu.VMEM((total, slots), jnp.int32),
            pltpu.VMEM((total, 2, slots), bf16),
            pltpu.VMEM((total, slots), bf16),
            pltpu.VMEM((total, slots), bf16),
            pltpu.VMEM((rows, wide), bf16),
            pltpu.VMEM((total, slots), f32),
            pltpu.VMEM((total, slots), f32),
            pltpu.VMEM((2, total, slots), f32),
            pltpu.VMEM((plane, line, 8, slots), bf16),
            pltpu.VMEM((8, slots), bf16),
            pltpu.VMEM((line, table, wide), bf16),
            pltpu.VMEM((line, 8, (plane + 1) * slots), bf16),
            pltpu.VMEM((line, (plane + 1) * slots, wide), bf16),
            pltpu.VMEM((line, 1, (plane + 1) * slots), f32),
            pltpu.VMEM((line, table, wide), f32),
            pltpu.VMEM((line - 1, table, wide), bf16),
            pltpu.VMEM((line + 1, table, wide), bf16),
            pltpu.VMEM((table - cells, wide), bf16),
            one, dma((4,)), one, dma((line, 2)),
            one, one, one, dma((line,)),
            one, one,
            one, one, one, one,
            one, dma((line, 3)),
            one, one,
            one, dma((line + 1, 3)),
            one, one,
            pltpu.SemaphoreType.REGULAR, pltpu.SemaphoreType.REGULAR,
        ],
        compiler_params=pltpu.CompilerParams(
            collective_id=0, has_side_effects=True, vmem_limit_bytes=62 * 1024 * 1024
        ),
    )(
        field.reshape(cells, wide),
        obs_cells.reshape(total, slots),
        obs_frac.reshape(total, 2, slots),
        obs_innov.reshape(total, slots),
        obs_rinv.reshape(total, slots),
        obs_jac.reshape(lat_n, line, inner, slots, wide),
    )
    grad, departures = pl.pallas_call(
        functools.partial(last_sums, rows, cols),
        out_shape=(
            jax.ShapeDtypeStruct((cells, wide), f32),
            jax.ShapeDtypeStruct((total, 1, slots), f32),
        ),
        in_specs=[vmem] * 3,
        out_specs=(vmem, vmem),
        compiler_params=pltpu.CompilerParams(vmem_limit_bytes=8 * 1024 * 1024),
    )(*parts[:2], parts[2].reshape(total, 1, slots))
    return departures, grad.reshape(rows, cols, wide)


def solution(mesh):
    placed = (
        P("lat", "lon", None),
        P(None, ("lat", "lon"), None, None),
        P(None, ("lat", "lon"), None, None),
        P(None, ("lat", "lon"), None),
        P(None, ("lat", "lon"), None),
        P(None, ("lat", "lon"), None),
    )
    return jax.shard_map(
        functools.partial(shards, (mesh.shape["lat"], mesh.shape["lon"])),
        mesh=mesh,
        in_specs=placed,
        out_specs=(P(None, ("lat", "lon"), None), P("lat", "lon", None)),
        check_vma=False,
    )
```

```python
import functools
import math

import jax
import jax.numpy as jnp
from jax import lax
from jax.experimental import pallas as pl
from jax.experimental.pallas import tpu as pltpu
from jax.sharding import PartitionSpec as P

MESH = pl.DeviceIdType.MESH
AWAY = -1000.0


def visit_order(z, line):
    half = line // 2
    if z < half:
        return [*range(half, line), *(p for p in range(half) if p != z), z]
    return [*range(half - 1, -1, -1), *(p for p in range(half, line) if p != z), z]


def pick(z, values):
    chosen = jnp.int32(values[0])
    for p in range(1, len(values)):
        chosen = jnp.where(z == p, jnp.int32(values[p]), chosen)
    return chosen


def weight_rows(position, frac, rows):
    ids = lax.broadcasted_iota(jnp.int32, (rows, position.shape[1]), 0).astype(jnp.float32)
    zero = jnp.zeros_like(ids)
    return jnp.where(
        ids == position, 1.0 - frac, jnp.where(ids == position + 1.0, frac, zero)
    )


def kernel(
    lat_n, lon_n, line, rows, cols, tile,
    field, cell_in, frac_in, innov_in, rinv_in, jac,
    gmain, hrecv, dep_out,
    cell_ref, frac_ref, innov_ref, rinv_ref,
    edge, innov, rinv, rowcol, meta, lent,
    tbl, met, jrecv, dep, part, gsend, rbuf, hsend,
    f_local, s_local, f_send, f_recv, e_send, e_own, b_send, e_recv, m_send, m_recv, l_send, l_recv, s_send, s_recv, j_send, j_recv, d_send, d_recv,
    g_send, g_recv, h_send, h_recv, from_low, from_high,
):
    inner = lon_n // line
    plane = lat_n * inner
    slots = jac.shape[3]
    cells = rows * cols
    halo = cells + cols
    lat, lon = lax.axis_index("lat"), lax.axis_index("lon")
    z, xi = lon // inner, lon % inner
    here = lat * inner + xi
    lat_up, lat_down = (lat + 1) % lat_n, (lat + lat_n - 1) % lat_n
    lon_up, lon_down = (lon + 1) % lon_n, (lon + lon_n - 1) % lon_n
    z_low, x_low = lon_down // inner, lon_down % inner
    orders = [visit_order(p, line) for p in range(line)]
    visits = [pick(z, [order[n] for order in orders]) for n in range(line)]

    def remote(src, dst, send, recv, to):
        return pltpu.make_async_remote_copy(
            src_ref=src, dst_ref=dst, send_sem=send, recv_sem=recv,
            device_id=to, device_id_type=MESH,
        )

    def landed(like, sem):
        pltpu.make_async_copy(like, like, sem).wait()

    def pieces(size, count):
        cuts = [-(-size * c // (16 * count)) * 16 for c in range(count)] + [size]
        return [pl.ds(a, b - a) for a, b in zip(cuts, cuts[1:])]

    field_pieces = pieces(cells, f_recv.shape[1])
    table_pieces = [pl.ds(cells, cols + 2 * rows), *pieces(cells, g_recv.shape[1] - 1)]

    def mate(i):
        to_lat, to_x = (lat + i // inner) % lat_n, (xi + i % inner) % inner
        return to_lat, to_x, (to_lat, z * inner + to_x)

    def lent_out(i, g):
        return (z == line - 1) & (i == moved) & (g == there)

    def source(i):
        return (lat + lat_n - i // inner) % lat_n, (xi + inner - i % inner) % inner

    moved = (lat_n // 2) * inner + inner // 2
    there = jnp.where(lat % 2 == 0, line - 2, max(line - 3, 0))
    lender, taker = z == line - 1, z == there
    spare = pl.ds(plane * slots, slots)

    has_low, has_high = z > 0, z < line - 1
    inside_line = has_low & has_high
    low, high = (lat, lon - inner), (lat, lon + inner)
    barrier = pltpu.get_barrier_semaphore()

    @pl.when(has_low)
    def _():
        pl.semaphore_signal(barrier, inc=1, device_id=low, device_id_type=MESH)

    @pl.when(has_high)
    def _():
        pl.semaphore_signal(barrier, inc=1, device_id=high, device_id_type=MESH)

    def greet(i, carry):
        pl.semaphore_signal(barrier, inc=1, device_id=mate(i)[2], device_id_type=MESH)
        return carry

    lax.fori_loop(1, plane, greet, 0)

    own_field = tbl.at[z, pl.ds(0, cells)]
    local = pltpu.make_async_copy(field, own_field, f_local)
    smalls = [
        pltpu.make_async_copy(src, dst, s_local.at[k])
        for k, (src, dst) in enumerate((
            (cell_in, cell_ref), (frac_in, frac_ref), (innov_in, innov_ref), (rinv_in, rinv_ref),
        ))
    ]
    for copy in (*smalls, local):
        copy.start()
    for g in visits:
        pltpu.make_async_copy(
            jac.at[lat, g, xi], jrecv.at[g, pl.ds(0, slots)], j_recv.at[g, 0]
        ).start()

    @pl.when(jnp.logical_not(has_low))
    def _():
        rbuf[z] = jnp.zeros(rbuf.shape[1:], rbuf.dtype)

    @pl.when(jnp.logical_not(has_high))
    def _():
        rbuf[line] = jnp.zeros(rbuf.shape[1:], rbuf.dtype)

    has_south, has_north = lat > 0, lat < lat_n - 1
    row_rim, edge_rim = pl.ds(cells, cols), pl.ds(halo, rows)
    tip = min(8, rows)
    corner_rim, rim = pl.ds(halo + rows, tip), pl.ds(cells, cols + 2 * rows)
    sent_rim = pl.ds(cells, cols + rows + tip)
    if rows > tip:
        tbl[z, pl.ds(halo + rows + tip, rows - tip), :] = jnp.zeros(
            (rows - tip, tbl.shape[2]), tbl.dtype
        )

    @pl.when(jnp.logical_not(has_north))
    def _():
        tbl[z, row_rim, :] = jnp.zeros((cols, tbl.shape[2]), tbl.dtype)
        tbl[z, corner_rim, :] = jnp.zeros((tip, tbl.shape[2]), tbl.dtype)

    @pl.when(jnp.logical_not(has_south))
    def _():
        hrecv[0] = jnp.zeros(hrecv.shape[1:], hrecv.dtype)
        hrecv[2] = jnp.zeros(hrecv.shape[1:], hrecv.dtype)

    for copy in smalls:
        copy.wait()
    innov[...] = innov_ref[...].astype(jnp.float32)
    rinv[...] = rinv_ref[...].astype(jnp.float32)
    cell = cell_ref[...].astype(jnp.float32)
    live = cell >= 0.0
    row = jnp.floor((cell + 0.5) * (1.0 / (cols + 1)))
    rowcol[0] = jnp.where(live, row, AWAY)
    rowcol[1] = jnp.where(live, cell - row * (cols + 1), AWAY)

    def build(i, carry):
        to_lat, to_x, _ = mate(i)
        for g in range(line):
            owner = to_lat * lon_n + g * inner + to_x
            meta[i, g] = jnp.concatenate(
                [
                    rowcol[0, pl.ds(owner, 1), :],
                    rowcol[1, pl.ds(owner, 1), :],
                    frac_ref[owner].astype(jnp.float32),
                    innov[pl.ds(owner, 1), :],
                    rinv[pl.ds(owner, 1), :],
                    jnp.zeros((2, slots), jnp.float32),
                ],
                axis=0,
            ).astype(meta.dtype)
        return carry

    lax.fori_loop(0, plane, build, 0)

    @pl.when(lender)
    def _():
        lent[...] = meta[moved, there]
        meta[moved, there] = jnp.full(lent.shape, AWAY, lent.dtype)
        jrecv[there, pl.ds(moved * slots, slots), :] = jnp.zeros(
            (slots, jrecv.shape[2]), jrecv.dtype
        )

    local.wait()
    edge[...] = jnp.concatenate(
        [tbl[z, pl.ds(r * cols, cols), :].astype(jnp.float32)[0:1] for r in range(rows)], axis=0
    ).astype(edge.dtype)
    pltpu.make_async_copy(meta.at[0], met.at[:, :, pl.ds(0, slots)], m_recv).start()
    pl.semaphore_wait(barrier, plane - 1 + has_low.astype(jnp.int32) + has_high.astype(jnp.int32))

    def send_field(g, c, up):
        piece = tbl.at[g, field_pieces[c]]
        remote(piece, piece, f_send, f_recv.at[g, c], high if up else low).start()

    def send_meta(i, carry):
        place = pl.ds(pl.multiple_of(i * slots, slots), slots)
        remote(meta.at[i], met.at[:, :, place], m_send, m_recv, mate(i)[2]).start()
        return carry

    half = plane // 2
    tip_at = plane - 2
    bounds = (0, half, tip_at, plane)
    moved_piece = 0 if moved < half else 1 if moved < tip_at else 2

    def piece_of(i):
        return (i >= half).astype(jnp.int32) + (i >= tip_at).astype(jnp.int32)

    def jac_landed(g, *which):
        for h in which:
            lanes = pl.ds(bounds[h] * slots, (bounds[h + 1] - bounds[h]) * slots)
            landed(jrecv.at[g, lanes], j_recv.at[g, h])

    def send_jac(n):
        g = visits[n]

        def one(i, carry):
            @pl.when(jnp.logical_not(lent_out(i, g)))
            def _():
                to_lat, to_x, at = mate(i)
                place = pl.ds(pl.multiple_of(i * slots, slots), slots)
                remote(
                    jac.at[to_lat, g, to_x], jrecv.at[g, place], j_send,
                    j_recv.at[g, piece_of(i)], at,
                ).start()

            return carry

        return one

    def send_edge():
        remote(edge, tbl.at[z_low, edge_rim], e_send, e_own, (lat, lon_down)).start()

        @pl.when(has_south)
        def _():
            remote(edge.at[pl.ds(0, tip)], tbl.at[z_low, corner_rim], e_send, e_own,
                   (lat_down, lon_down)).start()

    early = plane - plane // 4
    lax.fori_loop(1, plane, send_meta, 0)
    lax.fori_loop(1, 3, send_jac(0), 0)
    for c in range(len(field_pieces)):
        @pl.when(has_low & (z >= line // 2))
        def _():
            send_field(z, c, False)

        @pl.when(has_high & (z < line // 2))
        def _():
            send_field(z, c, True)

    @pl.when(has_south)
    def _():
        remote(tbl.at[z, pl.ds(0, cols)], tbl.at[z, row_rim], e_send, e_own,
               (lat_down, lon)).start()

    @pl.when(xi > 0)
    def _():
        send_edge()

    lax.fori_loop(3, early, send_jac(0), 0)

    for _ in range(line - 1):
        @pl.when(has_low)
        def _():
            pl.semaphore_signal(from_high, inc=1, device_id=low, device_id_type=MESH)

        @pl.when(has_high)
        def _():
            pl.semaphore_signal(from_low, inc=1, device_id=high, device_id_type=MESH)

        @pl.when(has_low)
        def _():
            pl.semaphore_wait(from_low, 1)

        @pl.when(has_high)
        def _():
            pl.semaphore_wait(from_high, 1)

    @pl.when(xi == 0)
    def _():
        send_edge()

    lax.fori_loop(early, plane, send_jac(0), 0)
    for n in range(1, line):
        lax.fori_loop(1, plane, send_jac(n), 0)

    @pl.when(lender)
    def _():
        to_lat, to_x, _ = mate(moved)
        at = (to_lat, there * inner + to_x)
        remote(lent, met.at[there, :, spare], l_send, l_recv, at).start()
        remote(jac.at[to_lat, there, to_x], jrecv.at[there, spare], j_send, s_recv, at).start()

    def field_landed(g, c):
        landed(tbl.at[g, field_pieces[c]], f_recv.at[g, c])

    def forward(d):
        for c in range(len(field_pieces)):
            @pl.when(inside_line & (z >= d))
            def _():
                field_landed(z - d, c)
                send_field(z - d, c, True)

            @pl.when(inside_line & (z + d < line))
            def _():
                field_landed(z + d, c)
                send_field(z + d, c, False)

    inside = jnp.where(lat < lat_n - 1, 1.0, 0.0)
    width = tile * slots
    tiles = plane // tile
    pad = -(-(max(rows, cols) + 1) // 8) * 8

    def terms(g, start, width):
        lanes = pl.ds(pl.multiple_of(start, slots), width)
        info = met[g, :, lanes].astype(jnp.float32)
        lat_w = weight_rows(info[0:1], info[2:3], pad)
        lon_w = weight_rows(info[1:2], info[3:4], pad)
        lon_c = lon_w[:cols]
        lon_e = lon_w[cols:cols + 1]
        lat_n_row = lat_w[rows:rows + 1] * inside
        first = lax.broadcasted_iota(jnp.int32, (rows, width), 0) == 0
        blocks = [lat_w[r:r + 1] * lon_c for r in range(rows)]
        blocks.append(lat_n_row * lon_c)
        blocks.append(lat_w[:rows] * lon_e)
        blocks.append(
            jnp.where(first, jnp.broadcast_to(lat_n_row * lon_e, (rows, width)), 0.0)
        )
        spread = jnp.concatenate(blocks, axis=0).astype(jnp.bfloat16).astype(jnp.float32)
        jac_t = jrecv[g, lanes]
        products = lax.dot_general(
            tbl[g], jac_t, (((1,), (1,)), ((), ())), preferred_element_type=jnp.float32
        )
        evolved = jnp.sum(spread * products, axis=0, keepdims=True)
        departure = jnp.where(info[0:1] >= 0.0, evolved - info[4:5], 0.0)
        dep[g, :, lanes] = departure
        return (spread * (info[5:6] * departure)).astype(jnp.bfloat16), jac_t

    def compute(n, g):
        into = part.at[n]

        def one_tile(t, carry):
            scaled, jac_t = terms(g, t * width, width)
            into[...] += jnp.dot(scaled, jac_t, preferred_element_type=jnp.float32)
            return carry

        if tiles > 1:
            into[...] = jnp.zeros(into.shape, into.dtype)
            lax.fori_loop(0, tiles, one_tile, 0)
        else:
            scaled, jac_t = terms(g, 0, width)
            into[...] = jnp.dot(scaled, jac_t, preferred_element_type=jnp.float32)

    def send_dep(g, first, last):
        def one(i, carry):
            @pl.when(jnp.logical_not(lent_out(i, g)))
            def _():
                to_lat, to_x = source(i)
                place = pl.ds(pl.multiple_of(i * slots, slots), slots)
                remote(
                    dep.at[g, :, place], dep_out.at[lat, g, xi], d_send, d_recv,
                    (to_lat, z * inner + to_x),
                ).start()

            return carry

        lax.fori_loop(max(first, 1), last, one, 0)
        if first == 0:
            pltpu.make_async_copy(
                dep.at[g, :, pl.ds(0, slots)], dep_out.at[lat, g, xi], d_recv
            ).start()

    def finish(n, incoming):
        g = visits[n]
        up = g > z
        next_z = jnp.where(up, z + 1, z - 1)
        slot = jnp.where((g == next_z) & jnp.logical_not(up), line, g)
        for c, at in enumerate(table_pieces):
            total = part[n, at, :]
            if incoming:
                landed(rbuf.at[g, at], g_recv.at[g, c])
                total = total + rbuf[g, at, :].astype(jnp.float32)
            gsend[n, at, :] = total.astype(gsend.dtype)
            remote(gsend.at[n, at], rbuf.at[slot, at], g_send, g_recv.at[slot, c],
                   (lat, next_z * inner + xi)).start()

    def pass_on(n):
        @pl.when(inside_line)
        def _():
            finish(n, True)

    for d in range(1, max(line // 2, 1)):
        forward(d)

    @pl.when(has_north)
    def _():
        landed(tbl.at[z, sent_rim], e_own)

    @pl.when(jnp.logical_not(has_north))
    def _():
        landed(edge, e_own)

    for i in range(1, line):
        remote(tbl.at[z, rim], tbl.at[z, rim], b_send, e_recv.at[z],
               (lat, (z + i) % line * inner + xi)).start()
    landed(met.at[:, :, pl.ds(0, plane * slots)], m_recv)
    for n in range(line - 1):
        g = visits[n]

        @pl.when(jnp.logical_not(inside_line))
        def _():
            for c in range(len(field_pieces)):
                field_landed(g, c)

        landed(tbl.at[g, rim], e_recv.at[g])
        jac_landed(g, *(h for h in range(3) if h != moved_piece))

        @pl.when(lent_out(moved, g))
        def _():
            rest = bounds[moved_piece + 1] - bounds[moved_piece] - 1
            if rest > 0:
                landed(jrecv.at[g, pl.ds(0, rest * slots)], j_recv.at[g, moved_piece])

        @pl.when(jnp.logical_not(lent_out(moved, g)))
        def _():
            jac_landed(g, moved_piece)

        compute(n, g)
        send_dep(g, 0, plane)

        @pl.when(jnp.logical_not(inside_line))
        def _():
            finish(n, False)

        if n == 0:
            for d in range(max(line // 2, 1), line - 1):
                forward(d)
            for c in range(len(field_pieces)):
                @pl.when(has_low & (z < line // 2))
                def _():
                    send_field(z, c, False)

                @pl.when(has_high & (z >= line // 2))
                def _():
                    send_field(z, c, True)
        elif n == 1:
            pass_on(0)
            pass_on(1)
        else:
            pass_on(n)

    main = pl.ds(0, cells)

    def arrived(at):
        return rbuf[z, at, :].astype(jnp.float32) + rbuf[line, at, :].astype(jnp.float32)

    def sums_landed(first, last):
        for c in range(first, last):
            at = table_pieces[c]

            @pl.when(has_low)
            def _():
                landed(rbuf.at[z, at], g_recv.at[z, c])

            @pl.when(has_high)
            def _():
                landed(rbuf.at[line, at], g_recv.at[line, c])

    def gather_rim():
        sums_landed(0, 1)
        part[line - 1, rim, :] += arrived(rim)

    def send_rim(values):
        hsend[...] = values.astype(hsend.dtype)
        remote(hsend.at[pl.ds(cols, rows)], hrecv.at[1], h_send, h_recv, (lat, lon_up)).start()

        @pl.when(has_north)
        def _():
            remote(hsend.at[pl.ds(cols + rows, tip)], hrecv.at[2, pl.ds(0, tip)], h_send, h_recv,
                   (lat_up, lon_up)).start()
            remote(hsend.at[pl.ds(0, cols)], hrecv.at[0], h_send, h_recv, (lat_up, lon)).start()

    def take_spare():
        landed(met.at[z, :, spare], l_recv)
        landed(jrecv.at[z, spare], s_recv)
        return terms(z, plane * slots, slots)

    def return_spare():
        to_lat, to_x = source(moved)
        remote(dep.at[z, :, spare], dep_out.at[lat, z, xi], s_send, d_recv,
               (to_lat, (line - 1) * inner + to_x)).start()

    def add(terms_of):
        scaled, jac_t = terms_of
        part[line - 1] += jnp.dot(scaled, jac_t, preferred_element_type=jnp.float32)

    def conclude(terms_of, send_rest):
        scaled, jac_t = terms_of
        send_rest()
        send_rim(part[line - 1, rim, :] + jnp.dot(
            scaled[cells:], jac_t, preferred_element_type=jnp.float32
        ))
        sums_landed(1, len(table_pieces))
        gmain[...] = arrived(main) + part[line - 1, main, :] + jnp.dot(
            scaled[:cells], jac_t, preferred_element_type=jnp.float32
        )

    if tiles > 1:
        jac_landed(z, 0, 1, 2)
        compute(line - 1, z)
        send_dep(z, 0, plane)

        @pl.when(taker)
        def _():
            add(take_spare())
            return_spare()

        gather_rim()
        send_rim(part[line - 1, rim, :])
        sums_landed(1, len(table_pieces))
        gmain[...] = part[line - 1, main, :] + arrived(main)
    else:
        jac_landed(z, 0)
        scaled, jac_t = terms(z, 0, half * slots)
        part[line - 1] = jnp.dot(scaled, jac_t, preferred_element_type=jnp.float32)
        send_dep(z, 0, half)
        jac_landed(z, 1)

        @pl.when(taker)
        def _():
            jac_landed(z, 2)
            add(terms(z, half * slots, half * slots))
            gather_rim()
            send_dep(z, half, plane)
            conclude(take_spare(), return_spare)

        @pl.when(jnp.logical_not(taker))
        def _():
            add(terms(z, half * slots, (tip_at - half) * slots))
            gather_rim()
            send_dep(z, half, tip_at)
            jac_landed(z, 2)
            conclude(
                terms(z, tip_at * slots, (plane - tip_at) * slots), lambda: send_dep(z, tip_at, plane)
            )

    others = pl.ds(0, (plane - 1) * slots)
    for up in (False, True):
        for i in range(line):
            sent = (z >= i) & has_high if up else (z + i < line) & has_low

            @pl.when(sent & (inside_line | (i == 0)))
            def _():
                landed(own_field, f_send)
    @pl.when(has_south)
    def _():
        landed(tbl.at[z, sent_rim], e_send)

    @pl.when(jnp.logical_not(has_south))
    def _():
        landed(edge, e_send)

    landed(tbl.at[pl.ds(0, line - 1), rim], b_send)
    landed(met.at[:, :, others], m_send)
    landed(jrecv.at[:, others], j_send)
    landed(dep.at[pl.ds(0, line - 1), :, others], d_send)
    landed(dep.at[0, :, pl.ds(0, (plane - 2) * slots)], d_send)

    @pl.when(jnp.logical_not(lender))
    def _():
        landed(dep.at[0, :, pl.ds(0, slots)], d_send)

    @pl.when(lender)
    def _():
        landed(lent, l_send)

    @pl.when(taker)
    def _():
        landed(dep.at[0, :, spare], s_send)

    landed(gsend, g_send)
    @pl.when(has_north)
    def _():
        landed(tbl.at[z, sent_rim], h_send)

    @pl.when(jnp.logical_not(has_north))
    def _():
        landed(edge, h_send)

    @pl.when(has_south)
    def _():
        landed(tbl.at[z, sent_rim], h_recv)

    @pl.when(jnp.logical_not(has_south))
    def _():
        landed(edge, h_recv)

    landed(dep_out, d_recv)


def last_sums(rows, cols, gmain, hrecv, dep, grad_out, dep_out):
    dep_out[...] = dep[...]
    grad_out[...] = gmain[...]
    grad_out[pl.ds(0, cols), :] += hrecv[0].astype(jnp.float32)
    east = hrecv[1].astype(jnp.float32)
    corner = hrecv[2].astype(jnp.float32)
    for r in range(rows):
        extra = east[r:r + 1]
        if r == 0:
            extra = extra + corner[0:1]
        grad_out[pl.ds(r * cols, 1), :] += extra


def shards(mesh_shape, field, obs_jac, obs_frac, obs_innov, obs_rinv, obs_cells):
    lat_n, lon_n = mesh_shape
    line = math.gcd(lon_n // 2, 4)
    inner = lon_n // line
    plane = lat_n * inner
    total = lat_n * lon_n
    rows, cols, wide = field.shape
    slots = obs_jac.shape[2]
    tile = math.gcd(plane, 8)
    cells = rows * cols
    table = cells + cols + 2 * rows
    f32, bf16 = jnp.float32, jnp.bfloat16
    dma = pltpu.SemaphoreType.DMA
    one = pltpu.SemaphoreType.DMA(())
    vmem = pl.BlockSpec(memory_space=pltpu.VMEM)
    anywhere = pl.BlockSpec(memory_space=pltpu.HBM)
    parts = pl.pallas_call(
        functools.partial(kernel, lat_n, lon_n, line, rows, cols, tile),
        out_shape=(
            pltpu.VMEM((cells, wide), f32),
            pltpu.VMEM((3, rows, wide), bf16),
            pltpu.VMEM((lat_n, line, inner, 1, slots), f32),
        ),
        in_specs=[anywhere] * 6,
        out_specs=(vmem,) * 3,
        scratch_shapes=[
            pltpu.VMEM((total, slots), jnp.int32),
            pltpu.VMEM((total, 2, slots), bf16),
            pltpu.VMEM((total, slots), bf16),
            pltpu.VMEM((total, slots), bf16),
            pltpu.VMEM((rows, wide), bf16),
            pltpu.VMEM((total, slots), f32),
            pltpu.VMEM((total, slots), f32),
            pltpu.VMEM((2, total, slots), f32),
            pltpu.VMEM((plane, line, 8, slots), bf16),
            pltpu.VMEM((8, slots), bf16),
            pltpu.VMEM((line, table, wide), bf16),
            pltpu.VMEM((line, 8, (plane + 1) * slots), bf16),
            pltpu.VMEM((line, (plane + 1) * slots, wide), bf16),
            pltpu.VMEM((line, 1, (plane + 1) * slots), f32),
            pltpu.VMEM((line, table, wide), f32),
            pltpu.VMEM((line - 1, table, wide), bf16),
            pltpu.VMEM((line + 1, table, wide), bf16),
            pltpu.VMEM((table - cells, wide), bf16),
            one, dma((4,)), one, dma((line, 2)),
            one, one, one, dma((line,)),
            one, one,
            one, one, one, one,
            one, dma((line, 3)),
            one, one,
            one, dma((line + 1, 3)),
            one, one,
            pltpu.SemaphoreType.REGULAR, pltpu.SemaphoreType.REGULAR,
        ],
        compiler_params=pltpu.CompilerParams(
            collective_id=0, has_side_effects=True, vmem_limit_bytes=62 * 1024 * 1024
        ),
    )(
        field.reshape(cells, wide),
        obs_cells.reshape(total, slots),
        obs_frac.reshape(total, 2, slots),
        obs_innov.reshape(total, slots),
        obs_rinv.reshape(total, slots),
        obs_jac.reshape(lat_n, line, inner, slots, wide),
    )
    grad, departures = pl.pallas_call(
        functools.partial(last_sums, rows, cols),
        out_shape=(
            jax.ShapeDtypeStruct((cells, wide), f32),
            jax.ShapeDtypeStruct((total, 1, slots), f32),
        ),
        in_specs=[vmem] * 3,
        out_specs=(vmem, vmem),
        compiler_params=pltpu.CompilerParams(vmem_limit_bytes=8 * 1024 * 1024),
    )(*parts[:2], parts[2].reshape(total, 1, slots))
    return departures, grad.reshape(rows, cols, wide)


def solution(mesh):
    placed = (
        P("lat", "lon", None),
        P(None, ("lat", "lon"), None, None),
        P(None, ("lat", "lon"), None, None),
        P(None, ("lat", "lon"), None),
        P(None, ("lat", "lon"), None),
        P(None, ("lat", "lon"), None),
    )
    return jax.shard_map(
        functools.partial(shards, (mesh.shape["lat"], mesh.shape["lon"])),
        mesh=mesh,
        in_specs=placed,
        out_specs=(P(None, ("lat", "lon"), None), P("lat", "lon", None)),
        check_vma=False,
    )
```

```python
import functools
import math

import jax
import jax.numpy as jnp
from jax import lax
from jax.experimental import pallas as pl
from jax.experimental.pallas import tpu as pltpu
from jax.sharding import PartitionSpec as P

MESH = pl.DeviceIdType.MESH
AWAY = -1000.0


def visit_order(z, line):
    half = line // 2
    if z < half:
        return [*range(half, line), *(p for p in range(half) if p != z), z]
    return [*range(half - 1, -1, -1), *(p for p in range(half, line) if p != z), z]


def pick(z, values):
    chosen = jnp.int32(values[0])
    for p in range(1, len(values)):
        chosen = jnp.where(z == p, jnp.int32(values[p]), chosen)
    return chosen


def weight_rows(position, frac, rows):
    ids = lax.broadcasted_iota(jnp.int32, (rows, position.shape[1]), 0).astype(jnp.float32)
    zero = jnp.zeros_like(ids)
    return jnp.where(
        ids == position, 1.0 - frac, jnp.where(ids == position + 1.0, frac, zero)
    )


def kernel(
    lat_n, lon_n, line, rows, cols, tile,
    field, cell_in, frac_in, innov_in, rinv_in, jac,
    gmain, hrecv, dep_out,
    cell_ref, frac_ref, innov_ref, rinv_ref,
    edge, innov, rinv, rowcol, meta, lent,
    tbl, met, jrecv, dep, part, gsend, rbuf, hsend,
    f_local, s_local, f_send, f_recv, e_send, e_own, b_send, e_recv, m_send, m_recv, l_send, l_recv, s_send, s_recv, j_send, j_recv, d_send, d_recv,
    g_send, g_recv, h_send, h_recv, from_low, from_high,
):
    inner = lon_n // line
    plane = lat_n * inner
    slots = jac.shape[3]
    cells = rows * cols
    halo = cells + cols
    lat, lon = lax.axis_index("lat"), lax.axis_index("lon")
    z, xi = lon // inner, lon % inner
    here = lat * inner + xi
    lat_up, lat_down = (lat + 1) % lat_n, (lat + lat_n - 1) % lat_n
    lon_up, lon_down = (lon + 1) % lon_n, (lon + lon_n - 1) % lon_n
    z_low, x_low = lon_down // inner, lon_down % inner
    orders = [visit_order(p, line) for p in range(line)]
    visits = [pick(z, [order[n] for order in orders]) for n in range(line)]

    def remote(src, dst, send, recv, to):
        return pltpu.make_async_remote_copy(
            src_ref=src, dst_ref=dst, send_sem=send, recv_sem=recv,
            device_id=to, device_id_type=MESH,
        )

    def landed(like, sem):
        pltpu.make_async_copy(like, like, sem).wait()

    def pieces(size, count):
        cuts = [-(-size * c // (16 * count)) * 16 for c in range(count)] + [size]
        return [pl.ds(a, b - a) for a, b in zip(cuts, cuts[1:])]

    field_pieces = pieces(cells, f_recv.shape[1])
    table_pieces = [pl.ds(cells, cols + 2 * rows), *pieces(cells, g_recv.shape[1] - 1)]

    def mate(i):
        to_lat, to_x = (lat + i // inner) % lat_n, (xi + i % inner) % inner
        return to_lat, to_x, (to_lat, z * inner + to_x)

    def lent_out(i, g):
        return (z == line - 1) & (i == moved) & (g == there)

    def source(i):
        return (lat + lat_n - i // inner) % lat_n, (xi + inner - i % inner) % inner

    moved = (lat_n // 2) * inner + inner // 2
    there = jnp.where(lat % 2 == 0, line - 2, max(line - 3, 0))
    lender, taker = z == line - 1, z == there
    spare = pl.ds(plane * slots, slots)

    has_low, has_high = z > 0, z < line - 1
    inside_line = has_low & has_high
    low, high = (lat, lon - inner), (lat, lon + inner)
    barrier = pltpu.get_barrier_semaphore()

    @pl.when(has_low)
    def _():
        pl.semaphore_signal(barrier, inc=1, device_id=low, device_id_type=MESH)

    @pl.when(has_high)
    def _():
        pl.semaphore_signal(barrier, inc=1, device_id=high, device_id_type=MESH)

    def greet(i, carry):
        pl.semaphore_signal(barrier, inc=1, device_id=mate(i)[2], device_id_type=MESH)
        return carry

    lax.fori_loop(1, plane, greet, 0)

    own_field = tbl.at[z, pl.ds(0, cells)]
    local = pltpu.make_async_copy(field, own_field, f_local)
    smalls = [
        pltpu.make_async_copy(src, dst, s_local.at[k])
        for k, (src, dst) in enumerate((
            (cell_in, cell_ref), (frac_in, frac_ref), (innov_in, innov_ref), (rinv_in, rinv_ref),
        ))
    ]
    for copy in (*smalls, local):
        copy.start()
    for g in visits:
        pltpu.make_async_copy(
            jac.at[lat, g, xi], jrecv.at[g, pl.ds(0, slots)], j_recv.at[g, 0]
        ).start()

    @pl.when(jnp.logical_not(has_low))
    def _():
        rbuf[z] = jnp.zeros(rbuf.shape[1:], rbuf.dtype)

    @pl.when(jnp.logical_not(has_high))
    def _():
        rbuf[line] = jnp.zeros(rbuf.shape[1:], rbuf.dtype)

    has_south, has_north = lat > 0, lat < lat_n - 1
    row_rim, edge_rim = pl.ds(cells, cols), pl.ds(halo, rows)
    tip = min(8, rows)
    corner_rim, rim = pl.ds(halo + rows, tip), pl.ds(cells, cols + 2 * rows)
    sent_rim = pl.ds(cells, cols + rows + tip)
    if rows > tip:
        tbl[z, pl.ds(halo + rows + tip, rows - tip), :] = jnp.zeros(
            (rows - tip, tbl.shape[2]), tbl.dtype
        )

    @pl.when(jnp.logical_not(has_north))
    def _():
        tbl[z, row_rim, :] = jnp.zeros((cols, tbl.shape[2]), tbl.dtype)
        tbl[z, corner_rim, :] = jnp.zeros((tip, tbl.shape[2]), tbl.dtype)

    @pl.when(jnp.logical_not(has_south))
    def _():
        hrecv[0] = jnp.zeros(hrecv.shape[1:], hrecv.dtype)
        hrecv[2] = jnp.zeros(hrecv.shape[1:], hrecv.dtype)

    for copy in smalls:
        copy.wait()
    innov[...] = innov_ref[...].astype(jnp.float32)
    rinv[...] = rinv_ref[...].astype(jnp.float32)
    cell = cell_ref[...].astype(jnp.float32)
    live = cell >= 0.0
    row = jnp.floor((cell + 0.5) * (1.0 / (cols + 1)))
    rowcol[0] = jnp.where(live, row, AWAY)
    rowcol[1] = jnp.where(live, cell - row * (cols + 1), AWAY)

    def build(i, carry):
        to_lat, to_x, _ = mate(i)
        for g in range(line):
            owner = to_lat * lon_n + g * inner + to_x
            meta[i, g] = jnp.concatenate(
                [
                    rowcol[0, pl.ds(owner, 1), :],
                    rowcol[1, pl.ds(owner, 1), :],
                    frac_ref[owner].astype(jnp.float32),
                    innov[pl.ds(owner, 1), :],
                    rinv[pl.ds(owner, 1), :],
                    jnp.zeros((2, slots), jnp.float32),
                ],
                axis=0,
            ).astype(meta.dtype)
        return carry

    lax.fori_loop(0, plane, build, 0)

    @pl.when(lender)
    def _():
        lent[...] = meta[moved, there]
        meta[moved, there] = jnp.full(lent.shape, AWAY, lent.dtype)
        jrecv[there, pl.ds(moved * slots, slots), :] = jnp.zeros(
            (slots, jrecv.shape[2]), jrecv.dtype
        )

    local.wait()
    edge[...] = jnp.concatenate(
        [tbl[z, pl.ds(r * cols, cols), :].astype(jnp.float32)[0:1] for r in range(rows)], axis=0
    ).astype(edge.dtype)
    pltpu.make_async_copy(meta.at[0], met.at[:, :, pl.ds(0, slots)], m_recv).start()
    pl.semaphore_wait(barrier, plane - 1 + has_low.astype(jnp.int32) + has_high.astype(jnp.int32))

    def send_field(g, c, up):
        piece = tbl.at[g, field_pieces[c]]
        remote(piece, piece, f_send, f_recv.at[g, c], high if up else low).start()

    def send_meta(i, carry):
        place = pl.ds(pl.multiple_of(i * slots, slots), slots)
        remote(meta.at[i], met.at[:, :, place], m_send, m_recv, mate(i)[2]).start()
        return carry

    half = plane // 2
    bounds = (0, half, plane - 1, plane)
    moved_piece = 0 if moved < half else 1 if moved < plane - 1 else 2

    def piece_of(i):
        return (i >= half).astype(jnp.int32) + (i >= plane - 1).astype(jnp.int32)

    def jac_landed(g, *which):
        for h in which:
            lanes = pl.ds(bounds[h] * slots, (bounds[h + 1] - bounds[h]) * slots)
            landed(jrecv.at[g, lanes], j_recv.at[g, h])

    def send_jac(n):
        g = visits[n]

        def one(i, carry):
            @pl.when(jnp.logical_not(lent_out(i, g)))
            def _():
                to_lat, to_x, at = mate(i)
                place = pl.ds(pl.multiple_of(i * slots, slots), slots)
                remote(
                    jac.at[to_lat, g, to_x], jrecv.at[g, place], j_send,
                    j_recv.at[g, piece_of(i)], at,
                ).start()

            return carry

        return one

    def send_edge():
        remote(edge, tbl.at[z_low, edge_rim], e_send, e_own, (lat, lon_down)).start()

        @pl.when(has_south)
        def _():
            remote(edge.at[pl.ds(0, tip)], tbl.at[z_low, corner_rim], e_send, e_own,
                   (lat_down, lon_down)).start()

    early = plane
    lax.fori_loop(1, plane, send_meta, 0)
    lax.fori_loop(1, 3, send_jac(0), 0)
    for c in range(len(field_pieces)):
        @pl.when(has_low & (z >= line // 2))
        def _():
            send_field(z, c, False)

        @pl.when(has_high & (z < line // 2))
        def _():
            send_field(z, c, True)

    @pl.when(has_south)
    def _():
        remote(tbl.at[z, pl.ds(0, cols)], tbl.at[z, row_rim], e_send, e_own,
               (lat_down, lon)).start()

    @pl.when(xi > 0)
    def _():
        send_edge()

    lax.fori_loop(3, early, send_jac(0), 0)

    for _ in range(line - 1):
        @pl.when(has_low)
        def _():
            pl.semaphore_signal(from_high, inc=1, device_id=low, device_id_type=MESH)

        @pl.when(has_high)
        def _():
            pl.semaphore_signal(from_low, inc=1, device_id=high, device_id_type=MESH)

        @pl.when(has_low)
        def _():
            pl.semaphore_wait(from_low, 1)

        @pl.when(has_high)
        def _():
            pl.semaphore_wait(from_high, 1)

    @pl.when(xi == 0)
    def _():
        send_edge()

    lax.fori_loop(early, plane, send_jac(0), 0)
    for n in range(1, line):
        lax.fori_loop(1, plane, send_jac(n), 0)

    @pl.when(lender)
    def _():
        to_lat, to_x, _ = mate(moved)
        at = (to_lat, there * inner + to_x)
        remote(lent, met.at[there, :, spare], l_send, l_recv, at).start()
        remote(jac.at[to_lat, there, to_x], jrecv.at[there, spare], j_send, s_recv, at).start()

    def field_landed(g, c):
        landed(tbl.at[g, field_pieces[c]], f_recv.at[g, c])

    def forward(d):
        for c in range(len(field_pieces)):
            @pl.when(inside_line & (z >= d))
            def _():
                field_landed(z - d, c)
                send_field(z - d, c, True)

            @pl.when(inside_line & (z + d < line))
            def _():
                field_landed(z + d, c)
                send_field(z + d, c, False)

    inside = jnp.where(lat < lat_n - 1, 1.0, 0.0)
    width = tile * slots
    tiles = plane // tile
    pad = -(-(max(rows, cols) + 1) // 8) * 8

    def terms(g, start, width):
        lanes = pl.ds(pl.multiple_of(start, slots), width)
        info = met[g, :, lanes].astype(jnp.float32)
        lat_w = weight_rows(info[0:1], info[2:3], pad)
        lon_w = weight_rows(info[1:2], info[3:4], pad)
        lon_c = lon_w[:cols]
        lon_e = lon_w[cols:cols + 1]
        lat_n_row = lat_w[rows:rows + 1] * inside
        first = lax.broadcasted_iota(jnp.int32, (rows, width), 0) == 0
        blocks = [lat_w[r:r + 1] * lon_c for r in range(rows)]
        blocks.append(lat_n_row * lon_c)
        blocks.append(lat_w[:rows] * lon_e)
        blocks.append(
            jnp.where(first, jnp.broadcast_to(lat_n_row * lon_e, (rows, width)), 0.0)
        )
        spread = jnp.concatenate(blocks, axis=0).astype(jnp.bfloat16).astype(jnp.float32)
        jac_t = jrecv[g, lanes]
        products = lax.dot_general(
            tbl[g], jac_t, (((1,), (1,)), ((), ())), preferred_element_type=jnp.float32
        )
        evolved = jnp.sum(spread * products, axis=0, keepdims=True)
        departure = jnp.where(info[0:1] >= 0.0, evolved - info[4:5], 0.0)
        dep[g, :, lanes] = departure
        return (spread * (info[5:6] * departure)).astype(jnp.bfloat16), jac_t

    def compute(n, g):
        into = part.at[n]

        def one_tile(t, carry):
            scaled, jac_t = terms(g, t * width, width)
            into[...] += jnp.dot(scaled, jac_t, preferred_element_type=jnp.float32)
            return carry

        if tiles > 1:
            into[...] = jnp.zeros(into.shape, into.dtype)
            lax.fori_loop(0, tiles, one_tile, 0)
        else:
            scaled, jac_t = terms(g, 0, width)
            into[...] = jnp.dot(scaled, jac_t, preferred_element_type=jnp.float32)

    def send_dep(g, first, last):
        def one(i, carry):
            @pl.when(jnp.logical_not(lent_out(i, g)))
            def _():
                to_lat, to_x = source(i)
                place = pl.ds(pl.multiple_of(i * slots, slots), slots)
                remote(
                    dep.at[g, :, place], dep_out.at[lat, g, xi], d_send, d_recv,
                    (to_lat, z * inner + to_x),
                ).start()

            return carry

        lax.fori_loop(max(first, 1), last, one, 0)
        if first == 0:
            pltpu.make_async_copy(
                dep.at[g, :, pl.ds(0, slots)], dep_out.at[lat, g, xi], d_recv
            ).start()

    def finish(n, incoming):
        g = visits[n]
        up = g > z
        next_z = jnp.where(up, z + 1, z - 1)
        slot = jnp.where((g == next_z) & jnp.logical_not(up), line, g)
        for c, at in enumerate(table_pieces):
            total = part[n, at, :]
            if incoming:
                landed(rbuf.at[g, at], g_recv.at[g, c])
                total = total + rbuf[g, at, :].astype(jnp.float32)
            gsend[n, at, :] = total.astype(gsend.dtype)
            remote(gsend.at[n, at], rbuf.at[slot, at], g_send, g_recv.at[slot, c],
                   (lat, next_z * inner + xi)).start()

    def pass_on(n):
        @pl.when(inside_line)
        def _():
            finish(n, True)

    for d in range(1, max(line // 2, 1)):
        forward(d)

    @pl.when(has_north)
    def _():
        landed(tbl.at[z, sent_rim], e_own)

    @pl.when(jnp.logical_not(has_north))
    def _():
        landed(edge, e_own)

    for i in range(1, line):
        remote(tbl.at[z, rim], tbl.at[z, rim], b_send, e_recv.at[z],
               (lat, (z + i) % line * inner + xi)).start()
    landed(met.at[:, :, pl.ds(0, plane * slots)], m_recv)
    for n in range(line - 1):
        g = visits[n]

        @pl.when(jnp.logical_not(inside_line))
        def _():
            for c in range(len(field_pieces)):
                field_landed(g, c)

        landed(tbl.at[g, rim], e_recv.at[g])
        jac_landed(g, *(h for h in range(3) if h != moved_piece))

        @pl.when(lent_out(moved, g))
        def _():
            rest = bounds[moved_piece + 1] - bounds[moved_piece] - 1
            if rest > 0:
                landed(jrecv.at[g, pl.ds(0, rest * slots)], j_recv.at[g, moved_piece])

        @pl.when(jnp.logical_not(lent_out(moved, g)))
        def _():
            jac_landed(g, moved_piece)

        compute(n, g)
        send_dep(g, 0, plane)

        @pl.when(jnp.logical_not(inside_line))
        def _():
            finish(n, False)

        if n == 0:
            for d in range(max(line // 2, 1), line - 1):
                forward(d)
            for c in range(len(field_pieces)):
                @pl.when(has_low & (z < line // 2))
                def _():
                    send_field(z, c, False)

                @pl.when(has_high & (z >= line // 2))
                def _():
                    send_field(z, c, True)
        elif n == 1:
            pass_on(0)
            pass_on(1)
        else:
            pass_on(n)

    main = pl.ds(0, cells)

    def arrived(at):
        return rbuf[z, at, :].astype(jnp.float32) + rbuf[line, at, :].astype(jnp.float32)

    def sums_landed(first, last):
        for c in range(first, last):
            at = table_pieces[c]

            @pl.when(has_low)
            def _():
                landed(rbuf.at[z, at], g_recv.at[z, c])

            @pl.when(has_high)
            def _():
                landed(rbuf.at[line, at], g_recv.at[line, c])

    def send_rim(values):
        sums_landed(0, 1)
        hsend[...] = (values + arrived(rim)).astype(hsend.dtype)
        remote(hsend.at[pl.ds(cols, rows)], hrecv.at[1], h_send, h_recv, (lat, lon_up)).start()

        @pl.when(has_north)
        def _():
            remote(hsend.at[pl.ds(cols + rows, tip)], hrecv.at[2, pl.ds(0, tip)], h_send, h_recv,
                   (lat_up, lon_up)).start()
            remote(hsend.at[pl.ds(0, cols)], hrecv.at[0], h_send, h_recv, (lat_up, lon)).start()

    def take_spare():
        landed(met.at[z, :, spare], l_recv)
        landed(jrecv.at[z, spare], s_recv)
        return terms(z, plane * slots, slots)

    def return_spare():
        to_lat, to_x = source(moved)
        remote(dep.at[z, :, spare], dep_out.at[lat, z, xi], s_send, d_recv,
               (to_lat, (line - 1) * inner + to_x)).start()

    def add(terms_of):
        scaled, jac_t = terms_of
        part[line - 1] += jnp.dot(scaled, jac_t, preferred_element_type=jnp.float32)

    def conclude(terms_of, send_rest):
        scaled, jac_t = terms_of
        send_rest()
        send_rim(part[line - 1, rim, :] + jnp.dot(
            scaled[cells:], jac_t, preferred_element_type=jnp.float32
        ))
        sums_landed(1, len(table_pieces))
        gmain[...] = arrived(main) + part[line - 1, main, :] + jnp.dot(
            scaled[:cells], jac_t, preferred_element_type=jnp.float32
        )

    if tiles > 1:
        jac_landed(z, 0, 1, 2)
        compute(line - 1, z)
        send_dep(z, 0, plane)

        @pl.when(taker)
        def _():
            add(take_spare())
            return_spare()

        send_rim(part[line - 1, rim, :])
        sums_landed(1, len(table_pieces))
        gmain[...] = part[line - 1, main, :] + arrived(main)
    else:
        jac_landed(z, 0)
        scaled, jac_t = terms(z, 0, half * slots)
        part[line - 1] = jnp.dot(scaled, jac_t, preferred_element_type=jnp.float32)
        send_dep(z, 0, half)
        jac_landed(z, 1)

        @pl.when(taker)
        def _():
            jac_landed(z, 2)
            add(terms(z, half * slots, half * slots))
            send_dep(z, half, plane)
            conclude(take_spare(), return_spare)

        @pl.when(jnp.logical_not(taker))
        def _():
            add(terms(z, half * slots, (half - 1) * slots))
            send_dep(z, half, plane - 1)
            jac_landed(z, 2)
            conclude(
                terms(z, (plane - 1) * slots, slots), lambda: send_dep(z, plane - 1, plane)
            )

    others = pl.ds(0, (plane - 1) * slots)
    for up in (False, True):
        for i in range(line):
            sent = (z >= i) & has_high if up else (z + i < line) & has_low

            @pl.when(sent & (inside_line | (i == 0)))
            def _():
                landed(own_field, f_send)
    @pl.when(has_south)
    def _():
        landed(tbl.at[z, sent_rim], e_send)

    @pl.when(jnp.logical_not(has_south))
    def _():
        landed(edge, e_send)

    landed(tbl.at[pl.ds(0, line - 1), rim], b_send)
    landed(met.at[:, :, others], m_send)
    landed(jrecv.at[:, others], j_send)
    landed(dep.at[pl.ds(0, line - 1), :, others], d_send)
    landed(dep.at[0, :, pl.ds(0, (plane - 2) * slots)], d_send)

    @pl.when(jnp.logical_not(lender))
    def _():
        landed(dep.at[0, :, pl.ds(0, slots)], d_send)

    @pl.when(lender)
    def _():
        landed(lent, l_send)

    @pl.when(taker)
    def _():
        landed(dep.at[0, :, spare], s_send)

    landed(gsend, g_send)
    @pl.when(has_north)
    def _():
        landed(tbl.at[z, sent_rim], h_send)

    @pl.when(jnp.logical_not(has_north))
    def _():
        landed(edge, h_send)

    @pl.when(has_south)
    def _():
        landed(tbl.at[z, sent_rim], h_recv)

    @pl.when(jnp.logical_not(has_south))
    def _():
        landed(edge, h_recv)

    landed(dep_out, d_recv)


def last_sums(rows, cols, gmain, hrecv, dep, grad_out, dep_out):
    dep_out[...] = dep[...]
    grad_out[...] = gmain[...]
    grad_out[pl.ds(0, cols), :] += hrecv[0].astype(jnp.float32)
    east = hrecv[1].astype(jnp.float32)
    corner = hrecv[2].astype(jnp.float32)
    for r in range(rows):
        extra = east[r:r + 1]
        if r == 0:
            extra = extra + corner[0:1]
        grad_out[pl.ds(r * cols, 1), :] += extra


def shards(mesh_shape, field, obs_jac, obs_frac, obs_innov, obs_rinv, obs_cells):
    lat_n, lon_n = mesh_shape
    line = math.gcd(lon_n // 2, 4)
    inner = lon_n // line
    plane = lat_n * inner
    total = lat_n * lon_n
    rows, cols, wide = field.shape
    slots = obs_jac.shape[2]
    tile = math.gcd(plane, 8)
    cells = rows * cols
    table = cells + cols + 2 * rows
    f32, bf16 = jnp.float32, jnp.bfloat16
    dma = pltpu.SemaphoreType.DMA
    one = pltpu.SemaphoreType.DMA(())
    vmem = pl.BlockSpec(memory_space=pltpu.VMEM)
    anywhere = pl.BlockSpec(memory_space=pltpu.HBM)
    parts = pl.pallas_call(
        functools.partial(kernel, lat_n, lon_n, line, rows, cols, tile),
        out_shape=(
            pltpu.VMEM((cells, wide), f32),
            pltpu.VMEM((3, rows, wide), bf16),
            pltpu.VMEM((lat_n, line, inner, 1, slots), f32),
        ),
        in_specs=[anywhere] * 6,
        out_specs=(vmem,) * 3,
        scratch_shapes=[
            pltpu.VMEM((total, slots), jnp.int32),
            pltpu.VMEM((total, 2, slots), bf16),
            pltpu.VMEM((total, slots), bf16),
            pltpu.VMEM((total, slots), bf16),
            pltpu.VMEM((rows, wide), bf16),
            pltpu.VMEM((total, slots), f32),
            pltpu.VMEM((total, slots), f32),
            pltpu.VMEM((2, total, slots), f32),
            pltpu.VMEM((plane, line, 8, slots), bf16),
            pltpu.VMEM((8, slots), bf16),
            pltpu.VMEM((line, table, wide), bf16),
            pltpu.VMEM((line, 8, (plane + 1) * slots), bf16),
            pltpu.VMEM((line, (plane + 1) * slots, wide), bf16),
            pltpu.VMEM((line, 1, (plane + 1) * slots), f32),
            pltpu.VMEM((line, table, wide), f32),
            pltpu.VMEM((line - 1, table, wide), bf16),
            pltpu.VMEM((line + 1, table, wide), bf16),
            pltpu.VMEM((table - cells, wide), bf16),
            one, dma((4,)), one, dma((line, 2)),
            one, one, one, dma((line,)),
            one, one,
            one, one, one, one,
            one, dma((line, 3)),
            one, one,
            one, dma((line + 1, 3)),
            one, one,
            pltpu.SemaphoreType.REGULAR, pltpu.SemaphoreType.REGULAR,
        ],
        compiler_params=pltpu.CompilerParams(
            collective_id=0, has_side_effects=True, vmem_limit_bytes=62 * 1024 * 1024
        ),
    )(
        field.reshape(cells, wide),
        obs_cells.reshape(total, slots),
        obs_frac.reshape(total, 2, slots),
        obs_innov.reshape(total, slots),
        obs_rinv.reshape(total, slots),
        obs_jac.reshape(lat_n, line, inner, slots, wide),
    )
    grad, departures = pl.pallas_call(
        functools.partial(last_sums, rows, cols),
        out_shape=(
            jax.ShapeDtypeStruct((cells, wide), f32),
            jax.ShapeDtypeStruct((total, 1, slots), f32),
        ),
        in_specs=[vmem] * 3,
        out_specs=(vmem, vmem),
        compiler_params=pltpu.CompilerParams(vmem_limit_bytes=8 * 1024 * 1024),
    )(*parts[:2], parts[2].reshape(total, 1, slots))
    return departures, grad.reshape(rows, cols, wide)


def solution(mesh):
    placed = (
        P("lat", "lon", None),
        P(None, ("lat", "lon"), None, None),
        P(None, ("lat", "lon"), None, None),
        P(None, ("lat", "lon"), None),
        P(None, ("lat", "lon"), None),
        P(None, ("lat", "lon"), None),
    )
    return jax.shard_map(
        functools.partial(shards, (mesh.shape["lat"], mesh.shape["lon"])),
        mesh=mesh,
        in_specs=placed,
        out_specs=(P(None, ("lat", "lon"), None), P("lat", "lon", None)),
        check_vma=False,
    )
```
